512 devices in a mesh: seq: 64 (over x, z, core), rep: 8 (over y).
Axes of the slice: x: 4, y: 8, z: 8, core: 2. Of those that a mesh axis runs over, the one named last changes fastest.
Arguments:
- token_ids: int32 [32, 4], P('rep'), parts along dimension 0, may hold values from 0 to 24703
- cache_lengths: int32 [32], P('rep'), parts along dimension 0, may hold values from 1 to 8192, 8216 in all
- embed_table: bfloat16 [2048, 24704], P('seq'), may hold values from -0.119628906 to 0.119628906
- key_cache: bfloat16 [32, 8192, 512], P('rep', 'seq'), parts along dimension 0, may hold values from -4000 to 4000
- value_cache: bfloat16 [32, 8192, 512], P('rep', 'seq'), parts along dimension 0, may hold values from -24 to 24
- norm_attn: bfloat16 [2048], replicated, may hold values from 0.25 to 1.75
- norm_mlp: bfloat16 [2048], replicated, may hold values from 0.25 to 1.75
- w_qkv: bfloat16 [2048, 3072], P(None, 'seq'), may hold values from -0.125 to 0.125
- w_out: bfloat16 [2048, 2048], P(None, 'seq'), may hold values from -0.125 to 0.125
- w_gate: bfloat16 [2048, 8192], P(None, 'seq'), may hold values from -0.125 to 0.125
- w_up: bfloat16 [2048, 8192], P(None, 'seq'), may hold values from -0.125 to 0.125
- w_down: bfloat16 [8192, 2048], P('seq'), may hold values from -0.0625 to 0.0625
Outputs:
- layer_out: bfloat16 [32, 4, 2048], P('rep'), parts along dimension 0
The draws below stay inside these ranges and needn't reach their ends.
There are 8 independent parts, one for each index of `rep`. The reference program is written for one: setup_inputs(seed, part) draws one part's arguments, and reference() takes and returns one part's arrays. A program takes and returns all parts, laid end to end along the dimension named above; an argument that names none is the same for every part. Nothing has to cross between parts.
All inputs are finite; a program needn't handle non-finite values.
Results may differ from the reference program's by a relative error of at most 0.012.
The reference program's roundings to bfloat16 on the way count: a program that leaves them out, or rounds other values in their place, can miss the bound.
Values may be sent and summed in bfloat16 or wider, within the bound.
A program may use at most 128 MiB of HBM per device.

```python
import math
import jax
import jax.numpy as jnp
import numpy as np
from jax import lax

D = 2048
H = 32
KVH = 8
HD = 64
FF = 8192
VOCAB = 24704
STEPS = 4
REQ = 4
CTX_DEV = 128
LMAX = 8192
QKV = 3072
N_SEQ = 64


def draw_key_cache(key, part):
    base_key = jax.random.fold_in(key, 0)
    shape = (REQ, LMAX, KVH * HD)
    values = jax.random.normal(base_key, shape, jnp.float32) * 8.0
    return jnp.clip(values, -4000.0, 4000.0).astype(jnp.bfloat16)


def with_ends(drawn, stream_key, low, top_value):
    extent = drawn.shape
    index_at = [jax.random.randint(jax.random.fold_in(stream_key, axis), (), 0, extent[axis]) for axis in range(len(extent))]
    drawn = drawn.at[tuple(index_at)].set(low)
    longest = extent.index(max(extent))
    index_at[longest] = (index_at[longest] + 1) % extent[longest]
    return drawn.at[tuple(index_at)].set(top_value)


def levels(own_key, shape, cuts, smallest, high):
    def one(position, parts):
        draws = jax.random.uniform(jax.random.fold_in(jax.random.fold_in(own_key, 6), position), (parts,), jnp.float32, smallest / len(cuts), high / len(cuts))
        return jnp.repeat(jnp.exp(draws), shape[position] // parts).reshape((-1,) + (1,) * (len(shape) - position - 1))

    loudness = one(*cuts[0])
    for cut in cuts[1:]:
        loudness = loudness * one(*cut)
    return loudness


def split_up(number_of, total, most, lean):
    portions = [(1 << 20) // math.isqrt(rank ** lean) + 1 for rank in range(2, number_of + 1)]
    spare, holding = total - most - (number_of - 1), [1] * (number_of - 1)
    while spare > 0:
        candidates = [i for i in range(number_of - 1) if holding[i] < most]
        whole, left = sum([portions[i] for i in candidates]), spare
        for i in candidates:
            addition = min(most - holding[i], max(1, left * portions[i] // whole), spare)
            holding[i] = holding[i] + addition
            spare = spare - addition
    return np.array([most] + holding)


def uneven_parts(key, count, total, limit, lean):
    if count == 2:
        one = jax.random.randint(key, (), max(1, total - limit), min(limit, total - 1) + 1)
        return jnp.stack([one, total - one])
    sizes = jnp.asarray(split_up(count, total, limit, lean), jnp.int32)
    twos = (count - 1) // 2
    donor, receiver = sizes[1:1 + 2 * twos:2], sizes[2:2 + 2 * twos:2]
    room = jnp.minimum(donor - 1, limit - receiver)
    passed = jax.random.randint(jax.random.fold_in(key, 1), (twos,), 0, 1 << 20) % (room + 1)
    sizes = sizes.at[1:1 + 2 * twos:2].set(donor - passed).at[2:2 + 2 * twos:2].set(receiver + passed)
    return sizes[jax.random.permutation(jax.random.fold_in(key, 2), count)]


def bell_draw(stream_key, dims, width, limit, cuts=(), held_as=jnp.bfloat16):
    level = levels(stream_key, dims, cuts, -0.22, 0.18) if cuts else 1.0
    drawn = jax.random.normal(stream_key, dims, jnp.float32) * width * level
    return jnp.minimum(jnp.maximum(drawn, -limit), limit).astype(held_as)


def setup_inputs(seed: int = 0, part: int = 0) -> dict:
    key_of = jax.random.split(jax.random.key(seed), 13)
    part_splits = jax.random.split(jax.random.fold_in(key_of[12], part), 13)
    token_ids = with_ends(jax.random.randint(part_splits[0], (REQ, STEPS), 0, VOCAB), jax.random.fold_in(part_splits[0], 1), 0, VOCAB - 1).astype(jnp.int32)
    cache_lengths = uneven_parts(part_splits[1], REQ, LMAX + 6 * STEPS, LMAX, 2).astype(jnp.int32)
    embed_table = bell_draw(key_of[2], (D, VOCAB), 0.02, 0.119628906, ((0, 64),))
    key_cache = draw_key_cache(jax.random.fold_in(jax.random.fold_in(key_of[12], part), 71), part)
    value_cache = bell_draw(part_splits[4], (REQ, LMAX, KVH * HD), 4.0, 24.0, ((1, 64),))
    norm_attn = jnp.clip(1.0 + 0.15 * jax.random.normal(key_of[5], (D,), jnp.float32), 0.25, 1.75).astype(jnp.bfloat16)
    norm_mlp = jnp.clip(1.0 + 0.15 * jax.random.normal(key_of[6], (D,), jnp.float32), 0.25, 1.75).astype(jnp.bfloat16)
    w_qkv = bell_draw(key_of[7], (D, QKV), D ** -0.5, 0.125, ((1, 64),))
    w_out = bell_draw(key_of[8], (H * HD, D), (H * HD) ** -0.5, 0.125, ((1, 64),))
    w_gate = bell_draw(key_of[9], (D, FF), D ** -0.5, 0.125, ((1, 64),))
    w_up = bell_draw(key_of[10], (D, FF), D ** -0.5, 0.125, ((1, 64),))
    w_down = bell_draw(key_of[11], (FF, D), FF ** -0.5, 0.0625, ((0, 64),))
    return {"token_ids": token_ids, "cache_lengths": cache_lengths, "embed_table": embed_table, "key_cache": key_cache, "value_cache": value_cache, "norm_attn": norm_attn, "norm_mlp": norm_mlp, "w_qkv": w_qkv, "w_out": w_out, "w_gate": w_gate, "w_up": w_up, "w_down": w_down}


norm_epsilon = 1e-05
embed_factor = 12.0
score_factor = 0.015625
branch_factor = 0.22
rope_base = 10000000.0
masked_floor = -1e+30

def rounded(values):
    return lax.optimization_barrier(values.astype(jnp.bfloat16)).astype(jnp.float32)

def rms_scale(resid, gain):
    mean_square = lax.optimization_barrier(jnp.mean(resid * resid, axis=-1, keepdims=True))
    return resid * lax.rsqrt(mean_square + norm_epsilon) * gain.astype(jnp.float32)

def rotate(vectors, where):
    half = vectors.shape[-1] // 2
    freqs = rope_base ** (-2.0 * jnp.arange(half, dtype=jnp.float32) / vectors.shape[-1])
    angle = where[..., None] * freqs
    cosine = jnp.cos(angle)
    sine = jnp.sin(angle)
    first_half = vectors[..., :half]
    second_half = vectors[..., half:]
    return jnp.concatenate([first_half * cosine - second_half * sine, second_half * cosine + first_half * sine], axis=-1)

def reference(token_ids, cache_lengths, embed_table, key_cache, value_cache, norm_attn, norm_mlp, w_qkv, w_out, w_gate, w_up, w_down):
    group = H // KVH
    att_width = H * HD
    kv_width = KVH * HD
    embedded = jnp.transpose(embed_table[:, token_ids].astype(jnp.float32), (1, 2, 0)) * embed_factor
    cache_keys = key_cache.astype(jnp.float32).reshape(REQ, LMAX, KVH, HD)
    cache_values = value_cache.astype(jnp.float32).reshape(REQ, N_SEQ, CTX_DEV, KVH, HD)
    slot_pos = jnp.arange(LMAX, dtype=jnp.int32)
    cache_valid = (slot_pos[None, :] < cache_lengths[:, None]).reshape(REQ, 1, 1, N_SEQ, CTX_DEV)
    fresh_keys = jnp.zeros((REQ, STEPS, KVH, HD), jnp.float32)
    fresh_values = jnp.zeros((REQ, STEPS, KVH, HD), jnp.float32)
    results = []
    for step_index in range(STEPS):
        resid = embedded[:, step_index, :]
        normed = rms_scale(resid, norm_attn).astype(jnp.bfloat16)
        qkv = jnp.dot(normed, w_qkv, preferred_element_type=jnp.float32).astype(jnp.bfloat16).astype(jnp.float32)
        where = (cache_lengths + step_index).astype(jnp.float32)[:, None]
        query = rounded(rotate(qkv[:, :att_width].reshape(REQ, H, HD), where))
        new_key = rounded(rotate(qkv[:, att_width:att_width + kv_width].reshape(REQ, KVH, HD), where))
        new_value = qkv[:, att_width + kv_width:].reshape(REQ, KVH, HD)
        fresh_keys = fresh_keys.at[:, step_index].set(new_key)
        fresh_values = fresh_values.at[:, step_index].set(new_value)
        grouped = query.reshape(REQ, KVH, group, HD)
        scores = jnp.einsum('rkgd,rpkd->rkgp', grouped, cache_keys) * score_factor
        blocked = scores.reshape(REQ, KVH, group, N_SEQ, CTX_DEV)
        block_max = lax.optimization_barrier(jnp.max(jnp.where(cache_valid, blocked, masked_floor), axis=-1))
        expo = jnp.exp(jnp.where(cache_valid, blocked - block_max[..., None], masked_floor))
        block_total = lax.optimization_barrier(jnp.sum(expo, axis=-1))
        block_out = jnp.einsum('rkgnp,rnpkd->rkgnd', rounded(expo), cache_values)
        fresh_scores = jnp.einsum('rkgd,rukd->rkgu', grouped, fresh_keys) * score_factor
        fresh_valid = (jnp.arange(STEPS, dtype=jnp.int32) <= step_index).reshape(1, 1, 1, STEPS)
        fresh_max = lax.optimization_barrier(jnp.max(jnp.where(fresh_valid, fresh_scores, masked_floor), axis=-1))
        fresh_expo = jnp.exp(jnp.where(fresh_valid, fresh_scores - fresh_max[..., None], masked_floor))
        fresh_total = lax.optimization_barrier(jnp.sum(fresh_expo, axis=-1))
        fresh_out = jnp.einsum('rkgu,rukd->rkgd', rounded(fresh_expo), fresh_values)
        overall = jnp.maximum(lax.optimization_barrier(jnp.max(block_max, axis=-1)), fresh_max)
        block_scale = jnp.exp(block_max - overall[..., None])
        fresh_scale = jnp.exp(fresh_max - overall)
        numer = lax.optimization_barrier(jnp.sum(block_scale[..., None] * block_out, axis=3)) + fresh_scale[..., None] * fresh_out
        denom = lax.optimization_barrier(jnp.sum(block_scale * block_total, axis=-1)) + fresh_scale * fresh_total
        attention = (numer / denom[..., None]).reshape(REQ, att_width).astype(jnp.bfloat16)
        projected = jnp.dot(attention, w_out, preferred_element_type=jnp.float32).astype(jnp.bfloat16)
        middle = resid + branch_factor * projected.astype(jnp.float32)
        normed_mlp = rms_scale(middle, norm_mlp).astype(jnp.bfloat16)
        gate = jnp.dot(normed_mlp, w_gate, preferred_element_type=jnp.float32)
        upward = jnp.dot(normed_mlp, w_up, preferred_element_type=jnp.float32)
        hidden = (jax.nn.silu(gate) * upward).astype(jnp.bfloat16)
        down = jnp.dot(hidden, w_down, preferred_element_type=jnp.float32)
        results.append((middle + branch_factor * down).astype(jnp.bfloat16))
    return jnp.stack(results, axis=1)
```

```python
import jax
import jax.numpy as jnp
from jax import lax
from jax.sharding import PartitionSpec as P

H = 32
KVH = 8
HD = 64
STEPS = 4


norm_epsilon = 1e-05
embed_factor = 12.0
score_factor = 0.015625
branch_factor = 0.22
rope_base = 10000000.0
masked_floor = -1e30


def rms_scale(resid, gain):
    mean_square = jnp.mean(resid * resid, axis=-1, keepdims=True)
    return resid * lax.rsqrt(mean_square + norm_epsilon) * gain.astype(jnp.float32)


def rotate(vectors, where):
    half = vectors.shape[-1] // 2
    freqs = rope_base ** (-2.0 * jnp.arange(half, dtype=jnp.float32) / vectors.shape[-1])
    angle = where[..., None] * freqs
    cosine = jnp.cos(angle)
    sine = jnp.sin(angle)
    first_half = vectors[..., :half]
    second_half = vectors[..., half:]
    return jnp.concatenate(
        [first_half * cosine - second_half * sine, second_half * cosine + first_half * sine],
        axis=-1,
    )


def partial_softmax(queries, keys, values, valid):
    scores = (
        jnp.einsum("rskgd,rpkd->rskgp", queries, keys, preferred_element_type=jnp.float32)
        * score_factor
    )
    maxima = jnp.max(jnp.where(valid, scores, masked_floor), axis=-1)
    expo = jnp.exp(jnp.where(valid, scores - maxima[..., None], masked_floor))
    totals = jnp.sum(expo, axis=-1)
    outputs = jnp.einsum(
        "rskgp,rpkd->rskgd", expo.astype(jnp.bfloat16), values, preferred_element_type=jnp.float32
    )
    return (maxima, totals, outputs)


def shards(
    token_ids,
    cache_lengths,
    embed_table,
    key_cache,
    value_cache,
    norm_attn,
    norm_mlp,
    w_qkv,
    w_out,
    w_gate,
    w_up,
    w_down,
):
    place = lax.axis_index("seq")
    req_all = token_ids.shape[0]
    steps = token_ids.shape[1]
    ctx_own = key_cache.shape[1]
    att_width = H * HD
    kv_width = KVH * HD
    group = H // KVH
    picked = jnp.take(embed_table, token_ids.reshape(-1), axis=1)
    whole = lax.all_gather(picked, "seq", axis=0, tiled=True)
    resid = jnp.transpose(whole, (1, 0)).reshape(req_all, steps, -1).astype(jnp.float32) * embed_factor
    slot_pos = place * ctx_own + jnp.arange(ctx_own, dtype=jnp.int32)
    cache_valid = (slot_pos[None, :] < cache_lengths[:, None]).reshape(req_all, 1, 1, 1, ctx_own)
    cache_keys = key_cache.reshape(req_all, ctx_own, KVH, HD)
    cache_values = value_cache.reshape(req_all, ctx_own, KVH, HD)

    normed = rms_scale(resid, norm_attn).astype(jnp.bfloat16)
    qkv_cols = jnp.einsum(
        "rsd,dc->rsc", normed, w_qkv, preferred_element_type=jnp.float32
    ).astype(jnp.bfloat16)
    qkv_all = lax.all_gather(qkv_cols, "seq", axis=2, tiled=True)
    where = (cache_lengths[:, None] + jnp.arange(steps, dtype=jnp.int32)[None, :]).astype(
        jnp.float32
    )
    queries = rotate(
        qkv_all[..., :att_width].reshape(req_all, steps, H, HD).astype(jnp.float32),
        where[..., None],
    ).astype(jnp.bfloat16)
    keys_new = rotate(
        qkv_all[..., att_width : att_width + kv_width]
        .reshape(req_all, steps, KVH, HD)
        .astype(jnp.float32),
        where[..., None],
    ).astype(jnp.bfloat16)
    values_new = qkv_all[..., att_width + kv_width :].reshape(req_all, steps, KVH, HD)
    grouped = queries.reshape(req_all, steps, KVH, group, HD)
    cache_max, cache_total, cache_out = partial_softmax(
        grouped, cache_keys, cache_values, cache_valid
    )
    fresh_valid = (
        jnp.arange(steps, dtype=jnp.int32)[None, :] <= jnp.arange(steps, dtype=jnp.int32)[:, None]
    ).reshape(1, steps, 1, 1, steps)
    fresh_max, fresh_total, fresh_out = partial_softmax(grouped, keys_new, values_new, fresh_valid)

    overall = jnp.maximum(lax.pmax(cache_max, "seq"), fresh_max)
    cache_scale = jnp.exp(cache_max - overall)
    packed = jnp.concatenate(
        [cache_scale[..., None] * cache_out, (cache_scale * cache_total)[..., None]], axis=-1
    )
    summed = lax.psum(packed, "seq")
    fresh_scale = jnp.exp(fresh_max - overall)
    numer = summed[..., :HD] + fresh_scale[..., None] * fresh_out
    denom = summed[..., HD] + fresh_scale * fresh_total
    attention = (numer / denom[..., None]).astype(jnp.bfloat16).reshape(req_all, steps, att_width)

    proj_cols = jnp.einsum(
        "rsa,ac->rsc", attention, w_out, preferred_element_type=jnp.float32
    ).astype(jnp.bfloat16)
    projected = lax.all_gather(proj_cols, "seq", axis=2, tiled=True)
    middle = resid + branch_factor * projected.astype(jnp.float32)
    normed_mlp = rms_scale(middle, norm_mlp).astype(jnp.bfloat16)
    gate = jnp.einsum("rsd,df->rsf", normed_mlp, w_gate, preferred_element_type=jnp.float32)
    upward = jnp.einsum("rsd,df->rsf", normed_mlp, w_up, preferred_element_type=jnp.float32)
    hidden = (jax.nn.silu(gate) * upward).astype(jnp.bfloat16)
    down_part = jnp.einsum("rsf,fd->rsd", hidden, w_down, preferred_element_type=jnp.float32)
    down = lax.psum(down_part, "seq")
    return (middle + branch_factor * down).astype(jnp.bfloat16)


def solution(mesh):
    return jax.shard_map(
        shards,
        mesh=mesh,
        in_specs=(
            P("rep", None),
            P("rep"),
            P("seq", None),
            P("rep", "seq", None),
            P("rep", "seq", None),
            P(),
            P(),
            P(None, "seq"),
            P(None, "seq"),
            P(None, "seq"),
            P(None, "seq"),
            P("seq", None),
        ),
        out_specs=P("rep", None, None),
        check_vma=False,
    )
```

```python
import functools

import jax
import jax.numpy as jnp
from jax import lax
from jax.experimental import pallas as pl
from jax.experimental.pallas import tpu as pltpu
from jax.sharding import PartitionSpec as P

H = 32
KVH = 8
HD = 64

MESH_ID = pl.DeviceIdType.MESH


def _exchange_kernel(n, gather, x_ref, o_ref, buf, send_sems, recv_sems, local_sem):
    me = lax.axis_index("seq")
    rep = lax.axis_index("rep")
    barrier = pltpu.get_barrier_semaphore()

    def greet(k, carry):
        peer = lax.rem(me + k, n)
        pl.semaphore_signal(barrier, inc=1, device_id=(peer, rep), device_id_type=MESH_ID)
        return carry

    lax.fori_loop(1, n, greet, 0)
    pl.semaphore_wait(barrier, n - 1)

    def source(peer):
        return x_ref if gather else x_ref.at[peer]

    def outgoing(peer):
        return pltpu.make_async_remote_copy(
            src_ref=source(peer),
            dst_ref=buf.at[me],
            send_sem=send_sems.at[peer],
            recv_sem=recv_sems.at[me],
            device_id=(peer, rep),
            device_id_type=MESH_ID,
        )

    def incoming(peer):
        return pltpu.make_async_remote_copy(
            src_ref=source(peer),
            dst_ref=buf.at[peer],
            send_sem=send_sems.at[peer],
            recv_sem=recv_sems.at[peer],
            device_id=(peer, rep),
            device_id_type=MESH_ID,
        )

    def send(k, carry):
        outgoing(lax.rem(me + k, n)).start()
        return carry

    lax.fori_loop(1, n, send, 0)
    local = pltpu.make_async_copy(source(me), buf.at[me], local_sem)
    local.start()

    def finish(k, carry):
        peer = lax.rem(me + k, n)
        outgoing(peer).wait_send()
        incoming(peer).wait_recv()
        return carry

    lax.fori_loop(1, n, finish, 0)
    local.wait()
    o_ref[...] = buf[...]


def exchange(x, n, gather, cid):
    blk = x.shape if gather else x.shape[1:]
    shape = (n,) + tuple(blk)
    nbytes = int(jnp.dtype(x.dtype).itemsize) * n
    for d in blk:
        nbytes *= int(d)
    return pl.pallas_call(
        functools.partial(_exchange_kernel, n, gather),
        out_shape=jax.ShapeDtypeStruct(shape, x.dtype),
        in_specs=[pl.BlockSpec(memory_space=pltpu.VMEM)],
        out_specs=pl.BlockSpec(memory_space=pltpu.VMEM),
        scratch_shapes=[
            pltpu.VMEM(shape, x.dtype),
            pltpu.SemaphoreType.DMA((n,)),
            pltpu.SemaphoreType.DMA((n,)),
            pltpu.SemaphoreType.DMA(()),
        ],
        compiler_params=pltpu.CompilerParams(collective_id=cid, has_side_effects=True),
        cost_estimate=pl.CostEstimate(flops=0, transcendentals=0, bytes_accessed=2 * nbytes),
        name="exchange_%d" % cid,
    )(x)


STEPS = 4
norm_epsilon = 1e-05
embed_factor = 12.0
score_factor = 0.015625
branch_factor = 0.22
rope_base = 10000000.0
masked_floor = -1e30


def rms_scale(resid, gain):
    mean_square = jnp.mean(resid * resid, axis=-1, keepdims=True)
    return resid * lax.rsqrt(mean_square + norm_epsilon) * gain.astype(jnp.float32)


def rotate(vectors, where):
    half = vectors.shape[-1] // 2
    freqs = rope_base ** (-2.0 * jnp.arange(half, dtype=jnp.float32) / vectors.shape[-1])
    angle = where[..., None] * freqs
    cosine = jnp.cos(angle)
    sine = jnp.sin(angle)
    first_half = vectors[..., :half]
    second_half = vectors[..., half:]
    return jnp.concatenate(
        [first_half * cosine - second_half * sine, second_half * cosine + first_half * sine],
        axis=-1,
    )


def partial_softmax(queries, keys, values, valid):
    scores = (
        jnp.einsum("rskgd,rpkd->rskgp", queries, keys, preferred_element_type=jnp.float32)
        * score_factor
    )
    maxima = jnp.max(jnp.where(valid, scores, masked_floor), axis=-1)
    expo = jnp.exp(jnp.where(valid, scores - maxima[..., None], masked_floor))
    totals = jnp.sum(expo, axis=-1)
    outputs = jnp.einsum(
        "rskgp,rpkd->rskgd", expo.astype(jnp.bfloat16), values, preferred_element_type=jnp.float32
    )
    return (maxima, totals, outputs)


def shards(
    token_ids,
    cache_lengths,
    embed_table,
    key_cache,
    value_cache,
    norm_attn,
    norm_mlp,
    w_qkv,
    w_out,
    w_gate,
    w_up,
    w_down,
):
    n = lax.axis_size("seq")
    place = lax.axis_index("seq")
    req_all = token_ids.shape[0]
    steps = token_ids.shape[1]
    rows = req_all * steps
    ctx_own = key_cache.shape[1]
    width = embed_table.shape[0] * n
    att_width = H * HD
    kv_width = KVH * HD
    group = H // KVH

    picked = jnp.take(embed_table, token_ids.reshape(-1), axis=1)
    whole = exchange(jnp.transpose(picked, (1, 0)), n, True, 0)
    resid = jnp.transpose(whole, (1, 0, 2)).reshape(rows, width).astype(jnp.float32) * embed_factor

    slot_pos = place * ctx_own + jnp.arange(ctx_own, dtype=jnp.int32)
    cache_valid = (slot_pos[None, :] < cache_lengths[:, None]).reshape(req_all, 1, 1, 1, ctx_own)
    cache_keys = key_cache.reshape(req_all, ctx_own, KVH, HD)
    cache_values = value_cache.reshape(req_all, ctx_own, KVH, HD)

    normed = rms_scale(resid, norm_attn).astype(jnp.bfloat16)
    qkv_cols = jnp.dot(normed, w_qkv, preferred_element_type=jnp.float32).astype(jnp.bfloat16)
    qkv_got = exchange(qkv_cols, n, True, 1)
    qkv_all = jnp.transpose(qkv_got, (1, 0, 2)).reshape(req_all, steps, -1)
    where = (cache_lengths[:, None] + jnp.arange(steps, dtype=jnp.int32)[None, :]).astype(
        jnp.float32
    )
    queries = rotate(
        qkv_all[..., :att_width].reshape(req_all, steps, H, HD).astype(jnp.float32),
        where[..., None],
    ).astype(jnp.bfloat16)
    keys_new = rotate(
        qkv_all[..., att_width : att_width + kv_width]
        .reshape(req_all, steps, KVH, HD)
        .astype(jnp.float32),
        where[..., None],
    ).astype(jnp.bfloat16)
    values_new = qkv_all[..., att_width + kv_width :].reshape(req_all, steps, KVH, HD)
    grouped = queries.reshape(req_all, steps, KVH, group, HD)
    cache_max, cache_total, cache_out = partial_softmax(
        grouped, cache_keys, cache_values, cache_valid
    )
    fresh_valid = (
        jnp.arange(steps, dtype=jnp.int32)[None, :] <= jnp.arange(steps, dtype=jnp.int32)[:, None]
    ).reshape(1, steps, 1, 1, steps)
    fresh_max, fresh_total, fresh_out = partial_softmax(grouped, keys_new, values_new, fresh_valid)

    pairs = rows * H // n
    lanes = 128
    packed = jnp.concatenate(
        [
            cache_out.reshape(n, pairs, HD),
            cache_max.reshape(n, pairs, 1),
            cache_total.reshape(n, pairs, 1),
            jnp.zeros((n, pairs, lanes - HD - 2), jnp.float32),
        ],
        axis=-1,
    )
    got = exchange(packed, n, False, 2)
    block_max = got[:, :, HD]
    block_total = got[:, :, HD + 1]
    block_out = got[:, :, :HD]
    own_fresh_max = lax.dynamic_index_in_dim(fresh_max.reshape(n, pairs), place, 0, False)
    own_fresh_total = lax.dynamic_index_in_dim(fresh_total.reshape(n, pairs), place, 0, False)
    own_fresh_out = lax.dynamic_index_in_dim(fresh_out.reshape(n, pairs, HD), place, 0, False)
    overall = jnp.maximum(jnp.max(block_max, axis=0), own_fresh_max)
    block_scale = jnp.exp(block_max - overall[None, :])
    fresh_scale = jnp.exp(own_fresh_max - overall)
    numer = jnp.sum(block_scale[..., None] * block_out, axis=0) + fresh_scale[:, None] * own_fresh_out
    denom = jnp.sum(block_scale * block_total, axis=0) + fresh_scale * own_fresh_total
    attention_own = (numer / denom[:, None]).astype(jnp.bfloat16).reshape(1, pairs * HD)
    attention = exchange(attention_own, n, True, 3).reshape(rows, att_width)

    proj_cols = jnp.dot(attention, w_out, preferred_element_type=jnp.float32).astype(jnp.bfloat16)
    proj_got = exchange(proj_cols, n, True, 4)
    projected = jnp.transpose(proj_got, (1, 0, 2)).reshape(rows, width)
    middle = resid + branch_factor * projected.astype(jnp.float32)
    normed_mlp = rms_scale(middle, norm_mlp).astype(jnp.bfloat16)
    gate = jnp.dot(normed_mlp, w_gate, preferred_element_type=jnp.float32)
    upward = jnp.dot(normed_mlp, w_up, preferred_element_type=jnp.float32)
    hidden = (jax.nn.silu(gate) * upward).astype(jnp.bfloat16)
    down_part = jnp.dot(hidden, w_down, preferred_element_type=jnp.float32)
    cols = width // n
    down_got = exchange(jnp.transpose(down_part.reshape(rows, n, cols), (1, 0, 2)), n, False, 5)
    down_own = jnp.sum(down_got, axis=0)
    middle_own = lax.dynamic_slice_in_dim(middle, place * cols, cols, axis=1)
    out_own = (middle_own + branch_factor * down_own).astype(jnp.bfloat16)
    out_got = exchange(out_own, n, True, 6)
    return jnp.transpose(out_got, (1, 0, 2)).reshape(req_all, steps, width)


def solution(mesh):
    return jax.shard_map(
        shards,
        mesh=mesh,
        in_specs=(
            P("rep", None),
            P("rep"),
            P("seq", None),
            P("rep", "seq", None),
            P("rep", "seq", None),
            P(),
            P(),
            P(None, "seq"),
            P(None, "seq"),
            P(None, "seq"),
            P(None, "seq"),
            P("seq", None),
        ),
        out_specs=P("rep", None, None),
        check_vma=False,
    )
```

```python
import functools

import jax
import jax.numpy as jnp
from jax import lax
from jax.experimental import pallas as pl
from jax.experimental.pallas import tpu as pltpu
from jax.sharding import PartitionSpec as P

H = 32
KVH = 8
HD = 64

MESH_ID = pl.DeviceIdType.MESH


def _greet(n, me, rep):
    barrier = pltpu.get_barrier_semaphore()

    def greet(k, carry):
        peer = lax.rem(me + k, n)
        pl.semaphore_signal(barrier, inc=1, device_id=(peer, rep), device_id_type=MESH_ID)
        return carry

    lax.fori_loop(1, n, greet, 0)
    pl.semaphore_wait(barrier, n - 1)


def _spread(n, me, rep, source, buf, send_sems, recv_sems, local_sem):
    def outgoing(peer):
        return pltpu.make_async_remote_copy(
            src_ref=source(peer),
            dst_ref=buf.at[me],
            send_sem=send_sems.at[peer],
            recv_sem=recv_sems.at[me],
            device_id=(peer, rep),
            device_id_type=MESH_ID,
        )

    def incoming(peer):
        return pltpu.make_async_remote_copy(
            src_ref=source(peer),
            dst_ref=buf.at[peer],
            send_sem=send_sems.at[peer],
            recv_sem=recv_sems.at[peer],
            device_id=(peer, rep),
            device_id_type=MESH_ID,
        )

    def send(k, carry):
        outgoing(lax.rem(me + k, n)).start()
        return carry

    lax.fori_loop(1, n, send, 0)
    local = pltpu.make_async_copy(source(me), buf.at[me], local_sem)
    local.start()

    def finish(k, carry):
        peer = lax.rem(me + k, n)
        outgoing(peer).wait_send()
        incoming(peer).wait_recv()
        return carry

    lax.fori_loop(1, n, finish, 0)
    local.wait()


def _exchange_kernel(n, gather, x_ref, o_ref, buf, send_sems, recv_sems, local_sem):
    me = lax.axis_index("seq")
    rep = lax.axis_index("rep")
    _greet(n, me, rep)
    source = (lambda peer: x_ref) if gather else (lambda peer: x_ref.at[peer])
    _spread(n, me, rep, source, buf, send_sems, recv_sems, local_sem)
    o_ref[...] = buf[...]


def _nbytes(shape, dtype):
    size = int(jnp.dtype(dtype).itemsize)
    for d in shape:
        size *= int(d)
    return size


def exchange(x, n, gather, cid):
    blk = x.shape if gather else x.shape[1:]
    shape = (n,) + tuple(blk)
    nbytes = _nbytes(shape, x.dtype)
    return pl.pallas_call(
        functools.partial(_exchange_kernel, n, gather),
        out_shape=jax.ShapeDtypeStruct(shape, x.dtype),
        in_specs=[pl.BlockSpec(memory_space=pltpu.VMEM)],
        out_specs=pl.BlockSpec(memory_space=pltpu.VMEM),
        scratch_shapes=[
            pltpu.VMEM(shape, x.dtype),
            pltpu.SemaphoreType.DMA((n,)),
            pltpu.SemaphoreType.DMA((n,)),
            pltpu.SemaphoreType.DMA(()),
        ],
        compiler_params=pltpu.CompilerParams(collective_id=cid, has_side_effects=True),
        cost_estimate=pl.CostEstimate(flops=0, transcendentals=0, bytes_accessed=2 * nbytes),
        name="exchange_%d" % cid,
    )(x)


def _two_phase_kernel(n, combine, n_extra, *refs):
    x_ref = refs[0]
    extras = refs[1 : 1 + n_extra]
    o_ref = refs[1 + n_extra]
    buf1, own, buf2, s1, r1, l1, s2, r2, l2 = refs[2 + n_extra :]
    me = lax.axis_index("seq")
    rep = lax.axis_index("rep")
    _greet(n, me, rep)
    _spread(n, me, rep, lambda peer: x_ref.at[peer], buf1, s1, r1, l1)
    own[...] = combine(buf1, *extras)
    _spread(n, me, rep, lambda peer: own, buf2, s2, r2, l2)
    o_ref[...] = buf2[...]


def two_phase(x, extras, combine, own_shape, own_dtype, n, cid):
    first = x.shape
    shape = (n,) + tuple(own_shape)
    nbytes = _nbytes(first, x.dtype) + _nbytes(shape, own_dtype)
    return pl.pallas_call(
        functools.partial(_two_phase_kernel, n, combine, len(extras)),
        out_shape=jax.ShapeDtypeStruct(shape, own_dtype),
        in_specs=[pl.BlockSpec(memory_space=pltpu.VMEM)] * (1 + len(extras)),
        out_specs=pl.BlockSpec(memory_space=pltpu.VMEM),
        scratch_shapes=[
            pltpu.VMEM(first, x.dtype),
            pltpu.VMEM(tuple(own_shape), own_dtype),
            pltpu.VMEM(shape, own_dtype),
            pltpu.SemaphoreType.DMA((n,)),
            pltpu.SemaphoreType.DMA((n,)),
            pltpu.SemaphoreType.DMA(()),
            pltpu.SemaphoreType.DMA((n,)),
            pltpu.SemaphoreType.DMA((n,)),
            pltpu.SemaphoreType.DMA(()),
        ],
        compiler_params=pltpu.CompilerParams(collective_id=cid, has_side_effects=True),
        cost_estimate=pl.CostEstimate(flops=0, transcendentals=0, bytes_accessed=2 * nbytes),
        name="two_phase_%d" % cid,
    )(x, *extras)


def _merge_combine(buf1, fresh_ref):
    blocks = buf1[...]
    fresh = fresh_ref[...]
    block_max = blocks[:, :, HD : HD + 1]
    fresh_max = fresh[:, HD : HD + 1]
    overall = jnp.maximum(jnp.max(block_max, axis=0), fresh_max)
    block_scale = jnp.exp(block_max - overall[None])
    fresh_scale = jnp.exp(fresh_max - overall)
    weighted = jnp.sum(block_scale * blocks, axis=0) + fresh_scale * fresh
    numer = weighted[:, :HD]
    denom = weighted[:, HD + 1 : HD + 2]
    return (numer / denom).astype(jnp.bfloat16)


def _down_combine(buf1, middle_ref):
    return (middle_ref[...] + branch_factor * jnp.sum(buf1[...], axis=0)).astype(jnp.bfloat16)


STEPS = 4
norm_epsilon = 1e-05
embed_factor = 12.0
score_factor = 0.015625
branch_factor = 0.22
rope_base = 10000000.0
masked_floor = -1e30


def rms_scale(resid, gain):
    mean_square = jnp.mean(resid * resid, axis=-1, keepdims=True)
    return resid * lax.rsqrt(mean_square + norm_epsilon) * gain.astype(jnp.float32)


def rotate(vectors, where):
    half = vectors.shape[-1] // 2
    freqs = rope_base ** (-2.0 * jnp.arange(half, dtype=jnp.float32) / vectors.shape[-1])
    angle = where[..., None] * freqs
    cosine = jnp.cos(angle)
    sine = jnp.sin(angle)
    first_half = vectors[..., :half]
    second_half = vectors[..., half:]
    return jnp.concatenate(
        [first_half * cosine - second_half * sine, second_half * cosine + first_half * sine],
        axis=-1,
    )


def partial_softmax(queries, keys, values, valid):
    scores = (
        jnp.einsum("rskgd,rpkd->rskgp", queries, keys, preferred_element_type=jnp.float32)
        * score_factor
    )
    maxima = jnp.max(jnp.where(valid, scores, masked_floor), axis=-1)
    expo = jnp.exp(jnp.where(valid, scores - maxima[..., None], masked_floor))
    totals = jnp.sum(expo, axis=-1)
    outputs = jnp.einsum(
        "rskgp,rpkd->rskgd", expo.astype(jnp.bfloat16), values, preferred_element_type=jnp.float32
    )
    return (maxima, totals, outputs)


def shards(
    token_ids,
    cache_lengths,
    embed_table,
    key_cache,
    value_cache,
    norm_attn,
    norm_mlp,
    w_qkv,
    w_out,
    w_gate,
    w_up,
    w_down,
):
    n = lax.axis_size("seq")
    place = lax.axis_index("seq")
    req_all = token_ids.shape[0]
    steps = token_ids.shape[1]
    rows = req_all * steps
    ctx_own = key_cache.shape[1]
    width = embed_table.shape[0] * n
    att_width = H * HD
    kv_width = KVH * HD
    group = H // KVH

    vocab = embed_table.shape[1]
    onehot = (
        token_ids.reshape(-1)[:, None] == jnp.arange(vocab, dtype=jnp.int32)[None, :]
    ).astype(embed_table.dtype)
    picked = lax.dot_general(
        onehot, embed_table, (((1,), (1,)), ((), ())), preferred_element_type=jnp.float32
    ).astype(embed_table.dtype)
    whole = exchange(picked, n, True, 0)
    resid = jnp.transpose(whole, (1, 0, 2)).reshape(rows, width).astype(jnp.float32) * embed_factor

    slot_pos = place * ctx_own + jnp.arange(ctx_own, dtype=jnp.int32)
    cache_valid = (slot_pos[None, :] < cache_lengths[:, None]).reshape(req_all, 1, 1, 1, ctx_own)
    cache_keys = key_cache.reshape(req_all, ctx_own, KVH, HD)
    cache_values = value_cache.reshape(req_all, ctx_own, KVH, HD)

    normed = rms_scale(resid, norm_attn).astype(jnp.bfloat16)
    qkv_cols = jnp.dot(normed, w_qkv, preferred_element_type=jnp.float32).astype(jnp.bfloat16)
    qkv_got = exchange(qkv_cols, n, True, 1)
    qkv_all = jnp.transpose(qkv_got, (1, 0, 2)).reshape(req_all, steps, -1)
    where = (cache_lengths[:, None] + jnp.arange(steps, dtype=jnp.int32)[None, :]).astype(
        jnp.float32
    )
    queries = rotate(
        qkv_all[..., :att_width].reshape(req_all, steps, H, HD).astype(jnp.float32),
        where[..., None],
    ).astype(jnp.bfloat16)
    keys_new = rotate(
        qkv_all[..., att_width : att_width + kv_width]
        .reshape(req_all, steps, KVH, HD)
        .astype(jnp.float32),
        where[..., None],
    ).astype(jnp.bfloat16)
    values_new = qkv_all[..., att_width + kv_width :].reshape(req_all, steps, KVH, HD)
    grouped = queries.reshape(req_all, steps, KVH, group, HD)
    cache_max, cache_total, cache_out = partial_softmax(
        grouped, cache_keys, cache_values, cache_valid
    )
    fresh_valid = (
        jnp.arange(steps, dtype=jnp.int32)[None, :] <= jnp.arange(steps, dtype=jnp.int32)[:, None]
    ).reshape(1, steps, 1, 1, steps)
    fresh_max, fresh_total, fresh_out = partial_softmax(grouped, keys_new, values_new, fresh_valid)

    pairs = rows * H // n
    lanes = 128
    packed = jnp.concatenate(
        [
            cache_out.reshape(n, pairs, HD),
            cache_max.reshape(n, pairs, 1),
            cache_total.reshape(n, pairs, 1),
            jnp.zeros((n, pairs, lanes - HD - 2), jnp.float32),
        ],
        axis=-1,
    )
    own_fresh_max = lax.dynamic_index_in_dim(fresh_max.reshape(n, pairs), place, 0, False)
    own_fresh_total = lax.dynamic_index_in_dim(fresh_total.reshape(n, pairs), place, 0, False)
    own_fresh_out = lax.dynamic_index_in_dim(fresh_out.reshape(n, pairs, HD), place, 0, False)
    fresh_packed = jnp.concatenate(
        [
            own_fresh_out,
            own_fresh_max[:, None],
            own_fresh_total[:, None],
            jnp.zeros((pairs, lanes - HD - 2), jnp.float32),
        ],
        axis=-1,
    )
    attention = two_phase(
        packed, [fresh_packed], _merge_combine, (pairs, HD), jnp.bfloat16, n, 2
    ).reshape(rows, att_width)

    proj_cols = jnp.dot(attention, w_out, preferred_element_type=jnp.float32).astype(jnp.bfloat16)
    proj_got = exchange(proj_cols, n, True, 3)
    projected = jnp.transpose(proj_got, (1, 0, 2)).reshape(rows, width)
    middle = resid + branch_factor * projected.astype(jnp.float32)
    normed_mlp = rms_scale(middle, norm_mlp).astype(jnp.bfloat16)
    gate = jnp.dot(normed_mlp, w_gate, preferred_element_type=jnp.float32)
    upward = jnp.dot(normed_mlp, w_up, preferred_element_type=jnp.float32)
    hidden = (jax.nn.silu(gate) * upward).astype(jnp.bfloat16)
    down_part = jnp.dot(hidden, w_down, preferred_element_type=jnp.float32)
    cols = width // n
    middle_own = lax.dynamic_slice_in_dim(middle, place * cols, cols, axis=1)
    down_send = jnp.transpose(down_part.reshape(rows, n, cols), (1, 0, 2))
    out_got = two_phase(down_send, [middle_own], _down_combine, (rows, cols), jnp.bfloat16, n, 4)
    return jnp.transpose(out_got, (1, 0, 2)).reshape(req_all, steps, width)


def solution(mesh):
    return jax.shard_map(
        shards,
        mesh=mesh,
        in_specs=(
            P("rep", None),
            P("rep"),
            P("seq", None),
            P("rep", "seq", None),
            P("rep", "seq", None),
            P(),
            P(),
            P(None, "seq"),
            P(None, "seq"),
            P(None, "seq"),
            P(None, "seq"),
            P("seq", None),
        ),
        out_specs=P("rep", None, None),
        check_vma=False,
    )
```

```python
import functools

import jax
import jax.numpy as jnp
from jax import lax
from jax.experimental import pallas as pl
from jax.experimental.pallas import tpu as pltpu
from jax.sharding import PartitionSpec as P

H = 32
KVH = 8
HD = 64

MESH_ID = pl.DeviceIdType.MESH


def _greet(n, me, rep):
    barrier = pltpu.get_barrier_semaphore()

    def greet(k, carry):
        peer = lax.rem(me + k, n)
        pl.semaphore_signal(barrier, inc=1, device_id=(peer, rep), device_id_type=MESH_ID)
        return carry

    lax.fori_loop(1, n, greet, 0)
    pl.semaphore_wait(barrier, n - 1)


def _spread(n, me, rep, source, buf, send_sems, recv_sems, local_sem):
    def outgoing(peer):
        return pltpu.make_async_remote_copy(
            src_ref=source(peer),
            dst_ref=buf.at[me],
            send_sem=send_sems.at[peer],
            recv_sem=recv_sems.at[me],
            device_id=(peer, rep),
            device_id_type=MESH_ID,
        )

    def incoming(peer):
        return pltpu.make_async_remote_copy(
            src_ref=source(peer),
            dst_ref=buf.at[peer],
            send_sem=send_sems.at[peer],
            recv_sem=recv_sems.at[peer],
            device_id=(peer, rep),
            device_id_type=MESH_ID,
        )

    def send(k, carry):
        outgoing(lax.rem(me + k, n)).start()
        return carry

    lax.fori_loop(1, n, send, 0)
    local = pltpu.make_async_copy(source(me), buf.at[me], local_sem)
    local.start()

    def finish(k, carry):
        peer = lax.rem(me + k, n)
        outgoing(peer).wait_send()
        incoming(peer).wait_recv()
        return carry

    lax.fori_loop(1, n, finish, 0)
    local.wait()


def _exchange_kernel(n, gather, x_ref, o_ref, buf, send_sems, recv_sems, local_sem):
    me = lax.axis_index("seq")
    rep = lax.axis_index("rep")
    _greet(n, me, rep)
    source = (lambda peer: x_ref) if gather else (lambda peer: x_ref.at[peer])
    _spread(n, me, rep, source, buf, send_sems, recv_sems, local_sem)
    o_ref[...] = buf[...]


def _nbytes(shape, dtype):
    size = int(jnp.dtype(dtype).itemsize)
    for d in shape:
        size *= int(d)
    return size


def exchange(x, n, gather, cid):
    blk = x.shape if gather else x.shape[1:]
    shape = (n,) + tuple(blk)
    nbytes = _nbytes(shape, x.dtype)
    return pl.pallas_call(
        functools.partial(_exchange_kernel, n, gather),
        out_shape=jax.ShapeDtypeStruct(shape, x.dtype),
        in_specs=[pl.BlockSpec(memory_space=pltpu.VMEM)],
        out_specs=pl.BlockSpec(memory_space=pltpu.VMEM),
        scratch_shapes=[
            pltpu.VMEM(shape, x.dtype),
            pltpu.SemaphoreType.DMA((n,)),
            pltpu.SemaphoreType.DMA((n,)),
            pltpu.SemaphoreType.DMA(()),
        ],
        compiler_params=pltpu.CompilerParams(collective_id=cid, has_side_effects=True),
        cost_estimate=pl.CostEstimate(flops=0, transcendentals=0, bytes_accessed=2 * nbytes),
        name="exchange_%d" % cid,
    )(x)


def _split(n):
    low = 1
    for c in range(1, n + 1):
        if n % c == 0 and c * c <= n:
            low = c
    return low


def _stage(m, mine, dev_of, rep, source, buf, send_sems, recv_sems, local_sem):
    def copy(j, slot):
        return pltpu.make_async_remote_copy(
            src_ref=source(j),
            dst_ref=buf.at[slot],
            send_sem=send_sems.at[j],
            recv_sem=recv_sems.at[slot],
            device_id=(dev_of(j), rep),
            device_id_type=MESH_ID,
        )

    def send(k, carry):
        j = lax.rem(mine + k, m)
        copy(j, mine).start()
        return carry

    lax.fori_loop(1, m, send, 0)
    local = pltpu.make_async_copy(source(mine), buf.at[mine], local_sem)
    local.start()

    def finish(k, carry):
        j = lax.rem(mine + k, m)
        copy(j, mine).wait_send()
        copy(j, j).wait_recv()
        return carry

    lax.fori_loop(1, m, finish, 0)
    local.wait()


def _greet2(low, high, hi, lo, rep):
    barrier = pltpu.get_barrier_semaphore()

    def near(k, carry):
        peer = hi * low + lax.rem(lo + k, low)
        pl.semaphore_signal(barrier, inc=1, device_id=(peer, rep), device_id_type=MESH_ID)
        return carry

    def far(k, carry):
        peer = lax.rem(hi + k, high) * low + lo
        pl.semaphore_signal(barrier, inc=1, device_id=(peer, rep), device_id_type=MESH_ID)
        return carry

    lax.fori_loop(1, low, near, 0)
    lax.fori_loop(1, high, far, 0)
    pl.semaphore_wait(barrier, low + high - 2)


def _gather2_kernel(n, low, x_ref, o_ref, buf1, buf2, s1, r1, l1, s2, r2, l2):
    high = n // low
    me = lax.axis_index("seq")
    rep = lax.axis_index("rep")
    hi = me // low
    lo = lax.rem(me, low)
    _greet2(low, high, hi, lo, rep)
    _stage(low, lo, lambda j: hi * low + j, rep, lambda j: x_ref, buf1, s1, r1, l1)
    _stage(high, hi, lambda j: j * low + lo, rep, lambda j: buf1, buf2, s2, r2, l2)
    o_ref[...] = buf2[...]


def gather2(x, n, cid):
    low = _split(n)
    high = n // low
    blk = tuple(x.shape)
    shape = (high, low) + blk
    nbytes = _nbytes(shape, x.dtype)
    out = pl.pallas_call(
        functools.partial(_gather2_kernel, n, low),
        out_shape=jax.ShapeDtypeStruct(shape, x.dtype),
        in_specs=[pl.BlockSpec(memory_space=pltpu.VMEM)],
        out_specs=pl.BlockSpec(memory_space=pltpu.VMEM),
        scratch_shapes=[
            pltpu.VMEM((low,) + blk, x.dtype),
            pltpu.VMEM(shape, x.dtype),
            pltpu.SemaphoreType.DMA((low,)),
            pltpu.SemaphoreType.DMA((low,)),
            pltpu.SemaphoreType.DMA(()),
            pltpu.SemaphoreType.DMA((high,)),
            pltpu.SemaphoreType.DMA((high,)),
            pltpu.SemaphoreType.DMA(()),
        ],
        compiler_params=pltpu.CompilerParams(collective_id=cid, has_side_effects=True),
        cost_estimate=pl.CostEstimate(flops=0, transcendentals=0, bytes_accessed=2 * nbytes),
        name="gather2_%d" % cid,
    )(x)
    return out.reshape((n,) + blk)


def _two_phase_kernel(n, combine, n_extra, *refs):
    x_ref = refs[0]
    extras = refs[1 : 1 + n_extra]
    o_ref = refs[1 + n_extra]
    buf1, own, buf2, s1, r1, l1, s2, r2, l2 = refs[2 + n_extra :]
    me = lax.axis_index("seq")
    rep = lax.axis_index("rep")
    _greet(n, me, rep)
    _spread(n, me, rep, lambda peer: x_ref.at[peer], buf1, s1, r1, l1)
    own[...] = combine(buf1, *extras)
    _spread(n, me, rep, lambda peer: own, buf2, s2, r2, l2)
    o_ref[...] = buf2[...]


def two_phase(x, extras, combine, own_shape, own_dtype, n, cid):
    first = x.shape
    shape = (n,) + tuple(own_shape)
    nbytes = _nbytes(first, x.dtype) + _nbytes(shape, own_dtype)
    return pl.pallas_call(
        functools.partial(_two_phase_kernel, n, combine, len(extras)),
        out_shape=jax.ShapeDtypeStruct(shape, own_dtype),
        in_specs=[pl.BlockSpec(memory_space=pltpu.VMEM)] * (1 + len(extras)),
        out_specs=pl.BlockSpec(memory_space=pltpu.VMEM),
        scratch_shapes=[
            pltpu.VMEM(first, x.dtype),
            pltpu.VMEM(tuple(own_shape), own_dtype),
            pltpu.VMEM(shape, own_dtype),
            pltpu.SemaphoreType.DMA((n,)),
            pltpu.SemaphoreType.DMA((n,)),
            pltpu.SemaphoreType.DMA(()),
            pltpu.SemaphoreType.DMA((n,)),
            pltpu.SemaphoreType.DMA((n,)),
            pltpu.SemaphoreType.DMA(()),
        ],
        compiler_params=pltpu.CompilerParams(collective_id=cid, has_side_effects=True),
        cost_estimate=pl.CostEstimate(flops=0, transcendentals=0, bytes_accessed=2 * nbytes),
        name="two_phase_%d" % cid,
    )(x, *extras)


def _merge_combine(buf1, fresh_ref):
    blocks = buf1[...]
    fresh = fresh_ref[...]
    block_max = blocks[:, :, HD : HD + 1]
    fresh_max = fresh[:, HD : HD + 1]
    overall = jnp.maximum(jnp.max(block_max, axis=0), fresh_max)
    block_scale = jnp.exp(block_max - overall[None])
    fresh_scale = jnp.exp(fresh_max - overall)
    weighted = jnp.sum(block_scale * blocks, axis=0) + fresh_scale * fresh
    numer = weighted[:, :HD]
    denom = weighted[:, HD + 1 : HD + 2]
    return (numer / denom).astype(jnp.bfloat16)


def _down_combine(buf1, middle_ref):
    return (middle_ref[...] + branch_factor * jnp.sum(buf1[...], axis=0)).astype(jnp.bfloat16)


STEPS = 4
norm_epsilon = 1e-05
embed_factor = 12.0
score_factor = 0.015625
branch_factor = 0.22
rope_base = 10000000.0
masked_floor = -1e30


def rms_scale(resid, gain):
    mean_square = jnp.mean(resid * resid, axis=-1, keepdims=True)
    return resid * lax.rsqrt(mean_square + norm_epsilon) * gain.astype(jnp.float32)


def rotate(vectors, where):
    half = vectors.shape[-1] // 2
    freqs = rope_base ** (-2.0 * jnp.arange(half, dtype=jnp.float32) / vectors.shape[-1])
    angle = where[..., None] * freqs
    cosine = jnp.cos(angle)
    sine = jnp.sin(angle)
    first_half = vectors[..., :half]
    second_half = vectors[..., half:]
    return jnp.concatenate(
        [first_half * cosine - second_half * sine, second_half * cosine + first_half * sine],
        axis=-1,
    )


def partial_softmax(queries, keys, values, valid):
    scores = (
        jnp.einsum("rskgd,rpkd->rskgp", queries, keys, preferred_element_type=jnp.float32)
        * score_factor
    )
    maxima = jnp.max(jnp.where(valid, scores, masked_floor), axis=-1)
    expo = jnp.exp(jnp.where(valid, scores - maxima[..., None], masked_floor))
    totals = jnp.sum(expo, axis=-1)
    outputs = jnp.einsum(
        "rskgp,rpkd->rskgd", expo.astype(jnp.bfloat16), values, preferred_element_type=jnp.float32
    )
    return (maxima, totals, outputs)


def shards(
    token_ids,
    cache_lengths,
    embed_table,
    key_cache,
    value_cache,
    norm_attn,
    norm_mlp,
    w_qkv,
    w_out,
    w_gate,
    w_up,
    w_down,
):
    n = lax.axis_size("seq")
    place = lax.axis_index("seq")
    req_all = token_ids.shape[0]
    steps = token_ids.shape[1]
    rows = req_all * steps
    ctx_own = key_cache.shape[1]
    width = embed_table.shape[0] * n
    att_width = H * HD
    kv_width = KVH * HD
    group = H // KVH

    vocab = embed_table.shape[1]
    onehot = (
        token_ids.reshape(-1)[:, None] == jnp.arange(vocab, dtype=jnp.int32)[None, :]
    ).astype(embed_table.dtype)
    picked = lax.dot_general(
        onehot, embed_table, (((1,), (1,)), ((), ())), preferred_element_type=jnp.float32
    ).astype(embed_table.dtype)
    whole = gather2(picked, n, 0)
    resid = jnp.transpose(whole, (1, 0, 2)).reshape(rows, width).astype(jnp.float32) * embed_factor

    slot_pos = place * ctx_own + jnp.arange(ctx_own, dtype=jnp.int32)
    cache_valid = (slot_pos[None, :] < cache_lengths[:, None]).reshape(req_all, 1, 1, 1, ctx_own)
    cache_keys = key_cache.reshape(req_all, ctx_own, KVH, HD)
    cache_values = value_cache.reshape(req_all, ctx_own, KVH, HD)

    normed = rms_scale(resid, norm_attn).astype(jnp.bfloat16)
    qkv_cols = jnp.dot(normed, w_qkv, preferred_element_type=jnp.float32).astype(jnp.bfloat16)
    qkv_got = gather2(qkv_cols, n, 1)
    qkv_all = jnp.transpose(qkv_got, (1, 0, 2)).reshape(req_all, steps, -1)
    where = (cache_lengths[:, None] + jnp.arange(steps, dtype=jnp.int32)[None, :]).astype(
        jnp.float32
    )
    queries = rotate(
        qkv_all[..., :att_width].reshape(req_all, steps, H, HD).astype(jnp.float32),
        where[..., None],
    ).astype(jnp.bfloat16)
    keys_new = rotate(
        qkv_all[..., att_width : att_width + kv_width]
        .reshape(req_all, steps, KVH, HD)
        .astype(jnp.float32),
        where[..., None],
    ).astype(jnp.bfloat16)
    values_new = qkv_all[..., att_width + kv_width :].reshape(req_all, steps, KVH, HD)
    grouped = queries.reshape(req_all, steps, KVH, group, HD)
    cache_max, cache_total, cache_out = partial_softmax(
        grouped, cache_keys, cache_values, cache_valid
    )
    fresh_valid = (
        jnp.arange(steps, dtype=jnp.int32)[None, :] <= jnp.arange(steps, dtype=jnp.int32)[:, None]
    ).reshape(1, steps, 1, 1, steps)
    fresh_max, fresh_total, fresh_out = partial_softmax(grouped, keys_new, values_new, fresh_valid)

    pairs = rows * H // n
    lanes = 128
    packed = jnp.concatenate(
        [
            cache_out.reshape(n, pairs, HD),
            cache_max.reshape(n, pairs, 1),
            cache_total.reshape(n, pairs, 1),
            jnp.zeros((n, pairs, lanes - HD - 2), jnp.float32),
        ],
        axis=-1,
    )
    own_fresh_max = lax.dynamic_index_in_dim(fresh_max.reshape(n, pairs), place, 0, False)
    own_fresh_total = lax.dynamic_index_in_dim(fresh_total.reshape(n, pairs), place, 0, False)
    own_fresh_out = lax.dynamic_index_in_dim(fresh_out.reshape(n, pairs, HD), place, 0, False)
    fresh_packed = jnp.concatenate(
        [
            own_fresh_out,
            own_fresh_max[:, None],
            own_fresh_total[:, None],
            jnp.zeros((pairs, lanes - HD - 2), jnp.float32),
        ],
        axis=-1,
    )
    attention = two_phase(
        packed, [fresh_packed], _merge_combine, (pairs, HD), jnp.bfloat16, n, 2
    ).reshape(rows, att_width)

    proj_cols = jnp.dot(attention, w_out, preferred_element_type=jnp.float32).astype(jnp.bfloat16)
    proj_got = gather2(proj_cols, n, 3)
    projected = jnp.transpose(proj_got, (1, 0, 2)).reshape(rows, width)
    middle = resid + branch_factor * projected.astype(jnp.float32)
    normed_mlp = rms_scale(middle, norm_mlp).astype(jnp.bfloat16)
    gate = jnp.dot(normed_mlp, w_gate, preferred_element_type=jnp.float32)
    upward = jnp.dot(normed_mlp, w_up, preferred_element_type=jnp.float32)
    hidden = (jax.nn.silu(gate) * upward).astype(jnp.bfloat16)
    down_part = jnp.dot(hidden, w_down, preferred_element_type=jnp.float32)
    cols = width // n
    middle_own = lax.dynamic_slice_in_dim(middle, place * cols, cols, axis=1)
    down_send = jnp.transpose(down_part.reshape(rows, n, cols), (1, 0, 2))
    out_got = two_phase(down_send, [middle_own], _down_combine, (rows, cols), jnp.bfloat16, n, 4)
    return jnp.transpose(out_got, (1, 0, 2)).reshape(req_all, steps, width)


def solution(mesh):
    return jax.shard_map(
        shards,
        mesh=mesh,
        in_specs=(
            P("rep", None),
            P("rep"),
            P("seq", None),
            P("rep", "seq", None),
            P("rep", "seq", None),
            P(),
            P(),
            P(None, "seq"),
            P(None, "seq"),
            P(None, "seq"),
            P(None, "seq"),
            P("seq", None),
        ),
        out_specs=P("rep", None, None),
        check_vma=False,
    )
```

```python
import functools

import jax
import jax.numpy as jnp
from jax import lax
from jax.experimental import pallas as pl
from jax.experimental.pallas import tpu as pltpu
from jax.sharding import PartitionSpec as P

H = 32
KVH = 8
HD = 64

MESH_ID = pl.DeviceIdType.MESH


def _greet(n, me, rep):
    barrier = pltpu.get_barrier_semaphore()

    def greet(k, carry):
        peer = lax.rem(me + k, n)
        pl.semaphore_signal(barrier, inc=1, device_id=(peer, rep), device_id_type=MESH_ID)
        return carry

    lax.fori_loop(1, n, greet, 0)
    pl.semaphore_wait(barrier, n - 1)


def _exchange_kernel(n, gather, x_ref, o_ref, buf, send_sems, recv_sems, local_sem):
    me = lax.axis_index("seq")
    rep = lax.axis_index("rep")
    _greet(n, me, rep)
    source = (lambda peer: x_ref) if gather else (lambda peer: x_ref.at[peer])
    _stage(n, me, lambda j: j, rep, source, buf, send_sems, recv_sems, local_sem)
    o_ref[...] = buf[...]


def _nbytes(shape, dtype):
    size = int(jnp.dtype(dtype).itemsize)
    for d in shape:
        size *= int(d)
    return size


def exchange(x, n, gather, cid):
    blk = x.shape if gather else x.shape[1:]
    shape = (n,) + tuple(blk)
    nbytes = _nbytes(shape, x.dtype)
    return pl.pallas_call(
        functools.partial(_exchange_kernel, n, gather),
        out_shape=jax.ShapeDtypeStruct(shape, x.dtype),
        in_specs=[pl.BlockSpec(memory_space=pltpu.VMEM)],
        out_specs=pl.BlockSpec(memory_space=pltpu.VMEM),
        scratch_shapes=[
            pltpu.VMEM(shape, x.dtype),
            pltpu.SemaphoreType.DMA(()),
            pltpu.SemaphoreType.DMA(()),
            pltpu.SemaphoreType.DMA(()),
        ],
        compiler_params=pltpu.CompilerParams(collective_id=cid, has_side_effects=True),
        cost_estimate=pl.CostEstimate(flops=0, transcendentals=0, bytes_accessed=2 * nbytes),
        name="exchange_%d" % cid,
    )(x)


def _split(n):
    low = 1
    for c in range(1, n + 1):
        if n % c == 0 and c * c <= n:
            low = c
    return low


def _stage(m, mine, dev_of, rep, source, buf, send_sem, recv_sem, local_sem):
    def copy(j, slot):
        return pltpu.make_async_remote_copy(
            src_ref=source(j),
            dst_ref=buf.at[slot],
            send_sem=send_sem,
            recv_sem=recv_sem,
            device_id=(dev_of(j), rep),
            device_id_type=MESH_ID,
        )

    def send(k, carry):
        j = lax.rem(mine + k, m)
        copy(j, mine).start()
        return carry

    lax.fori_loop(1, m, send, 0)
    local = pltpu.make_async_copy(source(mine), buf.at[mine], local_sem)
    local.start()
    rest = buf.at[pl.ds(0, m - 1)]
    every = pltpu.make_async_remote_copy(
        src_ref=rest,
        dst_ref=rest,
        send_sem=send_sem,
        recv_sem=recv_sem,
        device_id=(dev_of(lax.rem(mine + 1, m)), rep),
        device_id_type=MESH_ID,
    )
    every.wait_send()
    every.wait_recv()
    local.wait()


def _greet2(low, high, hi, lo, rep):
    barrier = pltpu.get_barrier_semaphore()

    def near(k, carry):
        peer = hi * low + lax.rem(lo + k, low)
        pl.semaphore_signal(barrier, inc=1, device_id=(peer, rep), device_id_type=MESH_ID)
        return carry

    def far(k, carry):
        peer = lax.rem(hi + k, high) * low + lo
        pl.semaphore_signal(barrier, inc=1, device_id=(peer, rep), device_id_type=MESH_ID)
        return carry

    lax.fori_loop(1, low, near, 0)
    lax.fori_loop(1, high, far, 0)
    pl.semaphore_wait(barrier, low + high - 2)


def _gather2_kernel(n, low, x_ref, o_ref, buf1, buf2, s1, r1, l1, s2, r2, l2):
    high = n // low
    me = lax.axis_index("seq")
    rep = lax.axis_index("rep")
    hi = me // low
    lo = lax.rem(me, low)
    _greet2(low, high, hi, lo, rep)
    _stage(low, lo, lambda j: hi * low + j, rep, lambda j: x_ref, buf1, s1, r1, l1)
    _stage(high, hi, lambda j: j * low + lo, rep, lambda j: buf1, buf2, s2, r2, l2)
    o_ref[...] = buf2[...]


def gather2(x, n, cid):
    low = _split(n)
    high = n // low
    blk = tuple(x.shape)
    shape = (high, low) + blk
    nbytes = _nbytes(shape, x.dtype)
    out = pl.pallas_call(
        functools.partial(_gather2_kernel, n, low),
        out_shape=jax.ShapeDtypeStruct(shape, x.dtype),
        in_specs=[pl.BlockSpec(memory_space=pltpu.VMEM)],
        out_specs=pl.BlockSpec(memory_space=pltpu.VMEM),
        scratch_shapes=[
            pltpu.VMEM((low,) + blk, x.dtype),
            pltpu.VMEM(shape, x.dtype),
            pltpu.SemaphoreType.DMA(()),
            pltpu.SemaphoreType.DMA(()),
            pltpu.SemaphoreType.DMA(()),
            pltpu.SemaphoreType.DMA(()),
            pltpu.SemaphoreType.DMA(()),
            pltpu.SemaphoreType.DMA(()),
        ],
        compiler_params=pltpu.CompilerParams(collective_id=cid, has_side_effects=True),
        cost_estimate=pl.CostEstimate(flops=0, transcendentals=0, bytes_accessed=2 * nbytes),
        name="gather2_%d" % cid,
    )(x)
    return out.reshape((n,) + blk)


def _two_phase_kernel(n, combine, n_extra, *refs):
    x_ref = refs[0]
    extras = refs[1 : 1 + n_extra]
    o_ref = refs[1 + n_extra]
    buf1, own, buf2, s1, r1, l1, s2, r2, l2 = refs[2 + n_extra :]
    me = lax.axis_index("seq")
    rep = lax.axis_index("rep")
    _greet(n, me, rep)
    _stage(n, me, lambda j: j, rep, lambda peer: x_ref.at[peer], buf1, s1, r1, l1)
    own[...] = combine(buf1, *extras)
    _stage(n, me, lambda j: j, rep, lambda peer: own, buf2, s2, r2, l2)
    o_ref[...] = buf2[...]


def two_phase(x, extras, combine, own_shape, own_dtype, n, cid):
    first = x.shape
    shape = (n,) + tuple(own_shape)
    nbytes = _nbytes(first, x.dtype) + _nbytes(shape, own_dtype)
    return pl.pallas_call(
        functools.partial(_two_phase_kernel, n, combine, len(extras)),
        out_shape=jax.ShapeDtypeStruct(shape, own_dtype),
        in_specs=[pl.BlockSpec(memory_space=pltpu.VMEM)] * (1 + len(extras)),
        out_specs=pl.BlockSpec(memory_space=pltpu.VMEM),
        scratch_shapes=[
            pltpu.VMEM(first, x.dtype),
            pltpu.VMEM(tuple(own_shape), own_dtype),
            pltpu.VMEM(shape, own_dtype),
            pltpu.SemaphoreType.DMA(()),
            pltpu.SemaphoreType.DMA(()),
            pltpu.SemaphoreType.DMA(()),
            pltpu.SemaphoreType.DMA(()),
            pltpu.SemaphoreType.DMA(()),
            pltpu.SemaphoreType.DMA(()),
        ],
        compiler_params=pltpu.CompilerParams(collective_id=cid, has_side_effects=True),
        cost_estimate=pl.CostEstimate(flops=0, transcendentals=0, bytes_accessed=2 * nbytes),
        name="two_phase_%d" % cid,
    )(x, *extras)


def _merge_combine(buf1, fresh_ref):
    blocks = buf1[...]
    fresh = fresh_ref[...]
    block_max = blocks[:, :, HD : HD + 1]
    fresh_max = fresh[:, HD : HD + 1]
    overall = jnp.maximum(jnp.max(block_max, axis=0), fresh_max)
    block_scale = jnp.exp(block_max - overall[None])
    fresh_scale = jnp.exp(fresh_max - overall)
    weighted = jnp.sum(block_scale * blocks, axis=0) + fresh_scale * fresh
    numer = weighted[:, :HD]
    denom = weighted[:, HD + 1 : HD + 2]
    return (numer / denom).astype(jnp.bfloat16)


def _down_combine(buf1, middle_ref):
    return (middle_ref[...] + branch_factor * jnp.sum(buf1[...], axis=0)).astype(jnp.bfloat16)


STEPS = 4
norm_epsilon = 1e-05
embed_factor = 12.0
score_factor = 0.015625
branch_factor = 0.22
rope_base = 10000000.0
masked_floor = -1e30


def rms_scale(resid, gain):
    mean_square = jnp.mean(resid * resid, axis=-1, keepdims=True)
    return resid * lax.rsqrt(mean_square + norm_epsilon) * gain.astype(jnp.float32)


def rotate(vectors, where):
    half = vectors.shape[-1] // 2
    freqs = rope_base ** (-2.0 * jnp.arange(half, dtype=jnp.float32) / vectors.shape[-1])
    angle = where[..., None] * freqs
    cosine = jnp.cos(angle)
    sine = jnp.sin(angle)
    first_half = vectors[..., :half]
    second_half = vectors[..., half:]
    return jnp.concatenate(
        [first_half * cosine - second_half * sine, second_half * cosine + first_half * sine],
        axis=-1,
    )


def partial_softmax(queries, keys, values, valid):
    scores = (
        jnp.einsum("rskgd,rpkd->rskgp", queries, keys, preferred_element_type=jnp.float32)
        * score_factor
    )
    maxima = jnp.max(jnp.where(valid, scores, masked_floor), axis=-1)
    expo = jnp.exp(jnp.where(valid, scores - maxima[..., None], masked_floor))
    totals = jnp.sum(expo, axis=-1)
    outputs = jnp.einsum(
        "rskgp,rpkd->rskgd", expo.astype(jnp.bfloat16), values, preferred_element_type=jnp.float32
    )
    return (maxima, totals, outputs)


def shards(
    token_ids,
    cache_lengths,
    embed_table,
    key_cache,
    value_cache,
    norm_attn,
    norm_mlp,
    w_qkv,
    w_out,
    w_gate,
    w_up,
    w_down,
):
    n = lax.axis_size("seq")
    place = lax.axis_index("seq")
    req_all = token_ids.shape[0]
    steps = token_ids.shape[1]
    rows = req_all * steps
    ctx_own = key_cache.shape[1]
    width = embed_table.shape[0] * n
    att_width = H * HD
    kv_width = KVH * HD
    group = H // KVH

    vocab = embed_table.shape[1]
    onehot = (
        token_ids.reshape(-1)[:, None] == jnp.arange(vocab, dtype=jnp.int32)[None, :]
    ).astype(embed_table.dtype)
    picked = lax.dot_general(
        onehot, embed_table, (((1,), (1,)), ((), ())), preferred_element_type=jnp.float32
    ).astype(embed_table.dtype)
    whole = gather2(picked, n, 0)
    resid = jnp.transpose(whole, (1, 0, 2)).reshape(rows, width).astype(jnp.float32) * embed_factor

    slot_pos = place * ctx_own + jnp.arange(ctx_own, dtype=jnp.int32)
    cache_valid = (slot_pos[None, :] < cache_lengths[:, None]).reshape(req_all, 1, 1, 1, ctx_own)
    cache_keys = key_cache.reshape(req_all, ctx_own, KVH, HD)
    cache_values = value_cache.reshape(req_all, ctx_own, KVH, HD)

    normed = rms_scale(resid, norm_attn).astype(jnp.bfloat16)
    qkv_cols = jnp.dot(normed, w_qkv, preferred_element_type=jnp.float32).astype(jnp.bfloat16)
    qkv_got = gather2(qkv_cols, n, 1)
    qkv_all = jnp.transpose(qkv_got, (1, 0, 2)).reshape(req_all, steps, -1)
    where = (cache_lengths[:, None] + jnp.arange(steps, dtype=jnp.int32)[None, :]).astype(
        jnp.float32
    )
    queries = rotate(
        qkv_all[..., :att_width].reshape(req_all, steps, H, HD).astype(jnp.float32),
        where[..., None],
    ).astype(jnp.bfloat16)
    keys_new = rotate(
        qkv_all[..., att_width : att_width + kv_width]
        .reshape(req_all, steps, KVH, HD)
        .astype(jnp.float32),
        where[..., None],
    ).astype(jnp.bfloat16)
    values_new = qkv_all[..., att_width + kv_width :].reshape(req_all, steps, KVH, HD)
    grouped = queries.reshape(req_all, steps, KVH, group, HD)
    cache_max, cache_total, cache_out = partial_softmax(
        grouped, cache_keys, cache_values, cache_valid
    )
    fresh_valid = (
        jnp.arange(steps, dtype=jnp.int32)[None, :] <= jnp.arange(steps, dtype=jnp.int32)[:, None]
    ).reshape(1, steps, 1, 1, steps)
    fresh_max, fresh_total, fresh_out = partial_softmax(grouped, keys_new, values_new, fresh_valid)

    pairs = rows * H // n
    lanes = 128
    packed = jnp.concatenate(
        [
            cache_out.reshape(n, pairs, HD),
            cache_max.reshape(n, pairs, 1),
            cache_total.reshape(n, pairs, 1),
            jnp.zeros((n, pairs, lanes - HD - 2), jnp.float32),
        ],
        axis=-1,
    )
    own_fresh_max = lax.dynamic_index_in_dim(fresh_max.reshape(n, pairs), place, 0, False)
    own_fresh_total = lax.dynamic_index_in_dim(fresh_total.reshape(n, pairs), place, 0, False)
    own_fresh_out = lax.dynamic_index_in_dim(fresh_out.reshape(n, pairs, HD), place, 0, False)
    fresh_packed = jnp.concatenate(
        [
            own_fresh_out,
            own_fresh_max[:, None],
            own_fresh_total[:, None],
            jnp.zeros((pairs, lanes - HD - 2), jnp.float32),
        ],
        axis=-1,
    )
    attention = two_phase(
        packed, [fresh_packed], _merge_combine, (pairs, HD), jnp.bfloat16, n, 2
    ).reshape(rows, att_width)

    proj_cols = jnp.dot(attention, w_out, preferred_element_type=jnp.float32).astype(jnp.bfloat16)
    proj_got = gather2(proj_cols, n, 3)
    projected = jnp.transpose(proj_got, (1, 0, 2)).reshape(rows, width)
    middle = resid + branch_factor * projected.astype(jnp.float32)
    normed_mlp = rms_scale(middle, norm_mlp).astype(jnp.bfloat16)
    gate = jnp.dot(normed_mlp, w_gate, preferred_element_type=jnp.float32)
    upward = jnp.dot(normed_mlp, w_up, preferred_element_type=jnp.float32)
    hidden = (jax.nn.silu(gate) * upward).astype(jnp.bfloat16)
    down_part = jnp.dot(hidden, w_down, preferred_element_type=jnp.float32)
    cols = width // n
    middle_own = lax.dynamic_slice_in_dim(middle, place * cols, cols, axis=1)
    down_send = jnp.transpose(down_part.reshape(rows, n, cols), (1, 0, 2))
    out_got = two_phase(down_send, [middle_own], _down_combine, (rows, cols), jnp.bfloat16, n, 4)
    return jnp.transpose(out_got, (1, 0, 2)).reshape(req_all, steps, width)


def solution(mesh):
    return jax.shard_map(
        shards,
        mesh=mesh,
        in_specs=(
            P("rep", None),
            P("rep"),
            P("seq", None),
            P("rep", "seq", None),
            P("rep", "seq", None),
            P(),
            P(),
            P(None, "seq"),
            P(None, "seq"),
            P(None, "seq"),
            P(None, "seq"),
            P("seq", None),
        ),
        out_specs=P("rep", None, None),
        check_vma=False,
    )
```

```python
import functools

import jax
import jax.numpy as jnp
from jax import lax
from jax.experimental import pallas as pl
from jax.experimental.pallas import tpu as pltpu
from jax.sharding import PartitionSpec as P

H = 32
KVH = 8
HD = 64

MESH_ID = pl.DeviceIdType.MESH


def _greet(n, me, rep):
    barrier = pltpu.get_barrier_semaphore()

    def greet(k, carry):
        peer = lax.rem(me + k, n)
        pl.semaphore_signal(barrier, inc=1, device_id=(peer, rep), device_id_type=MESH_ID)
        return carry

    lax.fori_loop(1, n, greet, 0)
    pl.semaphore_wait(barrier, n - 1)


def _exchange_kernel(n, gather, x_ref, o_ref, buf, send_sems, recv_sems, local_sem):
    me = lax.axis_index("seq")
    rep = lax.axis_index("rep")
    _greet(n, me, rep)
    source = (lambda peer: x_ref) if gather else (lambda peer: x_ref.at[peer])
    _stage(n, me, lambda j: j, rep, source, buf, send_sems, recv_sems, local_sem)
    o_ref[...] = buf[...]


def _nbytes(shape, dtype):
    size = int(jnp.dtype(dtype).itemsize)
    for d in shape:
        size *= int(d)
    return size


def exchange(x, n, gather, cid):
    blk = x.shape if gather else x.shape[1:]
    shape = (n,) + tuple(blk)
    nbytes = _nbytes(shape, x.dtype)
    return pl.pallas_call(
        functools.partial(_exchange_kernel, n, gather),
        out_shape=jax.ShapeDtypeStruct(shape, x.dtype),
        in_specs=[pl.BlockSpec(memory_space=pltpu.VMEM)],
        out_specs=pl.BlockSpec(memory_space=pltpu.VMEM),
        scratch_shapes=[
            pltpu.VMEM(shape, x.dtype),
            pltpu.SemaphoreType.DMA(()),
            pltpu.SemaphoreType.DMA(()),
            pltpu.SemaphoreType.DMA(()),
        ],
        compiler_params=pltpu.CompilerParams(collective_id=cid, has_side_effects=True),
        cost_estimate=pl.CostEstimate(flops=0, transcendentals=0, bytes_accessed=2 * nbytes),
        name="exchange_%d" % cid,
    )(x)


def _split(n):
    low = 1
    for c in range(1, n + 1):
        if n % c == 0 and c * c <= n:
            low = c
    return low


def _stage(m, mine, dev_of, rep, source, buf, send_sem, recv_sem, local_sem):
    def copy(j, slot):
        return pltpu.make_async_remote_copy(
            src_ref=source(j),
            dst_ref=buf.at[slot],
            send_sem=send_sem,
            recv_sem=recv_sem,
            device_id=(dev_of(j), rep),
            device_id_type=MESH_ID,
        )

    def send(k, carry):
        j = lax.rem(mine + k, m)
        copy(j, mine).start()
        return carry

    lax.fori_loop(1, m, send, 0)
    local = pltpu.make_async_copy(source(mine), buf.at[mine], local_sem)
    local.start()
    rest = buf.at[pl.ds(0, m - 1)]
    every = pltpu.make_async_remote_copy(
        src_ref=rest,
        dst_ref=rest,
        send_sem=send_sem,
        recv_sem=recv_sem,
        device_id=(dev_of(lax.rem(mine + 1, m)), rep),
        device_id_type=MESH_ID,
    )
    every.wait_send()
    every.wait_recv()
    local.wait()


def _greet2(low, high, hi, lo, rep):
    barrier = pltpu.get_barrier_semaphore()

    def near(k, carry):
        peer = hi * low + lax.rem(lo + k, low)
        pl.semaphore_signal(barrier, inc=1, device_id=(peer, rep), device_id_type=MESH_ID)
        return carry

    def far(k, carry):
        peer = lax.rem(hi + k, high) * low + lo
        pl.semaphore_signal(barrier, inc=1, device_id=(peer, rep), device_id_type=MESH_ID)
        return carry

    lax.fori_loop(1, low, near, 0)
    lax.fori_loop(1, high, far, 0)
    pl.semaphore_wait(barrier, low + high - 2)


def _gather2_kernel(n, low, x_ref, o_ref, buf1, buf2, s1, r1, l1, s2, r2, l2):
    high = n // low
    me = lax.axis_index("seq")
    rep = lax.axis_index("rep")
    hi = me // low
    lo = lax.rem(me, low)
    _greet2(low, high, hi, lo, rep)
    _stage(low, lo, lambda j: hi * low + j, rep, lambda j: x_ref, buf1, s1, r1, l1)
    _stage(high, hi, lambda j: j * low + lo, rep, lambda j: buf1, buf2, s2, r2, l2)
    o_ref[...] = buf2[...]


def gather2(x, n, cid):
    low = _split(n)
    high = n // low
    blk = tuple(x.shape)
    shape = (high, low) + blk
    nbytes = _nbytes(shape, x.dtype)
    out = pl.pallas_call(
        functools.partial(_gather2_kernel, n, low),
        out_shape=jax.ShapeDtypeStruct(shape, x.dtype),
        in_specs=[pl.BlockSpec(memory_space=pltpu.VMEM)],
        out_specs=pl.BlockSpec(memory_space=pltpu.VMEM),
        scratch_shapes=[
            pltpu.VMEM((low,) + blk, x.dtype),
            pltpu.VMEM(shape, x.dtype),
            pltpu.SemaphoreType.DMA(()),
            pltpu.SemaphoreType.DMA(()),
            pltpu.SemaphoreType.DMA(()),
            pltpu.SemaphoreType.DMA(()),
            pltpu.SemaphoreType.DMA(()),
            pltpu.SemaphoreType.DMA(()),
        ],
        compiler_params=pltpu.CompilerParams(collective_id=cid, has_side_effects=True),
        cost_estimate=pl.CostEstimate(flops=0, transcendentals=0, bytes_accessed=2 * nbytes),
        name="gather2_%d" % cid,
    )(x)
    return out.reshape((n,) + blk)


def _two_phase_kernel(n, combine, n_extra, *refs):
    x_ref = refs[0]
    extras = refs[1 : 1 + n_extra]
    o_ref = refs[1 + n_extra]
    buf1, own, buf2, s1, r1, l1, s2, r2, l2 = refs[2 + n_extra :]
    me = lax.axis_index("seq")
    rep = lax.axis_index("rep")
    _greet(n, me, rep)
    _stage(n, me, lambda j: j, rep, lambda peer: x_ref.at[peer], buf1, s1, r1, l1)
    own[...] = combine(buf1, *extras)
    _stage(n, me, lambda j: j, rep, lambda peer: own, buf2, s2, r2, l2)
    o_ref[...] = buf2[...]


def two_phase(x, extras, combine, own_shape, own_dtype, n, cid):
    first = x.shape
    shape = (n,) + tuple(own_shape)
    nbytes = _nbytes(first, x.dtype) + _nbytes(shape, own_dtype)
    return pl.pallas_call(
        functools.partial(_two_phase_kernel, n, combine, len(extras)),
        out_shape=jax.ShapeDtypeStruct(shape, own_dtype),
        in_specs=[pl.BlockSpec(memory_space=pltpu.VMEM)] * (1 + len(extras)),
        out_specs=pl.BlockSpec(memory_space=pltpu.VMEM),
        scratch_shapes=[
            pltpu.VMEM(first, x.dtype),
            pltpu.VMEM(tuple(own_shape), own_dtype),
            pltpu.VMEM(shape, own_dtype),
            pltpu.SemaphoreType.DMA(()),
            pltpu.SemaphoreType.DMA(()),
            pltpu.SemaphoreType.DMA(()),
            pltpu.SemaphoreType.DMA(()),
            pltpu.SemaphoreType.DMA(()),
            pltpu.SemaphoreType.DMA(()),
        ],
        compiler_params=pltpu.CompilerParams(collective_id=cid, has_side_effects=True),
        cost_estimate=pl.CostEstimate(flops=0, transcendentals=0, bytes_accessed=2 * nbytes),
        name="two_phase_%d" % cid,
    )(x, *extras)


def _mlp_kernel(
    n, proj_ref, resid_ref, gain_ref, gate_w_ref, up_w_ref, down_w_ref, o_ref,
    pbuf, mid, dsend, dbuf, own, obuf, s1, r1, l1, s2, r2, l2, s3, r3, l3,
):
    me = lax.axis_index("seq")
    rep = lax.axis_index("rep")
    cols, rows = own.shape
    _greet(n, me, rep)
    _stage(n, me, lambda j: j, rep, lambda j: proj_ref, pbuf, s1, r1, l1)
    projected = pbuf[...].astype(jnp.float32).reshape(n * cols, rows)
    middle = resid_ref[...] + branch_factor * projected
    mid[...] = middle.reshape(n, cols, rows)
    mean_square = jnp.mean(middle * middle, axis=0, keepdims=True)
    normed = (middle * lax.rsqrt(mean_square + norm_epsilon) * gain_ref[...]).astype(jnp.bfloat16)
    gate = jnp.dot(gate_w_ref[...], normed, preferred_element_type=jnp.float32)
    upward = jnp.dot(up_w_ref[...], normed, preferred_element_type=jnp.float32)
    hidden = (gate / (1.0 + jnp.exp(-gate)) * upward).astype(jnp.bfloat16)
    down = jnp.dot(down_w_ref[...], hidden, preferred_element_type=jnp.float32)
    dsend[...] = down.reshape(n, cols, rows)
    _stage(n, me, lambda j: j, rep, lambda j: dsend.at[j], dbuf, s2, r2, l2)
    total = jnp.sum(dbuf[...], axis=0)
    own[...] = (mid[me] + branch_factor * total).astype(jnp.bfloat16)
    _stage(n, me, lambda j: j, rep, lambda j: own, obuf, s3, r3, l3)
    o_ref[...] = obuf[...]


def mlp_block(proj_t, resid_t, gain, gate_w_t, up_w_t, down_w_t, n, cid):
    cols, rows = proj_t.shape
    width = n * cols
    sems = [pltpu.SemaphoreType.DMA(())] * 9
    flops = 2 * rows * width * gate_w_t.shape[0] * 3
    return pl.pallas_call(
        functools.partial(_mlp_kernel, n),
        out_shape=jax.ShapeDtypeStruct((n, cols, rows), jnp.bfloat16),
        in_specs=[pl.BlockSpec(memory_space=pltpu.VMEM)] * 6,
        out_specs=pl.BlockSpec(memory_space=pltpu.VMEM),
        scratch_shapes=[
            pltpu.VMEM((n, cols, rows), jnp.bfloat16),
            pltpu.VMEM((n, cols, rows), jnp.float32),
            pltpu.VMEM((n, cols, rows), jnp.float32),
            pltpu.VMEM((n, cols, rows), jnp.float32),
            pltpu.VMEM((cols, rows), jnp.bfloat16),
            pltpu.VMEM((n, cols, rows), jnp.bfloat16),
        ]
        + sems,
        compiler_params=pltpu.CompilerParams(collective_id=cid, has_side_effects=True),
        cost_estimate=pl.CostEstimate(
            flops=flops, transcendentals=rows * gate_w_t.shape[0], bytes_accessed=3 * 2 * width * gate_w_t.shape[0]
        ),
        name="mlp_block_%d" % cid,
    )(proj_t, resid_t, gain, gate_w_t, up_w_t, down_w_t)


def _merge_combine(buf1, fresh_ref):
    blocks = buf1[...]
    fresh = fresh_ref[...]
    block_max = blocks[:, :, HD : HD + 1]
    fresh_max = fresh[:, HD : HD + 1]
    overall = jnp.maximum(jnp.max(block_max, axis=0), fresh_max)
    block_scale = jnp.exp(block_max - overall[None])
    fresh_scale = jnp.exp(fresh_max - overall)
    weighted = jnp.sum(block_scale * blocks, axis=0) + fresh_scale * fresh
    numer = weighted[:, :HD]
    denom = weighted[:, HD + 1 : HD + 2]
    return (numer / denom).astype(jnp.bfloat16)


def _down_combine(buf1, middle_ref):
    return (middle_ref[...] + branch_factor * jnp.sum(buf1[...], axis=0)).astype(jnp.bfloat16)


STEPS = 4
norm_epsilon = 1e-05
embed_factor = 12.0
score_factor = 0.015625
branch_factor = 0.22
rope_base = 10000000.0
masked_floor = -1e30


def rms_scale(resid, gain):
    mean_square = jnp.mean(resid * resid, axis=-1, keepdims=True)
    return resid * lax.rsqrt(mean_square + norm_epsilon) * gain.astype(jnp.float32)


def rotate(vectors, where):
    half = vectors.shape[-1] // 2
    freqs = rope_base ** (-2.0 * jnp.arange(half, dtype=jnp.float32) / vectors.shape[-1])
    angle = where[..., None] * freqs
    cosine = jnp.cos(angle)
    sine = jnp.sin(angle)
    first_half = vectors[..., :half]
    second_half = vectors[..., half:]
    return jnp.concatenate(
        [first_half * cosine - second_half * sine, second_half * cosine + first_half * sine],
        axis=-1,
    )


def partial_softmax(queries, keys, values, valid):
    scores = (
        jnp.einsum("rskgd,rpkd->rskgp", queries, keys, preferred_element_type=jnp.float32)
        * score_factor
    )
    maxima = jnp.max(jnp.where(valid, scores, masked_floor), axis=-1)
    expo = jnp.exp(jnp.where(valid, scores - maxima[..., None], masked_floor))
    totals = jnp.sum(expo, axis=-1)
    outputs = jnp.einsum(
        "rskgp,rpkd->rskgd", expo.astype(jnp.bfloat16), values, preferred_element_type=jnp.float32
    )
    return (maxima, totals, outputs)


def shards(
    token_ids,
    cache_lengths,
    embed_table,
    key_cache,
    value_cache,
    norm_attn,
    norm_mlp,
    w_qkv,
    w_out,
    w_gate,
    w_up,
    w_down,
):
    n = lax.axis_size("seq")
    place = lax.axis_index("seq")
    req_all = token_ids.shape[0]
    steps = token_ids.shape[1]
    rows = req_all * steps
    ctx_own = key_cache.shape[1]
    width = embed_table.shape[0] * n
    att_width = H * HD
    kv_width = KVH * HD
    group = H // KVH

    vocab = embed_table.shape[1]
    onehot = (
        token_ids.reshape(-1)[:, None] == jnp.arange(vocab, dtype=jnp.int32)[None, :]
    ).astype(embed_table.dtype)
    picked = lax.dot_general(
        onehot, embed_table, (((1,), (1,)), ((), ())), preferred_element_type=jnp.float32
    ).astype(embed_table.dtype)
    whole = exchange(picked, n, True, 0)
    resid = jnp.transpose(whole, (1, 0, 2)).reshape(rows, width).astype(jnp.float32) * embed_factor

    slot_pos = place * ctx_own + jnp.arange(ctx_own, dtype=jnp.int32)
    cache_valid = (slot_pos[None, :] < cache_lengths[:, None]).reshape(req_all, 1, 1, 1, ctx_own)
    cache_keys = key_cache.reshape(req_all, ctx_own, KVH, HD)
    cache_values = value_cache.reshape(req_all, ctx_own, KVH, HD)

    normed = rms_scale(resid, norm_attn).astype(jnp.bfloat16)
    qkv_cols = jnp.dot(normed, w_qkv, preferred_element_type=jnp.float32).astype(jnp.bfloat16)
    qkv_got = exchange(qkv_cols, n, True, 1)
    qkv_all = jnp.transpose(qkv_got, (1, 0, 2)).reshape(req_all, steps, -1)
    where = (cache_lengths[:, None] + jnp.arange(steps, dtype=jnp.int32)[None, :]).astype(
        jnp.float32
    )
    queries = rotate(
        qkv_all[..., :att_width].reshape(req_all, steps, H, HD).astype(jnp.float32),
        where[..., None],
    ).astype(jnp.bfloat16)
    keys_new = rotate(
        qkv_all[..., att_width : att_width + kv_width]
        .reshape(req_all, steps, KVH, HD)
        .astype(jnp.float32),
        where[..., None],
    ).astype(jnp.bfloat16)
    values_new = qkv_all[..., att_width + kv_width :].reshape(req_all, steps, KVH, HD)
    grouped = queries.reshape(req_all, steps, KVH, group, HD)
    cache_max, cache_total, cache_out = partial_softmax(
        grouped, cache_keys, cache_values, cache_valid
    )
    fresh_valid = (
        jnp.arange(steps, dtype=jnp.int32)[None, :] <= jnp.arange(steps, dtype=jnp.int32)[:, None]
    ).reshape(1, steps, 1, 1, steps)
    fresh_max, fresh_total, fresh_out = partial_softmax(grouped, keys_new, values_new, fresh_valid)

    pairs = rows * H // n
    lanes = 128
    packed = jnp.concatenate(
        [
            cache_out.reshape(n, pairs, HD),
            cache_max.reshape(n, pairs, 1),
            cache_total.reshape(n, pairs, 1),
            jnp.zeros((n, pairs, lanes - HD - 2), jnp.float32),
        ],
        axis=-1,
    )
    own_fresh_max = lax.dynamic_index_in_dim(fresh_max.reshape(n, pairs), place, 0, False)
    own_fresh_total = lax.dynamic_index_in_dim(fresh_total.reshape(n, pairs), place, 0, False)
    own_fresh_out = lax.dynamic_index_in_dim(fresh_out.reshape(n, pairs, HD), place, 0, False)
    fresh_packed = jnp.concatenate(
        [
            own_fresh_out,
            own_fresh_max[:, None],
            own_fresh_total[:, None],
            jnp.zeros((pairs, lanes - HD - 2), jnp.float32),
        ],
        axis=-1,
    )
    attention = two_phase(
        packed, [fresh_packed], _merge_combine, (pairs, HD), jnp.bfloat16, n, 2
    ).reshape(rows, att_width)

    proj_cols = jnp.dot(attention, w_out, preferred_element_type=jnp.float32).astype(jnp.bfloat16)
    cols = width // n
    out_got = mlp_block(
        jnp.transpose(proj_cols, (1, 0)),
        jnp.transpose(resid, (1, 0)),
        norm_mlp.astype(jnp.float32).reshape(width, 1),
        jnp.transpose(w_gate, (1, 0)),
        jnp.transpose(w_up, (1, 0)),
        jnp.transpose(w_down, (1, 0)),
        n,
        3,
    )
    return jnp.transpose(out_got, (2, 0, 1)).reshape(req_all, steps, width)


def solution(mesh):
    return jax.shard_map(
        shards,
        mesh=mesh,
        in_specs=(
            P("rep", None),
            P("rep"),
            P("seq", None),
            P("rep", "seq", None),
            P("rep", "seq", None),
            P(),
            P(),
            P(None, "seq"),
            P(None, "seq"),
            P(None, "seq"),
            P(None, "seq"),
            P("seq", None),
        ),
        out_specs=P("rep", None, None),
        check_vma=False,
    )
```

```python
import functools

import jax
import jax.numpy as jnp
from jax import lax
from jax.experimental import pallas as pl
from jax.experimental.pallas import tpu as pltpu
from jax.sharding import PartitionSpec as P

H = 32
KVH = 8
HD = 64

MESH_ID = pl.DeviceIdType.MESH


def _greet(n, me, rep):
    barrier = pltpu.get_barrier_semaphore()

    def greet(k, carry):
        peer = lax.rem(me + k, n)
        pl.semaphore_signal(barrier, inc=1, device_id=(peer, rep), device_id_type=MESH_ID)
        return carry

    lax.fori_loop(1, n, greet, 0)
    pl.semaphore_wait(barrier, n - 1)


def _exchange_kernel(n, gather, x_ref, o_ref, buf, send_sems, recv_sems, local_sem):
    me = lax.axis_index("seq")
    rep = lax.axis_index("rep")
    _greet(n, me, rep)
    source = (lambda peer: x_ref) if gather else (lambda peer: x_ref.at[peer])
    _stage(n, me, lambda j: j, rep, source, buf, send_sems, recv_sems, local_sem)
    o_ref[...] = buf[...]


def _nbytes(shape, dtype):
    size = int(jnp.dtype(dtype).itemsize)
    for d in shape:
        size *= int(d)
    return size


def exchange(x, n, gather, cid):
    blk = x.shape if gather else x.shape[1:]
    shape = (n,) + tuple(blk)
    nbytes = _nbytes(shape, x.dtype)
    return pl.pallas_call(
        functools.partial(_exchange_kernel, n, gather),
        out_shape=jax.ShapeDtypeStruct(shape, x.dtype),
        in_specs=[pl.BlockSpec(memory_space=pltpu.VMEM)],
        out_specs=pl.BlockSpec(memory_space=pltpu.VMEM),
        scratch_shapes=[
            pltpu.VMEM(shape, x.dtype),
            pltpu.SemaphoreType.DMA(()),
            pltpu.SemaphoreType.DMA(()),
            pltpu.SemaphoreType.DMA(()),
        ],
        compiler_params=pltpu.CompilerParams(collective_id=cid, has_side_effects=True),
        cost_estimate=pl.CostEstimate(flops=0, transcendentals=0, bytes_accessed=2 * nbytes),
        name="exchange_%d" % cid,
    )(x)


def _split(n):
    low = 1
    for c in range(1, n + 1):
        if n % c == 0 and c * c <= n:
            low = c
    return low


def _stage(m, mine, dev_of, rep, source, buf, send_sem, recv_sem, local_sem):
    def copy(j, slot):
        return pltpu.make_async_remote_copy(
            src_ref=source(j),
            dst_ref=buf.at[slot],
            send_sem=send_sem,
            recv_sem=recv_sem,
            device_id=(dev_of(j), rep),
            device_id_type=MESH_ID,
        )

    def send(k, carry):
        j = lax.rem(mine + k, m)
        copy(j, mine).start()
        return carry

    lax.fori_loop(1, m, send, 0)
    local = pltpu.make_async_copy(source(mine), buf.at[mine], local_sem)
    local.start()
    rest = buf.at[pl.ds(0, m - 1)]
    every = pltpu.make_async_remote_copy(
        src_ref=rest,
        dst_ref=rest,
        send_sem=send_sem,
        recv_sem=recv_sem,
        device_id=(dev_of(lax.rem(mine + 1, m)), rep),
        device_id_type=MESH_ID,
    )
    every.wait_send()
    every.wait_recv()
    local.wait()


def _greet2(low, high, hi, lo, rep):
    barrier = pltpu.get_barrier_semaphore()

    def near(k, carry):
        peer = hi * low + lax.rem(lo + k, low)
        pl.semaphore_signal(barrier, inc=1, device_id=(peer, rep), device_id_type=MESH_ID)
        return carry

    def far(k, carry):
        peer = lax.rem(hi + k, high) * low + lo
        pl.semaphore_signal(barrier, inc=1, device_id=(peer, rep), device_id_type=MESH_ID)
        return carry

    lax.fori_loop(1, low, near, 0)
    lax.fori_loop(1, high, far, 0)
    pl.semaphore_wait(barrier, low + high - 2)


def _gather2_kernel(n, low, x_ref, o_ref, buf1, buf2, s1, r1, l1, s2, r2, l2):
    high = n // low
    me = lax.axis_index("seq")
    rep = lax.axis_index("rep")
    hi = me // low
    lo = lax.rem(me, low)
    _greet2(low, high, hi, lo, rep)
    _stage(low, lo, lambda j: hi * low + j, rep, lambda j: x_ref, buf1, s1, r1, l1)
    _stage(high, hi, lambda j: j * low + lo, rep, lambda j: buf1, buf2, s2, r2, l2)
    o_ref[...] = buf2[...]


def gather2(x, n, cid):
    low = _split(n)
    high = n // low
    blk = tuple(x.shape)
    shape = (high, low) + blk
    nbytes = _nbytes(shape, x.dtype)
    out = pl.pallas_call(
        functools.partial(_gather2_kernel, n, low),
        out_shape=jax.ShapeDtypeStruct(shape, x.dtype),
        in_specs=[pl.BlockSpec(memory_space=pltpu.VMEM)],
        out_specs=pl.BlockSpec(memory_space=pltpu.VMEM),
        scratch_shapes=[
            pltpu.VMEM((low,) + blk, x.dtype),
            pltpu.VMEM(shape, x.dtype),
            pltpu.SemaphoreType.DMA(()),
            pltpu.SemaphoreType.DMA(()),
            pltpu.SemaphoreType.DMA(()),
            pltpu.SemaphoreType.DMA(()),
            pltpu.SemaphoreType.DMA(()),
            pltpu.SemaphoreType.DMA(()),
        ],
        compiler_params=pltpu.CompilerParams(collective_id=cid, has_side_effects=True),
        cost_estimate=pl.CostEstimate(flops=0, transcendentals=0, bytes_accessed=2 * nbytes),
        name="gather2_%d" % cid,
    )(x)
    return out.reshape((n,) + blk)


def _two_phase_kernel(n, combine, n_extra, *refs):
    x_ref = refs[0]
    extras = refs[1 : 1 + n_extra]
    o_ref = refs[1 + n_extra]
    buf1, own, buf2, s1, r1, l1, s2, r2, l2 = refs[2 + n_extra :]
    me = lax.axis_index("seq")
    rep = lax.axis_index("rep")
    _greet(n, me, rep)
    _stage(n, me, lambda j: j, rep, lambda peer: x_ref.at[peer], buf1, s1, r1, l1)
    own[...] = combine(buf1, *extras)
    _stage(n, me, lambda j: j, rep, lambda peer: own, buf2, s2, r2, l2)
    o_ref[...] = buf2[...]


def two_phase(x, extras, combine, own_shape, own_dtype, n, cid):
    first = x.shape
    shape = (n,) + tuple(own_shape)
    nbytes = _nbytes(first, x.dtype) + _nbytes(shape, own_dtype)
    return pl.pallas_call(
        functools.partial(_two_phase_kernel, n, combine, len(extras)),
        out_shape=jax.ShapeDtypeStruct(shape, own_dtype),
        in_specs=[pl.BlockSpec(memory_space=pltpu.VMEM)] * (1 + len(extras)),
        out_specs=pl.BlockSpec(memory_space=pltpu.VMEM),
        scratch_shapes=[
            pltpu.VMEM(first, x.dtype),
            pltpu.VMEM(tuple(own_shape), own_dtype),
            pltpu.VMEM(shape, own_dtype),
            pltpu.SemaphoreType.DMA(()),
            pltpu.SemaphoreType.DMA(()),
            pltpu.SemaphoreType.DMA(()),
            pltpu.SemaphoreType.DMA(()),
            pltpu.SemaphoreType.DMA(()),
            pltpu.SemaphoreType.DMA(()),
        ],
        compiler_params=pltpu.CompilerParams(collective_id=cid, has_side_effects=True),
        cost_estimate=pl.CostEstimate(flops=0, transcendentals=0, bytes_accessed=2 * nbytes),
        name="two_phase_%d" % cid,
    )(x, *extras)


def _merge_combine(buf1, fresh_ref):
    blocks = buf1[...]
    fresh = fresh_ref[...]
    block_max = blocks[:, :, HD : HD + 1]
    fresh_max = fresh[:, HD : HD + 1]
    overall = jnp.maximum(jnp.max(block_max, axis=0), fresh_max)
    block_scale = jnp.exp(block_max - overall[None])
    fresh_scale = jnp.exp(fresh_max - overall)
    weighted = jnp.sum(block_scale * blocks, axis=0) + fresh_scale * fresh
    numer = weighted[:, :HD]
    denom = weighted[:, HD + 1 : HD + 2]
    return (numer / denom).astype(jnp.bfloat16)


def _down_combine(buf1, middle_ref):
    return (middle_ref[...] + branch_factor * jnp.sum(buf1[...], axis=0)).astype(jnp.bfloat16)


STEPS = 4
norm_epsilon = 1e-05
embed_factor = 12.0
score_factor = 0.015625
branch_factor = 0.22
rope_base = 10000000.0
masked_floor = -1e30


def rms_scale(resid, gain):
    mean_square = jnp.mean(resid * resid, axis=-1, keepdims=True)
    return resid * lax.rsqrt(mean_square + norm_epsilon) * gain.astype(jnp.float32)


def rotate(vectors, where):
    half = vectors.shape[-1] // 2
    freqs = rope_base ** (-2.0 * jnp.arange(half, dtype=jnp.float32) / vectors.shape[-1])
    angle = where[..., None] * freqs
    cosine = jnp.cos(angle)
    sine = jnp.sin(angle)
    first_half = vectors[..., :half]
    second_half = vectors[..., half:]
    return jnp.concatenate(
        [first_half * cosine - second_half * sine, second_half * cosine + first_half * sine],
        axis=-1,
    )


def partial_softmax(queries, keys, values, valid):
    scores = (
        jnp.einsum("rskgd,rpkd->rskgp", queries, keys, preferred_element_type=jnp.float32)
        * score_factor
    )
    maxima = jnp.max(jnp.where(valid, scores, masked_floor), axis=-1)
    expo = jnp.exp(jnp.where(valid, scores - maxima[..., None], masked_floor))
    totals = jnp.sum(expo, axis=-1)
    outputs = jnp.einsum(
        "rskgp,rpkd->rskgd", expo.astype(jnp.bfloat16), values, preferred_element_type=jnp.float32
    )
    return (maxima, totals, outputs)


def shards(
    token_ids,
    cache_lengths,
    embed_table,
    key_cache,
    value_cache,
    norm_attn,
    norm_mlp,
    w_qkv,
    w_out,
    w_gate,
    w_up,
    w_down,
):
    n = lax.axis_size("seq")
    place = lax.axis_index("seq")
    req_all = token_ids.shape[0]
    steps = token_ids.shape[1]
    rows = req_all * steps
    ctx_own = key_cache.shape[1]
    width = embed_table.shape[0] * n
    att_width = H * HD
    kv_width = KVH * HD
    group = H // KVH

    vocab = embed_table.shape[1]
    onehot = (
        token_ids.reshape(-1)[:, None] == jnp.arange(vocab, dtype=jnp.int32)[None, :]
    ).astype(embed_table.dtype)
    picked = lax.dot_general(
        onehot, embed_table, (((1,), (1,)), ((), ())), preferred_element_type=jnp.float32
    ).astype(embed_table.dtype)
    whole = exchange(picked, n, True, 0)
    resid = jnp.transpose(whole, (1, 0, 2)).reshape(rows, width).astype(jnp.float32) * embed_factor

    slot_pos = place * ctx_own + jnp.arange(ctx_own, dtype=jnp.int32)
    cache_valid = (slot_pos[None, :] < cache_lengths[:, None]).reshape(req_all, 1, 1, 1, ctx_own)
    cache_keys = key_cache.reshape(req_all, ctx_own, KVH, HD)
    cache_values = value_cache.reshape(req_all, ctx_own, KVH, HD)

    normed = rms_scale(resid, norm_attn).astype(jnp.bfloat16)
    qkv_cols = jnp.dot(normed, w_qkv, preferred_element_type=jnp.float32).astype(jnp.bfloat16)
    qkv_got = exchange(qkv_cols, n, True, 1)
    qkv_all = jnp.transpose(qkv_got, (1, 0, 2)).reshape(req_all, steps, -1)
    where = (cache_lengths[:, None] + jnp.arange(steps, dtype=jnp.int32)[None, :]).astype(
        jnp.float32
    )
    queries = rotate(
        qkv_all[..., :att_width].reshape(req_all, steps, H, HD).astype(jnp.float32),
        where[..., None],
    ).astype(jnp.bfloat16)
    keys_new = rotate(
        qkv_all[..., att_width : att_width + kv_width]
        .reshape(req_all, steps, KVH, HD)
        .astype(jnp.float32),
        where[..., None],
    ).astype(jnp.bfloat16)
    values_new = qkv_all[..., att_width + kv_width :].reshape(req_all, steps, KVH, HD)
    grouped = queries.reshape(req_all, steps, KVH, group, HD)
    cache_max, cache_total, cache_out = partial_softmax(
        grouped, cache_keys, cache_values, cache_valid
    )
    fresh_valid = (
        jnp.arange(steps, dtype=jnp.int32)[None, :] <= jnp.arange(steps, dtype=jnp.int32)[:, None]
    ).reshape(1, steps, 1, 1, steps)
    fresh_max, fresh_total, fresh_out = partial_softmax(grouped, keys_new, values_new, fresh_valid)

    pairs = rows * H // n
    lanes = 128
    packed = jnp.concatenate(
        [
            cache_out.reshape(n, pairs, HD),
            cache_max.reshape(n, pairs, 1),
            cache_total.reshape(n, pairs, 1),
            jnp.zeros((n, pairs, lanes - HD - 2), jnp.float32),
        ],
        axis=-1,
    )
    own_fresh_max = lax.dynamic_index_in_dim(fresh_max.reshape(n, pairs), place, 0, False)
    own_fresh_total = lax.dynamic_index_in_dim(fresh_total.reshape(n, pairs), place, 0, False)
    own_fresh_out = lax.dynamic_index_in_dim(fresh_out.reshape(n, pairs, HD), place, 0, False)
    fresh_packed = jnp.concatenate(
        [
            own_fresh_out,
            own_fresh_max[:, None],
            own_fresh_total[:, None],
            jnp.zeros((pairs, lanes - HD - 2), jnp.float32),
        ],
        axis=-1,
    )
    attention = two_phase(
        packed, [fresh_packed], _merge_combine, (pairs, HD), jnp.bfloat16, n, 2
    ).reshape(rows, att_width)

    proj_cols = jnp.dot(attention, w_out, preferred_element_type=jnp.float32).astype(jnp.bfloat16)
    proj_got = exchange(proj_cols, n, True, 3)
    projected = jnp.transpose(proj_got, (1, 0, 2)).reshape(rows, width)
    middle = resid + branch_factor * projected.astype(jnp.float32)
    normed_mlp = rms_scale(middle, norm_mlp).astype(jnp.bfloat16)
    gate = jnp.dot(normed_mlp, w_gate, preferred_element_type=jnp.float32)
    upward = jnp.dot(normed_mlp, w_up, preferred_element_type=jnp.float32)
    hidden = (jax.nn.silu(gate) * upward).astype(jnp.bfloat16)
    down_part = jnp.dot(hidden, w_down, preferred_element_type=jnp.float32)
    cols = width // n
    middle_own = lax.dynamic_slice_in_dim(middle, place * cols, cols, axis=1)
    down_send = jnp.transpose(down_part.reshape(rows, n, cols), (1, 0, 2))
    out_got = two_phase(down_send, [middle_own], _down_combine, (rows, cols), jnp.bfloat16, n, 4)
    return jnp.transpose(out_got, (1, 0, 2)).reshape(req_all, steps, width)


def solution(mesh):
    return jax.shard_map(
        shards,
        mesh=mesh,
        in_specs=(
            P("rep", None),
            P("rep"),
            P("seq", None),
            P("rep", "seq", None),
            P("rep", "seq", None),
            P(),
            P(),
            P(None, "seq"),
            P(None, "seq"),
            P(None, "seq"),
            P(None, "seq"),
            P("seq", None),
        ),
        out_specs=P("rep", None, None),
        check_vma=False,
    )
```

```python
import functools

import jax
import jax.numpy as jnp
from jax import lax
from jax.experimental import pallas as pl
from jax.experimental.pallas import tpu as pltpu
from jax.sharding import PartitionSpec as P

H = 32
KVH = 8
HD = 64

MESH_ID = pl.DeviceIdType.MESH


def _greet(n, me, rep):
    barrier = pltpu.get_barrier_semaphore()

    def greet(k, carry):
        peer = lax.rem(me + k, n)
        pl.semaphore_signal(barrier, inc=1, device_id=(peer, rep), device_id_type=MESH_ID)
        return carry

    lax.fori_loop(1, n, greet, 0)
    pl.semaphore_wait(barrier, n - 1)


def _exchange_kernel(n, gather, x_ref, o_ref, buf, send_sems, recv_sems, local_sem):
    me = lax.axis_index("seq")
    rep = lax.axis_index("rep")
    _greet(n, me, rep)
    source = (lambda peer: x_ref) if gather else (lambda peer: x_ref.at[peer])
    _stage(n, me, lambda j: j, rep, source, buf, send_sems, recv_sems, local_sem)
    o_ref[...] = buf[...]


def _nbytes(shape, dtype):
    size = int(jnp.dtype(dtype).itemsize)
    for d in shape:
        size *= int(d)
    return size


def exchange(x, n, gather, cid):
    blk = x.shape if gather else x.shape[1:]
    shape = (n,) + tuple(blk)
    nbytes = _nbytes(shape, x.dtype)
    return pl.pallas_call(
        functools.partial(_exchange_kernel, n, gather),
        out_shape=jax.ShapeDtypeStruct(shape, x.dtype),
        in_specs=[pl.BlockSpec(memory_space=pltpu.VMEM)],
        out_specs=pl.BlockSpec(memory_space=pltpu.VMEM),
        scratch_shapes=[
            pltpu.VMEM(shape, x.dtype),
            pltpu.SemaphoreType.DMA(()),
            pltpu.SemaphoreType.DMA(()),
            pltpu.SemaphoreType.DMA(()),
        ],
        compiler_params=pltpu.CompilerParams(collective_id=cid, has_side_effects=True),
        cost_estimate=pl.CostEstimate(flops=0, transcendentals=0, bytes_accessed=2 * nbytes),
        name="exchange_%d" % cid,
    )(x)


def _split(n):
    low = 1
    for c in range(1, n + 1):
        if n % c == 0 and c * c <= n:
            low = c
    return low


def _stage(m, mine, dev_of, rep, source, buf, send_sem, recv_sem, local_sem):
    def copy(j, slot):
        return pltpu.make_async_remote_copy(
            src_ref=source(j),
            dst_ref=buf.at[slot],
            send_sem=send_sem,
            recv_sem=recv_sem,
            device_id=(dev_of(j), rep),
            device_id_type=MESH_ID,
        )

    def send(k, carry):
        j = lax.rem(mine + k, m)
        copy(j, mine).start()
        return carry

    lax.fori_loop(1, m, send, 0)
    local = pltpu.make_async_copy(source(mine), buf.at[mine], local_sem)
    local.start()
    rest = buf.at[pl.ds(0, m - 1)]
    every = pltpu.make_async_remote_copy(
        src_ref=rest,
        dst_ref=rest,
        send_sem=send_sem,
        recv_sem=recv_sem,
        device_id=(dev_of(lax.rem(mine + 1, m)), rep),
        device_id_type=MESH_ID,
    )
    every.wait_send()
    every.wait_recv()
    local.wait()


def _greet2(low, high, hi, lo, rep):
    barrier = pltpu.get_barrier_semaphore()

    def near(k, carry):
        peer = hi * low + lax.rem(lo + k, low)
        pl.semaphore_signal(barrier, inc=1, device_id=(peer, rep), device_id_type=MESH_ID)
        return carry

    def far(k, carry):
        peer = lax.rem(hi + k, high) * low + lo
        pl.semaphore_signal(barrier, inc=1, device_id=(peer, rep), device_id_type=MESH_ID)
        return carry

    lax.fori_loop(1, low, near, 0)
    lax.fori_loop(1, high, far, 0)
    pl.semaphore_wait(barrier, low + high - 2)


def _gather2_kernel(n, low, x_ref, o_ref, buf1, buf2, s1, r1, l1, s2, r2, l2):
    high = n // low
    me = lax.axis_index("seq")
    rep = lax.axis_index("rep")
    hi = me // low
    lo = lax.rem(me, low)
    _greet2(low, high, hi, lo, rep)
    _stage(low, lo, lambda j: hi * low + j, rep, lambda j: x_ref, buf1, s1, r1, l1)
    _stage(high, hi, lambda j: j * low + lo, rep, lambda j: buf1, buf2, s2, r2, l2)
    o_ref[...] = buf2[...]


def gather2(x, n, cid):
    low = _split(n)
    high = n // low
    blk = tuple(x.shape)
    shape = (high, low) + blk
    nbytes = _nbytes(shape, x.dtype)
    out = pl.pallas_call(
        functools.partial(_gather2_kernel, n, low),
        out_shape=jax.ShapeDtypeStruct(shape, x.dtype),
        in_specs=[pl.BlockSpec(memory_space=pltpu.VMEM)],
        out_specs=pl.BlockSpec(memory_space=pltpu.VMEM),
        scratch_shapes=[
            pltpu.VMEM((low,) + blk, x.dtype),
            pltpu.VMEM(shape, x.dtype),
            pltpu.SemaphoreType.DMA(()),
            pltpu.SemaphoreType.DMA(()),
            pltpu.SemaphoreType.DMA(()),
            pltpu.SemaphoreType.DMA(()),
            pltpu.SemaphoreType.DMA(()),
            pltpu.SemaphoreType.DMA(()),
        ],
        compiler_params=pltpu.CompilerParams(collective_id=cid, has_side_effects=True),
        cost_estimate=pl.CostEstimate(flops=0, transcendentals=0, bytes_accessed=2 * nbytes),
        name="gather2_%d" % cid,
    )(x)
    return out.reshape((n,) + blk)


def _two_phase_kernel(n, combine, n_extra, *refs):
    x_ref = refs[0]
    extras = refs[1 : 1 + n_extra]
    o_ref = refs[1 + n_extra]
    buf1, own, buf2, s1, r1, l1, s2, r2, l2 = refs[2 + n_extra :]
    me = lax.axis_index("seq")
    rep = lax.axis_index("rep")
    _greet(n, me, rep)
    _stage(n, me, lambda j: j, rep, lambda peer: x_ref.at[peer], buf1, s1, r1, l1)
    own[...] = combine(buf1, *extras)
    _stage(n, me, lambda j: j, rep, lambda peer: own, buf2, s2, r2, l2)
    o_ref[...] = buf2[...]


def two_phase(x, extras, combine, own_shape, own_dtype, n, cid):
    first = x.shape
    shape = (n,) + tuple(own_shape)
    nbytes = _nbytes(first, x.dtype) + _nbytes(shape, own_dtype)
    return pl.pallas_call(
        functools.partial(_two_phase_kernel, n, combine, len(extras)),
        out_shape=jax.ShapeDtypeStruct(shape, own_dtype),
        in_specs=[pl.BlockSpec(memory_space=pltpu.VMEM)] * (1 + len(extras)),
        out_specs=pl.BlockSpec(memory_space=pltpu.VMEM),
        scratch_shapes=[
            pltpu.VMEM(first, x.dtype),
            pltpu.VMEM(tuple(own_shape), own_dtype),
            pltpu.VMEM(shape, own_dtype),
            pltpu.SemaphoreType.DMA(()),
            pltpu.SemaphoreType.DMA(()),
            pltpu.SemaphoreType.DMA(()),
            pltpu.SemaphoreType.DMA(()),
            pltpu.SemaphoreType.DMA(()),
            pltpu.SemaphoreType.DMA(()),
        ],
        compiler_params=pltpu.CompilerParams(collective_id=cid, has_side_effects=True),
        cost_estimate=pl.CostEstimate(flops=0, transcendentals=0, bytes_accessed=2 * nbytes),
        name="two_phase_%d" % cid,
    )(x, *extras)


def _wait_all(view, rep, peer, send_sem, recv_sem, do_send, do_recv):
    every = pltpu.make_async_remote_copy(
        src_ref=view,
        dst_ref=view,
        send_sem=send_sem,
        recv_sem=recv_sem,
        device_id=(peer, rep),
        device_id_type=MESH_ID,
    )
    if do_send:
        every.wait_send()
    if do_recv:
        every.wait_recv()


def _attend_kernel(
    n, owners, x_ref, fresh_ref, w_ref, o_ref,
    buf1, own, buf2, proj, buf3, s1, r1, l1, s2, r2, l2, s3, r3, l3,
):
    me = lax.axis_index("seq")
    rep = lax.axis_index("rep")
    other = lax.rem(me + 1, n)
    _greet(n, me, rep)
    is_owner = me < owners

    def send_one(k, carry):
        peer = lax.rem(me + k, n)

        @pl.when(peer < owners)
        def _():
            pltpu.make_async_remote_copy(
                src_ref=x_ref.at[peer],
                dst_ref=buf1.at[me],
                send_sem=s1,
                recv_sem=r1,
                device_id=(peer, rep),
                device_id_type=MESH_ID,
            ).start()

        return carry

    lax.fori_loop(1, n, send_one, 0)

    @pl.when(is_owner)
    def _():
        local = pltpu.make_async_copy(x_ref.at[me], buf1.at[me], l1)
        local.start()
        _wait_all(buf1.at[pl.ds(0, owners - 1)], rep, other, s1, r1, True, False)
        _wait_all(buf1.at[pl.ds(0, n - 1)], rep, other, s1, r1, False, True)
        local.wait()
        blocks = buf1[...]
        fresh = fresh_ref[me]
        block_max = blocks[:, :, HD : HD + 1]
        fresh_max = fresh[:, HD : HD + 1]
        overall = jnp.maximum(jnp.max(block_max, axis=0), fresh_max)
        block_scale = jnp.exp(block_max - overall[None])
        fresh_scale = jnp.exp(fresh_max - overall)
        weighted = jnp.sum(block_scale * blocks, axis=0) + fresh_scale * fresh
        own[...] = (weighted[:, :HD] / weighted[:, HD + 1 : HD + 2]).astype(jnp.bfloat16)

        def spread(k, carry):
            peer = lax.rem(me + k, n)
            pltpu.make_async_remote_copy(
                src_ref=own,
                dst_ref=buf2.at[me],
                send_sem=s2,
                recv_sem=r2,
                device_id=(peer, rep),
                device_id_type=MESH_ID,
            ).start()
            return carry

        lax.fori_loop(1, n, spread, 0)
        local2 = pltpu.make_async_copy(own, buf2.at[me], l2)
        local2.start()
        _wait_all(buf2.at[pl.ds(0, n - 1)], rep, other, s2, r2, True, False)
        _wait_all(buf2.at[pl.ds(0, owners - 1)], rep, other, s2, r2, False, True)
        local2.wait()

    @pl.when(jnp.logical_not(is_owner))
    def _():
        _wait_all(buf1.at[pl.ds(0, owners)], rep, other, s1, r1, True, False)
        _wait_all(buf2.at[pl.ds(0, owners)], rep, other, s2, r2, False, True)

    rows, cols = proj.shape

    def head(h, acc):
        start = pl.multiple_of(h * HD, HD)
        return acc + jnp.dot(
            buf2[h], w_ref[pl.ds(start, HD), :], preferred_element_type=jnp.float32
        )

    acc = lax.fori_loop(0, owners, head, jnp.zeros((rows, cols), jnp.float32))
    proj[...] = acc.astype(jnp.bfloat16)
    _stage(n, me, lambda j: j, rep, lambda j: proj, buf3, s3, r3, l3)
    o_ref[...] = buf3[...]


def attend(packed, fresh, w_out, n, cid):
    owners, rows, lanes = packed.shape
    cols = w_out.shape[1]
    sems = [pltpu.SemaphoreType.DMA(())] * 9
    return pl.pallas_call(
        functools.partial(_attend_kernel, n, owners),
        out_shape=jax.ShapeDtypeStruct((n, rows, cols), jnp.bfloat16),
        in_specs=[pl.BlockSpec(memory_space=pltpu.VMEM)] * 3,
        out_specs=pl.BlockSpec(memory_space=pltpu.VMEM),
        scratch_shapes=[
            pltpu.VMEM((n, rows, lanes), jnp.float32),
            pltpu.VMEM((rows, HD), jnp.bfloat16),
            pltpu.VMEM((n, rows, HD), jnp.bfloat16),
            pltpu.VMEM((rows, cols), jnp.bfloat16),
            pltpu.VMEM((n, rows, cols), jnp.bfloat16),
        ]
        + sems,
        compiler_params=pltpu.CompilerParams(collective_id=cid, has_side_effects=True),
        cost_estimate=pl.CostEstimate(
            flops=2 * rows * owners * HD * cols,
            transcendentals=n * rows,
            bytes_accessed=2 * (_nbytes((n, rows, lanes), jnp.float32) + _nbytes(w_out.shape, w_out.dtype)),
        ),
        name="attend_%d" % cid,
    )(packed, fresh, w_out)


def _merge_combine(buf1, fresh_ref):
    blocks = buf1[...]
    fresh = fresh_ref[...]
    block_max = blocks[:, :, HD : HD + 1]
    fresh_max = fresh[:, HD : HD + 1]
    overall = jnp.maximum(jnp.max(block_max, axis=0), fresh_max)
    block_scale = jnp.exp(block_max - overall[None])
    fresh_scale = jnp.exp(fresh_max - overall)
    weighted = jnp.sum(block_scale * blocks, axis=0) + fresh_scale * fresh
    numer = weighted[:, :HD]
    denom = weighted[:, HD + 1 : HD + 2]
    return (numer / denom).astype(jnp.bfloat16)


def _down_combine(buf1, middle_ref):
    return (middle_ref[...] + branch_factor * jnp.sum(buf1[...], axis=0)).astype(jnp.bfloat16)


STEPS = 4
norm_epsilon = 1e-05
embed_factor = 12.0
score_factor = 0.015625
branch_factor = 0.22
rope_base = 10000000.0
masked_floor = -1e30


def rms_scale(resid, gain):
    mean_square = jnp.mean(resid * resid, axis=-1, keepdims=True)
    return resid * lax.rsqrt(mean_square + norm_epsilon) * gain.astype(jnp.float32)


def rotate(vectors, where):
    half = vectors.shape[-1] // 2
    freqs = rope_base ** (-2.0 * jnp.arange(half, dtype=jnp.float32) / vectors.shape[-1])
    angle = where[..., None] * freqs
    cosine = jnp.cos(angle)
    sine = jnp.sin(angle)
    first_half = vectors[..., :half]
    second_half = vectors[..., half:]
    return jnp.concatenate(
        [first_half * cosine - second_half * sine, second_half * cosine + first_half * sine],
        axis=-1,
    )


def partial_softmax(queries, keys, values, valid):
    scores = (
        jnp.einsum("rskgd,rpkd->rskgp", queries, keys, preferred_element_type=jnp.float32)
        * score_factor
    )
    maxima = jnp.max(jnp.where(valid, scores, masked_floor), axis=-1)
    expo = jnp.exp(jnp.where(valid, scores - maxima[..., None], masked_floor))
    totals = jnp.sum(expo, axis=-1)
    outputs = jnp.einsum(
        "rskgp,rpkd->rskgd", expo.astype(jnp.bfloat16), values, preferred_element_type=jnp.float32
    )
    return (maxima, totals, outputs)


def shards(
    token_ids,
    cache_lengths,
    embed_table,
    key_cache,
    value_cache,
    norm_attn,
    norm_mlp,
    w_qkv,
    w_out,
    w_gate,
    w_up,
    w_down,
):
    n = lax.axis_size("seq")
    place = lax.axis_index("seq")
    req_all = token_ids.shape[0]
    steps = token_ids.shape[1]
    rows = req_all * steps
    ctx_own = key_cache.shape[1]
    width = embed_table.shape[0] * n
    att_width = H * HD
    kv_width = KVH * HD
    group = H // KVH

    vocab = embed_table.shape[1]
    onehot = (
        token_ids.reshape(-1)[:, None] == jnp.arange(vocab, dtype=jnp.int32)[None, :]
    ).astype(embed_table.dtype)
    picked = lax.dot_general(
        onehot, embed_table, (((1,), (1,)), ((), ())), preferred_element_type=jnp.float32
    ).astype(embed_table.dtype)
    whole = exchange(picked, n, True, 0)
    resid = jnp.transpose(whole, (1, 0, 2)).reshape(rows, width).astype(jnp.float32) * embed_factor

    slot_pos = place * ctx_own + jnp.arange(ctx_own, dtype=jnp.int32)
    cache_valid = (slot_pos[None, :] < cache_lengths[:, None]).reshape(req_all, 1, 1, 1, ctx_own)
    cache_keys = key_cache.reshape(req_all, ctx_own, KVH, HD)
    cache_values = value_cache.reshape(req_all, ctx_own, KVH, HD)

    normed = rms_scale(resid, norm_attn).astype(jnp.bfloat16)
    qkv_cols = jnp.dot(normed, w_qkv, preferred_element_type=jnp.float32).astype(jnp.bfloat16)
    qkv_got = exchange(qkv_cols, n, True, 1)
    qkv_all = jnp.transpose(qkv_got, (1, 0, 2)).reshape(req_all, steps, -1)
    where = (cache_lengths[:, None] + jnp.arange(steps, dtype=jnp.int32)[None, :]).astype(
        jnp.float32
    )
    queries = rotate(
        qkv_all[..., :att_width].reshape(req_all, steps, H, HD).astype(jnp.float32),
        where[..., None],
    ).astype(jnp.bfloat16)
    keys_new = rotate(
        qkv_all[..., att_width : att_width + kv_width]
        .reshape(req_all, steps, KVH, HD)
        .astype(jnp.float32),
        where[..., None],
    ).astype(jnp.bfloat16)
    values_new = qkv_all[..., att_width + kv_width :].reshape(req_all, steps, KVH, HD)
    grouped = queries.reshape(req_all, steps, KVH, group, HD)
    cache_max, cache_total, cache_out = partial_softmax(
        grouped, cache_keys, cache_values, cache_valid
    )
    fresh_valid = (
        jnp.arange(steps, dtype=jnp.int32)[None, :] <= jnp.arange(steps, dtype=jnp.int32)[:, None]
    ).reshape(1, steps, 1, 1, steps)
    fresh_max, fresh_total, fresh_out = partial_softmax(grouped, keys_new, values_new, fresh_valid)

    lanes = 128

    def by_head(out, top, total):
        return jnp.concatenate(
            [
                jnp.transpose(out.reshape(rows, H, HD), (1, 0, 2)),
                jnp.transpose(top.reshape(rows, H), (1, 0))[..., None],
                jnp.transpose(total.reshape(rows, H), (1, 0))[..., None],
                jnp.zeros((H, rows, lanes - HD - 2), jnp.float32),
            ],
            axis=-1,
        )

    proj_got = attend(
        by_head(cache_out, cache_max, cache_total),
        by_head(fresh_out, fresh_max, fresh_total),
        w_out,
        n,
        2,
    )
    projected = jnp.transpose(proj_got, (1, 0, 2)).reshape(rows, width)
    middle = resid + branch_factor * projected.astype(jnp.float32)
    normed_mlp = rms_scale(middle, norm_mlp).astype(jnp.bfloat16)
    gate = jnp.dot(normed_mlp, w_gate, preferred_element_type=jnp.float32)
    upward = jnp.dot(normed_mlp, w_up, preferred_element_type=jnp.float32)
    hidden = (jax.nn.silu(gate) * upward).astype(jnp.bfloat16)
    down_part = jnp.dot(hidden, w_down, preferred_element_type=jnp.float32)
    cols = width // n
    middle_own = lax.dynamic_slice_in_dim(middle, place * cols, cols, axis=1)
    down_send = jnp.transpose(down_part.reshape(rows, n, cols), (1, 0, 2))
    out_got = two_phase(down_send, [middle_own], _down_combine, (rows, cols), jnp.bfloat16, n, 3)
    return jnp.transpose(out_got, (1, 0, 2)).reshape(req_all, steps, width)


def solution(mesh):
    return jax.shard_map(
        shards,
        mesh=mesh,
        in_specs=(
            P("rep", None),
            P("rep"),
            P("seq", None),
            P("rep", "seq", None),
            P("rep", "seq", None),
            P(),
            P(),
            P(None, "seq"),
            P(None, "seq"),
            P(None, "seq"),
            P(None, "seq"),
            P("seq", None),
        ),
        out_specs=P("rep", None, None),
        check_vma=False,
    )
```

```python
import functools

import jax
import jax.numpy as jnp
from jax import lax
from jax.experimental import pallas as pl
from jax.experimental.pallas import tpu as pltpu
from jax.sharding import PartitionSpec as P

H = 32
KVH = 8
HD = 64

MESH_ID = pl.DeviceIdType.MESH


def _greet(n, me, rep):
    barrier = pltpu.get_barrier_semaphore()

    def greet(k, carry):
        peer = lax.rem(me + k, n)
        pl.semaphore_signal(barrier, inc=1, device_id=(peer, rep), device_id_type=MESH_ID)
        return carry

    lax.fori_loop(1, n, greet, 0)
    pl.semaphore_wait(barrier, n - 1)


def _exchange_kernel(n, gather, x_ref, o_ref, buf, send_sems, recv_sems, local_sem):
    me = lax.axis_index("seq")
    rep = lax.axis_index("rep")
    _greet(n, me, rep)
    source = (lambda peer: x_ref) if gather else (lambda peer: x_ref.at[peer])
    _stage(n, me, lambda j: j, rep, source, buf, send_sems, recv_sems, local_sem)
    o_ref[...] = buf[...]


def _nbytes(shape, dtype):
    size = int(jnp.dtype(dtype).itemsize)
    for d in shape:
        size *= int(d)
    return size


def exchange(x, n, gather, cid):
    blk = x.shape if gather else x.shape[1:]
    shape = (n,) + tuple(blk)
    nbytes = _nbytes(shape, x.dtype)
    return pl.pallas_call(
        functools.partial(_exchange_kernel, n, gather),
        out_shape=jax.ShapeDtypeStruct(shape, x.dtype),
        in_specs=[pl.BlockSpec(memory_space=pltpu.VMEM)],
        out_specs=pl.BlockSpec(memory_space=pltpu.VMEM),
        scratch_shapes=[
            pltpu.VMEM(shape, x.dtype),
            pltpu.SemaphoreType.DMA(()),
            pltpu.SemaphoreType.DMA(()),
            pltpu.SemaphoreType.DMA(()),
        ],
        compiler_params=pltpu.CompilerParams(collective_id=cid, has_side_effects=True),
        cost_estimate=pl.CostEstimate(flops=0, transcendentals=0, bytes_accessed=2 * nbytes),
        name="exchange_%d" % cid,
    )(x)


def _split(n):
    low = 1
    for c in range(1, n + 1):
        if n % c == 0 and c * c <= n:
            low = c
    return low


def _stage(m, mine, dev_of, rep, source, buf, send_sem, recv_sem, local_sem):
    def copy(j, slot):
        return pltpu.make_async_remote_copy(
            src_ref=source(j),
            dst_ref=buf.at[slot],
            send_sem=send_sem,
            recv_sem=recv_sem,
            device_id=(dev_of(j), rep),
            device_id_type=MESH_ID,
        )

    def send(k, carry):
        j = lax.rem(mine + k, m)
        copy(j, mine).start()
        return carry

    lax.fori_loop(1, m, send, 0)
    local = pltpu.make_async_copy(source(mine), buf.at[mine], local_sem)
    local.start()
    rest = buf.at[pl.ds(0, m - 1)]
    every = pltpu.make_async_remote_copy(
        src_ref=rest,
        dst_ref=rest,
        send_sem=send_sem,
        recv_sem=recv_sem,
        device_id=(dev_of(lax.rem(mine + 1, m)), rep),
        device_id_type=MESH_ID,
    )
    every.wait_send()
    every.wait_recv()
    local.wait()


def _greet2(low, high, hi, lo, rep):
    barrier = pltpu.get_barrier_semaphore()

    def near(k, carry):
        peer = hi * low + lax.rem(lo + k, low)
        pl.semaphore_signal(barrier, inc=1, device_id=(peer, rep), device_id_type=MESH_ID)
        return carry

    def far(k, carry):
        peer = lax.rem(hi + k, high) * low + lo
        pl.semaphore_signal(barrier, inc=1, device_id=(peer, rep), device_id_type=MESH_ID)
        return carry

    lax.fori_loop(1, low, near, 0)
    lax.fori_loop(1, high, far, 0)
    pl.semaphore_wait(barrier, low + high - 2)


def _gather2_kernel(n, low, x_ref, o_ref, buf1, buf2, s1, r1, l1, s2, r2, l2):
    high = n // low
    me = lax.axis_index("seq")
    rep = lax.axis_index("rep")
    hi = me // low
    lo = lax.rem(me, low)
    _greet2(low, high, hi, lo, rep)
    _stage(low, lo, lambda j: hi * low + j, rep, lambda j: x_ref, buf1, s1, r1, l1)
    _stage(high, hi, lambda j: j * low + lo, rep, lambda j: buf1, buf2, s2, r2, l2)
    o_ref[...] = buf2[...]


def gather2(x, n, cid):
    low = _split(n)
    high = n // low
    blk = tuple(x.shape)
    shape = (high, low) + blk
    nbytes = _nbytes(shape, x.dtype)
    out = pl.pallas_call(
        functools.partial(_gather2_kernel, n, low),
        out_shape=jax.ShapeDtypeStruct(shape, x.dtype),
        in_specs=[pl.BlockSpec(memory_space=pltpu.VMEM)],
        out_specs=pl.BlockSpec(memory_space=pltpu.VMEM),
        scratch_shapes=[
            pltpu.VMEM((low,) + blk, x.dtype),
            pltpu.VMEM(shape, x.dtype),
            pltpu.SemaphoreType.DMA(()),
            pltpu.SemaphoreType.DMA(()),
            pltpu.SemaphoreType.DMA(()),
            pltpu.SemaphoreType.DMA(()),
            pltpu.SemaphoreType.DMA(()),
            pltpu.SemaphoreType.DMA(()),
        ],
        compiler_params=pltpu.CompilerParams(collective_id=cid, has_side_effects=True),
        cost_estimate=pl.CostEstimate(flops=0, transcendentals=0, bytes_accessed=2 * nbytes),
        name="gather2_%d" % cid,
    )(x)
    return out.reshape((n,) + blk)


def _two_phase_kernel(n, combine, n_extra, *refs):
    x_ref = refs[0]
    extras = refs[1 : 1 + n_extra]
    o_ref = refs[1 + n_extra]
    buf1, own, buf2, s1, r1, l1, s2, r2, l2 = refs[2 + n_extra :]
    me = lax.axis_index("seq")
    rep = lax.axis_index("rep")
    _greet(n, me, rep)
    _stage(n, me, lambda j: j, rep, lambda peer: x_ref.at[peer], buf1, s1, r1, l1)
    own[...] = combine(buf1, *extras)
    _stage(n, me, lambda j: j, rep, lambda peer: own, buf2, s2, r2, l2)
    o_ref[...] = buf2[...]


def two_phase(x, extras, combine, own_shape, own_dtype, n, cid):
    first = x.shape
    shape = (n,) + tuple(own_shape)
    nbytes = _nbytes(first, x.dtype) + _nbytes(shape, own_dtype)
    return pl.pallas_call(
        functools.partial(_two_phase_kernel, n, combine, len(extras)),
        out_shape=jax.ShapeDtypeStruct(shape, own_dtype),
        in_specs=[pl.BlockSpec(memory_space=pltpu.VMEM)] * (1 + len(extras)),
        out_specs=pl.BlockSpec(memory_space=pltpu.VMEM),
        scratch_shapes=[
            pltpu.VMEM(first, x.dtype),
            pltpu.VMEM(tuple(own_shape), own_dtype),
            pltpu.VMEM(shape, own_dtype),
            pltpu.SemaphoreType.DMA(()),
            pltpu.SemaphoreType.DMA(()),
            pltpu.SemaphoreType.DMA(()),
            pltpu.SemaphoreType.DMA(()),
            pltpu.SemaphoreType.DMA(()),
            pltpu.SemaphoreType.DMA(()),
        ],
        compiler_params=pltpu.CompilerParams(collective_id=cid, has_side_effects=True),
        cost_estimate=pl.CostEstimate(flops=0, transcendentals=0, bytes_accessed=2 * nbytes),
        name="two_phase_%d" % cid,
    )(x, *extras)


def _merge_combine(buf1, fresh_ref):
    blocks = buf1[...]
    fresh = fresh_ref[...]
    block_max = blocks[:, :, HD : HD + 1]
    fresh_max = fresh[:, HD : HD + 1]
    overall = jnp.maximum(jnp.max(block_max, axis=0), fresh_max)
    block_scale = jnp.exp(block_max - overall[None])
    fresh_scale = jnp.exp(fresh_max - overall)
    weighted = jnp.sum(block_scale * blocks, axis=0) + fresh_scale * fresh
    numer = weighted[:, :HD]
    denom = weighted[:, HD + 1 : HD + 2]
    return (numer / denom).astype(jnp.bfloat16)


def _down_combine(buf1, middle_ref):
    return (middle_ref[...] + branch_factor * jnp.sum(buf1[...], axis=0)).astype(jnp.bfloat16)


STEPS = 4
norm_epsilon = 1e-05
embed_factor = 12.0
score_factor = 0.015625
branch_factor = 0.22
rope_base = 10000000.0
masked_floor = -1e30


def rms_scale(resid, gain):
    mean_square = jnp.mean(resid * resid, axis=-1, keepdims=True)
    return resid * lax.rsqrt(mean_square + norm_epsilon) * gain.astype(jnp.float32)


def rotate(vectors, where):
    half = vectors.shape[-1] // 2
    freqs = rope_base ** (-2.0 * jnp.arange(half, dtype=jnp.float32) / vectors.shape[-1])
    angle = where[..., None] * freqs
    cosine = jnp.cos(angle)
    sine = jnp.sin(angle)
    first_half = vectors[..., :half]
    second_half = vectors[..., half:]
    return jnp.concatenate(
        [first_half * cosine - second_half * sine, second_half * cosine + first_half * sine],
        axis=-1,
    )


def partial_softmax(queries, keys, values, valid):
    scores = (
        jnp.einsum("rskgd,rpkd->rskgp", queries, keys, preferred_element_type=jnp.float32)
        * score_factor
    )
    maxima = jnp.max(jnp.where(valid, scores, masked_floor), axis=-1)
    expo = jnp.exp(jnp.where(valid, scores - maxima[..., None], masked_floor))
    totals = jnp.sum(expo, axis=-1)
    outputs = jnp.einsum(
        "rskgp,rpkd->rskgd", expo.astype(jnp.bfloat16), values, preferred_element_type=jnp.float32
    )
    return (maxima, totals, outputs)


def shards(
    token_ids,
    cache_lengths,
    embed_table,
    key_cache,
    value_cache,
    norm_attn,
    norm_mlp,
    w_qkv,
    w_out,
    w_gate,
    w_up,
    w_down,
):
    n = lax.axis_size("seq")
    place = lax.axis_index("seq")
    req_all = token_ids.shape[0]
    steps = token_ids.shape[1]
    rows = req_all * steps
    ctx_own = key_cache.shape[1]
    width = embed_table.shape[0] * n
    att_width = H * HD
    kv_width = KVH * HD
    group = H // KVH

    vocab = embed_table.shape[1]
    onehot = (
        token_ids.reshape(-1)[:, None] == jnp.arange(vocab, dtype=jnp.int32)[None, :]
    ).astype(embed_table.dtype)
    picked = lax.dot_general(
        onehot, embed_table, (((1,), (1,)), ((), ())), preferred_element_type=jnp.float32
    ).astype(embed_table.dtype)
    whole = exchange(picked, n, True, 0)
    resid = jnp.transpose(whole, (1, 0, 2)).reshape(rows, width).astype(jnp.float32) * embed_factor

    slot_pos = place * ctx_own + jnp.arange(ctx_own, dtype=jnp.int32)
    cache_valid = (slot_pos[None, :] < cache_lengths[:, None]).reshape(req_all, 1, 1, 1, ctx_own)
    cache_keys = key_cache.reshape(req_all, ctx_own, KVH, HD)
    cache_values = value_cache.reshape(req_all, ctx_own, KVH, HD)

    normed = rms_scale(resid, norm_attn).astype(jnp.bfloat16)
    qkv_cols = jnp.dot(normed, w_qkv, preferred_element_type=jnp.float32).astype(jnp.bfloat16)
    qkv_got = exchange(qkv_cols, n, True, 1)
    qkv_all = jnp.transpose(qkv_got, (1, 0, 2)).reshape(req_all, steps, -1)
    where = (cache_lengths[:, None] + jnp.arange(steps, dtype=jnp.int32)[None, :]).astype(
        jnp.float32
    )
    queries = rotate(
        qkv_all[..., :att_width].reshape(req_all, steps, H, HD).astype(jnp.float32),
        where[..., None],
    ).astype(jnp.bfloat16)
    keys_new = rotate(
        qkv_all[..., att_width : att_width + kv_width]
        .reshape(req_all, steps, KVH, HD)
        .astype(jnp.float32),
        where[..., None],
    ).astype(jnp.bfloat16)
    values_new = qkv_all[..., att_width + kv_width :].reshape(req_all, steps, KVH, HD)
    grouped = queries.reshape(req_all, steps, KVH, group, HD)
    pick = (jnp.arange(H, dtype=jnp.int32)[:, None] // group) == jnp.arange(KVH, dtype=jnp.int32)[None, :]
    widened = jnp.where(
        pick[None, None, :, :, None], queries[:, :, :, None, :], jnp.zeros((), queries.dtype)
    ).reshape(req_all, steps * H, kv_width)
    scores = (
        jnp.einsum("rqc,rpc->rqp", widened, key_cache, preferred_element_type=jnp.float32)
        * score_factor
    )
    flat_valid = cache_valid.reshape(req_all, 1, ctx_own)
    flat_max = jnp.max(jnp.where(flat_valid, scores, masked_floor), axis=-1)
    expo = jnp.exp(jnp.where(flat_valid, scores - flat_max[..., None], masked_floor))
    flat_total = jnp.sum(expo, axis=-1)
    spread_out = jnp.einsum(
        "rqp,rpc->rqc", expo.astype(jnp.bfloat16), value_cache, preferred_element_type=jnp.float32
    ).reshape(req_all, steps, H, KVH, HD)
    picked_out = jnp.sum(jnp.where(pick[None, None, :, :, None], spread_out, 0.0), axis=3)
    cache_max = flat_max.reshape(req_all, steps, KVH, group)
    cache_total = flat_total.reshape(req_all, steps, KVH, group)
    cache_out = picked_out.reshape(req_all, steps, KVH, group, HD)
    fresh_valid = (
        jnp.arange(steps, dtype=jnp.int32)[None, :] <= jnp.arange(steps, dtype=jnp.int32)[:, None]
    ).reshape(1, steps, 1, 1, steps)
    fresh_max, fresh_total, fresh_out = partial_softmax(grouped, keys_new, values_new, fresh_valid)

    pairs = rows * H // n
    lanes = 128
    packed = jnp.concatenate(
        [
            cache_out.reshape(n, pairs, HD),
            cache_max.reshape(n, pairs, 1),
            cache_total.reshape(n, pairs, 1),
            jnp.zeros((n, pairs, lanes - HD - 2), jnp.float32),
        ],
        axis=-1,
    )
    own_fresh_max = lax.dynamic_index_in_dim(fresh_max.reshape(n, pairs), place, 0, False)
    own_fresh_total = lax.dynamic_index_in_dim(fresh_total.reshape(n, pairs), place, 0, False)
    own_fresh_out = lax.dynamic_index_in_dim(fresh_out.reshape(n, pairs, HD), place, 0, False)
    fresh_packed = jnp.concatenate(
        [
            own_fresh_out,
            own_fresh_max[:, None],
            own_fresh_total[:, None],
            jnp.zeros((pairs, lanes - HD - 2), jnp.float32),
        ],
        axis=-1,
    )
    attention = two_phase(
        packed, [fresh_packed], _merge_combine, (pairs, HD), jnp.bfloat16, n, 2
    ).reshape(rows, att_width)

    proj_cols = jnp.dot(attention, w_out, preferred_element_type=jnp.float32).astype(jnp.bfloat16)
    proj_got = exchange(proj_cols, n, True, 3)
    projected = jnp.transpose(proj_got, (1, 0, 2)).reshape(rows, width)
    middle = resid + branch_factor * projected.astype(jnp.float32)
    normed_mlp = rms_scale(middle, norm_mlp).astype(jnp.bfloat16)
    gate = jnp.dot(normed_mlp, w_gate, preferred_element_type=jnp.float32)
    upward = jnp.dot(normed_mlp, w_up, preferred_element_type=jnp.float32)
    hidden = (jax.nn.silu(gate) * upward).astype(jnp.bfloat16)
    down_part = jnp.dot(hidden, w_down, preferred_element_type=jnp.float32)
    cols = width // n
    middle_own = lax.dynamic_slice_in_dim(middle, place * cols, cols, axis=1)
    down_send = jnp.transpose(down_part.reshape(rows, n, cols), (1, 0, 2))
    out_got = two_phase(down_send, [middle_own], _down_combine, (rows, cols), jnp.bfloat16, n, 4)
    return jnp.transpose(out_got, (1, 0, 2)).reshape(req_all, steps, width)


def solution(mesh):
    return jax.shard_map(
        shards,
        mesh=mesh,
        in_specs=(
            P("rep", None),
            P("rep"),
            P("seq", None),
            P("rep", "seq", None),
            P("rep", "seq", None),
            P(),
            P(),
            P(None, "seq"),
            P(None, "seq"),
            P(None, "seq"),
            P(None, "seq"),
            P("seq", None),
        ),
        out_specs=P("rep", None, None),
        check_vma=False,
    )
```

```python
import functools

import jax
import jax.numpy as jnp
from jax import lax
from jax.experimental import pallas as pl
from jax.experimental.pallas import tpu as pltpu
from jax.sharding import PartitionSpec as P

H = 32
KVH = 8
HD = 64

MESH_ID = pl.DeviceIdType.MESH


def _greet(n, me, rep):
    barrier = pltpu.get_barrier_semaphore()

    def greet(k, carry):
        peer = lax.rem(me + k, n)
        pl.semaphore_signal(barrier, inc=1, device_id=(peer, rep), device_id_type=MESH_ID)
        return carry

    lax.fori_loop(1, n, greet, 0)
    pl.semaphore_wait(barrier, n - 1)


def _exchange_kernel(n, gather, x_ref, o_ref, buf, send_sems, recv_sems, local_sem):
    me = lax.axis_index("seq")
    rep = lax.axis_index("rep")
    source = (lambda peer: x_ref) if gather else (lambda peer: x_ref.at[peer])
    _stage(n, me, lambda j: j, rep, source, buf, send_sems, recv_sems, local_sem)
    o_ref[...] = buf[...]


def _nbytes(shape, dtype):
    size = int(jnp.dtype(dtype).itemsize)
    for d in shape:
        size *= int(d)
    return size


def exchange(x, n, gather, cid):
    blk = x.shape if gather else x.shape[1:]
    shape = (n,) + tuple(blk)
    nbytes = _nbytes(shape, x.dtype)
    return pl.pallas_call(
        functools.partial(_exchange_kernel, n, gather),
        out_shape=jax.ShapeDtypeStruct(shape, x.dtype),
        in_specs=[pl.BlockSpec(memory_space=pltpu.VMEM)],
        out_specs=pl.BlockSpec(memory_space=pltpu.VMEM),
        scratch_shapes=[
            pltpu.VMEM(shape, x.dtype),
            pltpu.SemaphoreType.DMA(()),
            pltpu.SemaphoreType.DMA(()),
            pltpu.SemaphoreType.DMA(()),
        ],
        compiler_params=pltpu.CompilerParams(has_side_effects=True),
        cost_estimate=pl.CostEstimate(flops=0, transcendentals=0, bytes_accessed=2 * nbytes),
        name="exchange_%d" % cid,
    )(x)


def _split(n):
    low = 1
    for c in range(1, n + 1):
        if n % c == 0 and c * c <= n:
            low = c
    return low


def _stage(m, mine, dev_of, rep, source, buf, send_sem, recv_sem, local_sem):
    def copy(j, slot):
        return pltpu.make_async_remote_copy(
            src_ref=source(j),
            dst_ref=buf.at[slot],
            send_sem=send_sem,
            recv_sem=recv_sem,
            device_id=(dev_of(j), rep),
            device_id_type=MESH_ID,
        )

    def send(k, carry):
        j = lax.rem(mine + k, m)
        copy(j, mine).start()
        return carry

    lax.fori_loop(1, m, send, 0)
    local = pltpu.make_async_copy(source(mine), buf.at[mine], local_sem)
    local.start()
    rest = buf.at[pl.ds(0, m - 1)]
    every = pltpu.make_async_remote_copy(
        src_ref=rest,
        dst_ref=rest,
        send_sem=send_sem,
        recv_sem=recv_sem,
        device_id=(dev_of(lax.rem(mine + 1, m)), rep),
        device_id_type=MESH_ID,
    )
    every.wait_send()
    every.wait_recv()
    local.wait()


def _greet2(low, high, hi, lo, rep):
    barrier = pltpu.get_barrier_semaphore()

    def near(k, carry):
        peer = hi * low + lax.rem(lo + k, low)
        pl.semaphore_signal(barrier, inc=1, device_id=(peer, rep), device_id_type=MESH_ID)
        return carry

    def far(k, carry):
        peer = lax.rem(hi + k, high) * low + lo
        pl.semaphore_signal(barrier, inc=1, device_id=(peer, rep), device_id_type=MESH_ID)
        return carry

    lax.fori_loop(1, low, near, 0)
    lax.fori_loop(1, high, far, 0)
    pl.semaphore_wait(barrier, low + high - 2)


def _gather2_kernel(n, low, x_ref, o_ref, buf1, buf2, s1, r1, l1, s2, r2, l2):
    high = n // low
    me = lax.axis_index("seq")
    rep = lax.axis_index("rep")
    hi = me // low
    lo = lax.rem(me, low)
    _greet2(low, high, hi, lo, rep)
    _stage(low, lo, lambda j: hi * low + j, rep, lambda j: x_ref, buf1, s1, r1, l1)
    _stage(high, hi, lambda j: j * low + lo, rep, lambda j: buf1, buf2, s2, r2, l2)
    o_ref[...] = buf2[...]


def gather2(x, n, cid):
    low = _split(n)
    high = n // low
    blk = tuple(x.shape)
    shape = (high, low) + blk
    nbytes = _nbytes(shape, x.dtype)
    out = pl.pallas_call(
        functools.partial(_gather2_kernel, n, low),
        out_shape=jax.ShapeDtypeStruct(shape, x.dtype),
        in_specs=[pl.BlockSpec(memory_space=pltpu.VMEM)],
        out_specs=pl.BlockSpec(memory_space=pltpu.VMEM),
        scratch_shapes=[
            pltpu.VMEM((low,) + blk, x.dtype),
            pltpu.VMEM(shape, x.dtype),
            pltpu.SemaphoreType.DMA(()),
            pltpu.SemaphoreType.DMA(()),
            pltpu.SemaphoreType.DMA(()),
            pltpu.SemaphoreType.DMA(()),
            pltpu.SemaphoreType.DMA(()),
            pltpu.SemaphoreType.DMA(()),
        ],
        compiler_params=pltpu.CompilerParams(has_side_effects=True),
        cost_estimate=pl.CostEstimate(flops=0, transcendentals=0, bytes_accessed=2 * nbytes),
        name="gather2_%d" % cid,
    )(x)
    return out.reshape((n,) + blk)


def _two_phase_kernel(n, combine, n_extra, *refs):
    x_ref = refs[0]
    extras = refs[1 : 1 + n_extra]
    o_ref = refs[1 + n_extra]
    buf1, own, buf2, s1, r1, l1, s2, r2, l2 = refs[2 + n_extra :]
    me = lax.axis_index("seq")
    rep = lax.axis_index("rep")
    _stage(n, me, lambda j: j, rep, lambda peer: x_ref.at[peer], buf1, s1, r1, l1)
    own[...] = combine(buf1, *extras)
    _stage(n, me, lambda j: j, rep, lambda peer: own, buf2, s2, r2, l2)
    o_ref[...] = buf2[...]


def two_phase(x, extras, combine, own_shape, own_dtype, n, cid):
    first = x.shape
    shape = (n,) + tuple(own_shape)
    nbytes = _nbytes(first, x.dtype) + _nbytes(shape, own_dtype)
    return pl.pallas_call(
        functools.partial(_two_phase_kernel, n, combine, len(extras)),
        out_shape=jax.ShapeDtypeStruct(shape, own_dtype),
        in_specs=[pl.BlockSpec(memory_space=pltpu.VMEM)] * (1 + len(extras)),
        out_specs=pl.BlockSpec(memory_space=pltpu.VMEM),
        scratch_shapes=[
            pltpu.VMEM(first, x.dtype),
            pltpu.VMEM(tuple(own_shape), own_dtype),
            pltpu.VMEM(shape, own_dtype),
            pltpu.SemaphoreType.DMA(()),
            pltpu.SemaphoreType.DMA(()),
            pltpu.SemaphoreType.DMA(()),
            pltpu.SemaphoreType.DMA(()),
            pltpu.SemaphoreType.DMA(()),
            pltpu.SemaphoreType.DMA(()),
        ],
        compiler_params=pltpu.CompilerParams(has_side_effects=True),
        cost_estimate=pl.CostEstimate(flops=0, transcendentals=0, bytes_accessed=2 * nbytes),
        name="two_phase_%d" % cid,
    )(x, *extras)


def _merge_combine(buf1, fresh_ref):
    blocks = buf1[...]
    fresh = fresh_ref[...]
    block_max = blocks[:, :, HD : HD + 1]
    fresh_max = fresh[:, HD : HD + 1]
    overall = jnp.maximum(jnp.max(block_max, axis=0), fresh_max)
    block_scale = jnp.exp(block_max - overall[None])
    fresh_scale = jnp.exp(fresh_max - overall)
    weighted = jnp.sum(block_scale * blocks, axis=0) + fresh_scale * fresh
    numer = weighted[:, :HD]
    denom = weighted[:, HD + 1 : HD + 2]
    return (numer / denom).astype(jnp.bfloat16)


def _down_combine(buf1, middle_ref):
    return (middle_ref[...] + branch_factor * jnp.sum(buf1[...], axis=0)).astype(jnp.bfloat16)


STEPS = 4
norm_epsilon = 1e-05
embed_factor = 12.0
score_factor = 0.015625
branch_factor = 0.22
rope_base = 10000000.0
masked_floor = -1e30


def rms_scale(resid, gain):
    mean_square = jnp.mean(resid * resid, axis=-1, keepdims=True)
    return resid * lax.rsqrt(mean_square + norm_epsilon) * gain.astype(jnp.float32)


def rotate(vectors, where):
    half = vectors.shape[-1] // 2
    freqs = rope_base ** (-2.0 * jnp.arange(half, dtype=jnp.float32) / vectors.shape[-1])
    angle = where[..., None] * freqs
    cosine = jnp.cos(angle)
    sine = jnp.sin(angle)
    first_half = vectors[..., :half]
    second_half = vectors[..., half:]
    return jnp.concatenate(
        [first_half * cosine - second_half * sine, second_half * cosine + first_half * sine],
        axis=-1,
    )


def partial_softmax(queries, keys, values, valid):
    scores = (
        jnp.einsum("rskgd,rpkd->rskgp", queries, keys, preferred_element_type=jnp.float32)
        * score_factor
    )
    maxima = jnp.max(jnp.where(valid, scores, masked_floor), axis=-1)
    expo = jnp.exp(jnp.where(valid, scores - maxima[..., None], masked_floor))
    totals = jnp.sum(expo, axis=-1)
    outputs = jnp.einsum(
        "rskgp,rpkd->rskgd", expo.astype(jnp.bfloat16), values, preferred_element_type=jnp.float32
    )
    return (maxima, totals, outputs)


def shards(
    token_ids,
    cache_lengths,
    embed_table,
    key_cache,
    value_cache,
    norm_attn,
    norm_mlp,
    w_qkv,
    w_out,
    w_gate,
    w_up,
    w_down,
):
    n = lax.axis_size("seq")
    place = lax.axis_index("seq")
    req_all = token_ids.shape[0]
    steps = token_ids.shape[1]
    rows = req_all * steps
    ctx_own = key_cache.shape[1]
    width = embed_table.shape[0] * n
    att_width = H * HD
    kv_width = KVH * HD
    group = H // KVH

    vocab = embed_table.shape[1]
    onehot = (
        token_ids.reshape(-1)[:, None] == jnp.arange(vocab, dtype=jnp.int32)[None, :]
    ).astype(embed_table.dtype)
    picked = lax.dot_general(
        onehot, embed_table, (((1,), (1,)), ((), ())), preferred_element_type=jnp.float32
    ).astype(embed_table.dtype)
    whole = exchange(picked, n, True, 0)
    resid = jnp.transpose(whole, (1, 0, 2)).reshape(rows, width).astype(jnp.float32) * embed_factor

    slot_pos = place * ctx_own + jnp.arange(ctx_own, dtype=jnp.int32)
    cache_valid = (slot_pos[None, :] < cache_lengths[:, None]).reshape(req_all, 1, 1, 1, ctx_own)
    cache_keys = key_cache.reshape(req_all, ctx_own, KVH, HD)
    cache_values = value_cache.reshape(req_all, ctx_own, KVH, HD)

    normed = rms_scale(resid, norm_attn).astype(jnp.bfloat16)
    qkv_cols = jnp.dot(normed, w_qkv, preferred_element_type=jnp.float32).astype(jnp.bfloat16)
    qkv_got = exchange(qkv_cols, n, True, 1)
    qkv_all = jnp.transpose(qkv_got, (1, 0, 2)).reshape(req_all, steps, -1)
    where = (cache_lengths[:, None] + jnp.arange(steps, dtype=jnp.int32)[None, :]).astype(
        jnp.float32
    )
    queries = rotate(
        qkv_all[..., :att_width].reshape(req_all, steps, H, HD).astype(jnp.float32),
        where[..., None],
    ).astype(jnp.bfloat16)
    keys_new = rotate(
        qkv_all[..., att_width : att_width + kv_width]
        .reshape(req_all, steps, KVH, HD)
        .astype(jnp.float32),
        where[..., None],
    ).astype(jnp.bfloat16)
    values_new = qkv_all[..., att_width + kv_width :].reshape(req_all, steps, KVH, HD)
    grouped = queries.reshape(req_all, steps, KVH, group, HD)
    cache_max, cache_total, cache_out = partial_softmax(
        grouped, cache_keys, cache_values, cache_valid
    )
    fresh_valid = (
        jnp.arange(steps, dtype=jnp.int32)[None, :] <= jnp.arange(steps, dtype=jnp.int32)[:, None]
    ).reshape(1, steps, 1, 1, steps)
    fresh_max, fresh_total, fresh_out = partial_softmax(grouped, keys_new, values_new, fresh_valid)

    pairs = rows * H // n
    lanes = 128
    packed = jnp.concatenate(
        [
            cache_out.reshape(n, pairs, HD),
            cache_max.reshape(n, pairs, 1),
            cache_total.reshape(n, pairs, 1),
            jnp.zeros((n, pairs, lanes - HD - 2), jnp.float32),
        ],
        axis=-1,
    )
    own_fresh_max = lax.dynamic_index_in_dim(fresh_max.reshape(n, pairs), place, 0, False)
    own_fresh_total = lax.dynamic_index_in_dim(fresh_total.reshape(n, pairs), place, 0, False)
    own_fresh_out = lax.dynamic_index_in_dim(fresh_out.reshape(n, pairs, HD), place, 0, False)
    fresh_packed = jnp.concatenate(
        [
            own_fresh_out,
            own_fresh_max[:, None],
            own_fresh_total[:, None],
            jnp.zeros((pairs, lanes - HD - 2), jnp.float32),
        ],
        axis=-1,
    )
    attention = two_phase(
        packed, [fresh_packed], _merge_combine, (pairs, HD), jnp.bfloat16, n, 2
    ).reshape(rows, att_width)

    proj_cols = jnp.dot(attention, w_out, preferred_element_type=jnp.float32).astype(jnp.bfloat16)
    proj_got = exchange(proj_cols, n, True, 3)
    projected = jnp.transpose(proj_got, (1, 0, 2)).reshape(rows, width)
    middle = resid + branch_factor * projected.astype(jnp.float32)
    normed_mlp = rms_scale(middle, norm_mlp).astype(jnp.bfloat16)
    gate = jnp.dot(normed_mlp, w_gate, preferred_element_type=jnp.float32)
    upward = jnp.dot(normed_mlp, w_up, preferred_element_type=jnp.float32)
    hidden = (jax.nn.silu(gate) * upward).astype(jnp.bfloat16)
    down_part = jnp.dot(hidden, w_down, preferred_element_type=jnp.float32)
    cols = width // n
    middle_own = lax.dynamic_slice_in_dim(middle, place * cols, cols, axis=1)
    down_send = jnp.transpose(down_part.reshape(rows, n, cols), (1, 0, 2))
    out_got = two_phase(down_send, [middle_own], _down_combine, (rows, cols), jnp.bfloat16, n, 4)
    return jnp.transpose(out_got, (1, 0, 2)).reshape(req_all, steps, width)


def solution(mesh):
    return jax.shard_map(
        shards,
        mesh=mesh,
        in_specs=(
            P("rep", None),
            P("rep"),
            P("seq", None),
            P("rep", "seq", None),
            P("rep", "seq", None),
            P(),
            P(),
            P(None, "seq"),
            P(None, "seq"),
            P(None, "seq"),
            P(None, "seq"),
            P("seq", None),
        ),
        out_specs=P("rep", None, None),
        check_vma=False,
    )
```

```python
import functools

import jax
import jax.numpy as jnp
from jax import lax
from jax.experimental import pallas as pl
from jax.experimental.pallas import tpu as pltpu
from jax.sharding import PartitionSpec as P

H = 32
KVH = 8
HD = 64

MESH_ID = pl.DeviceIdType.MESH


def _greet(n, me, rep):
    barrier = pltpu.get_barrier_semaphore()

    def greet(k, carry):
        peer = lax.rem(me + k, n)
        pl.semaphore_signal(barrier, inc=1, device_id=(peer, rep), device_id_type=MESH_ID)
        return carry

    lax.fori_loop(1, n, greet, 0)
    pl.semaphore_wait(barrier, n - 1)


def _exchange_kernel(n, gather, x_ref, o_ref, buf, send_sems, recv_sems, local_sem):
    me = lax.axis_index("seq")
    rep = lax.axis_index("rep")
    _greet(n, me, rep)
    source = (lambda peer: x_ref) if gather else (lambda peer: x_ref.at[peer])
    _stage(n, me, lambda j: j, rep, source, buf, send_sems, recv_sems, local_sem)
    o_ref[...] = buf[...]


def _nbytes(shape, dtype):
    size = int(jnp.dtype(dtype).itemsize)
    for d in shape:
        size *= int(d)
    return size


def exchange(x, n, gather, cid):
    blk = x.shape if gather else x.shape[1:]
    shape = (n,) + tuple(blk)
    nbytes = _nbytes(shape, x.dtype)
    return pl.pallas_call(
        functools.partial(_exchange_kernel, n, gather),
        out_shape=jax.ShapeDtypeStruct(shape, x.dtype),
        in_specs=[pl.BlockSpec(memory_space=pltpu.VMEM)],
        out_specs=pl.BlockSpec(memory_space=pltpu.VMEM),
        scratch_shapes=[
            pltpu.VMEM(shape, x.dtype),
            pltpu.SemaphoreType.DMA(()),
            pltpu.SemaphoreType.DMA(()),
            pltpu.SemaphoreType.DMA(()),
        ],
        compiler_params=pltpu.CompilerParams(collective_id=cid, has_side_effects=True),
        cost_estimate=pl.CostEstimate(flops=0, transcendentals=0, bytes_accessed=2 * nbytes),
        name="exchange_%d" % cid,
    )(x)


def _split(n):
    low = 1
    for c in range(1, n + 1):
        if n % c == 0 and c * c <= n:
            low = c
    return low


def _stage(m, mine, dev_of, rep, source, buf, send_sem, recv_sem, local_sem):
    def copy(j, slot):
        return pltpu.make_async_remote_copy(
            src_ref=source(j),
            dst_ref=buf.at[slot],
            send_sem=send_sem,
            recv_sem=recv_sem,
            device_id=(dev_of(j), rep),
            device_id_type=MESH_ID,
        )

    def send(k, carry):
        j = lax.rem(mine + k, m)
        copy(j, mine).start()
        return carry

    lax.fori_loop(1, m, send, 0)
    local = pltpu.make_async_copy(source(mine), buf.at[mine], local_sem)
    local.start()
    rest = buf.at[pl.ds(0, m - 1)]
    every = pltpu.make_async_remote_copy(
        src_ref=rest,
        dst_ref=rest,
        send_sem=send_sem,
        recv_sem=recv_sem,
        device_id=(dev_of(lax.rem(mine + 1, m)), rep),
        device_id_type=MESH_ID,
    )
    every.wait_send()
    every.wait_recv()
    local.wait()


def _greet2(low, high, hi, lo, rep):
    barrier = pltpu.get_barrier_semaphore()

    def near(k, carry):
        peer = hi * low + lax.rem(lo + k, low)
        pl.semaphore_signal(barrier, inc=1, device_id=(peer, rep), device_id_type=MESH_ID)
        return carry

    def far(k, carry):
        peer = lax.rem(hi + k, high) * low + lo
        pl.semaphore_signal(barrier, inc=1, device_id=(peer, rep), device_id_type=MESH_ID)
        return carry

    lax.fori_loop(1, low, near, 0)
    lax.fori_loop(1, high, far, 0)
    pl.semaphore_wait(barrier, low + high - 2)


def _gather2_kernel(n, low, x_ref, o_ref, buf1, buf2, s1, r1, l1, s2, r2, l2):
    high = n // low
    me = lax.axis_index("seq")
    rep = lax.axis_index("rep")
    hi = me // low
    lo = lax.rem(me, low)
    _greet2(low, high, hi, lo, rep)
    _stage(low, lo, lambda j: hi * low + j, rep, lambda j: x_ref, buf1, s1, r1, l1)
    _stage(high, hi, lambda j: j * low + lo, rep, lambda j: buf1, buf2, s2, r2, l2)
    o_ref[...] = buf2[...]


def gather2(x, n, cid):
    low = _split(n)
    high = n // low
    blk = tuple(x.shape)
    shape = (high, low) + blk
    nbytes = _nbytes(shape, x.dtype)
    out = pl.pallas_call(
        functools.partial(_gather2_kernel, n, low),
        out_shape=jax.ShapeDtypeStruct(shape, x.dtype),
        in_specs=[pl.BlockSpec(memory_space=pltpu.VMEM)],
        out_specs=pl.BlockSpec(memory_space=pltpu.VMEM),
        scratch_shapes=[
            pltpu.VMEM((low,) + blk, x.dtype),
            pltpu.VMEM(shape, x.dtype),
            pltpu.SemaphoreType.DMA(()),
            pltpu.SemaphoreType.DMA(()),
            pltpu.SemaphoreType.DMA(()),
            pltpu.SemaphoreType.DMA(()),
            pltpu.SemaphoreType.DMA(()),
            pltpu.SemaphoreType.DMA(()),
        ],
        compiler_params=pltpu.CompilerParams(collective_id=cid, has_side_effects=True),
        cost_estimate=pl.CostEstimate(flops=0, transcendentals=0, bytes_accessed=2 * nbytes),
        name="gather2_%d" % cid,
    )(x)
    return out.reshape((n,) + blk)


def _two_phase_kernel(n, combine, n_extra, *refs):
    x_ref = refs[0]
    extras = refs[1 : 1 + n_extra]
    o_ref = refs[1 + n_extra]
    buf1, own, buf2, s1, r1, l1, s2, r2, l2 = refs[2 + n_extra :]
    me = lax.axis_index("seq")
    rep = lax.axis_index("rep")
    _greet(n, me, rep)
    _stage(n, me, lambda j: j, rep, lambda peer: x_ref.at[peer], buf1, s1, r1, l1)
    own[...] = combine(buf1, *extras)
    _stage(n, me, lambda j: j, rep, lambda peer: own, buf2, s2, r2, l2)
    o_ref[...] = buf2[...]


def two_phase(x, extras, combine, own_shape, own_dtype, n, cid):
    first = x.shape
    shape = (n,) + tuple(own_shape)
    nbytes = _nbytes(first, x.dtype) + _nbytes(shape, own_dtype)
    return pl.pallas_call(
        functools.partial(_two_phase_kernel, n, combine, len(extras)),
        out_shape=jax.ShapeDtypeStruct(shape, own_dtype),
        in_specs=[pl.BlockSpec(memory_space=pltpu.VMEM)] * (1 + len(extras)),
        out_specs=pl.BlockSpec(memory_space=pltpu.VMEM),
        scratch_shapes=[
            pltpu.VMEM(first, x.dtype),
            pltpu.VMEM(tuple(own_shape), own_dtype),
            pltpu.VMEM(shape, own_dtype),
            pltpu.SemaphoreType.DMA(()),
            pltpu.SemaphoreType.DMA(()),
            pltpu.SemaphoreType.DMA(()),
            pltpu.SemaphoreType.DMA(()),
            pltpu.SemaphoreType.DMA(()),
            pltpu.SemaphoreType.DMA(()),
        ],
        compiler_params=pltpu.CompilerParams(collective_id=cid, has_side_effects=True),
        cost_estimate=pl.CostEstimate(flops=0, transcendentals=0, bytes_accessed=2 * nbytes),
        name="two_phase_%d" % cid,
    )(x, *extras)


def _merge_combine(buf1, fresh_ref):
    blocks = buf1[...]
    fresh = fresh_ref[...]
    block_max = blocks[:, :, HD : HD + 1]
    fresh_max = fresh[:, HD : HD + 1]
    overall = jnp.maximum(jnp.max(block_max, axis=0), fresh_max)
    block_scale = jnp.exp(block_max - overall[None])
    fresh_scale = jnp.exp(fresh_max - overall)
    weighted = jnp.sum(block_scale * blocks, axis=0) + fresh_scale * fresh
    numer = weighted[:, :HD]
    denom = weighted[:, HD + 1 : HD + 2]
    return (numer / denom).astype(jnp.bfloat16)


def _down_combine(buf1, middle_ref):
    return (middle_ref[...] + branch_factor * jnp.sum(buf1[...], axis=0)).astype(jnp.bfloat16)


STEPS = 4
norm_epsilon = 1e-05
embed_factor = 12.0
score_factor = 0.015625
branch_factor = 0.22
rope_base = 10000000.0
masked_floor = -1e30


def rms_scale(resid, gain):
    mean_square = jnp.mean(resid * resid, axis=-1, keepdims=True)
    return resid * lax.rsqrt(mean_square + norm_epsilon) * gain.astype(jnp.float32)


def rms_columns(resid, gain):
    mean_square = jnp.mean(resid * resid, axis=0, keepdims=True)
    return resid * lax.rsqrt(mean_square + norm_epsilon) * gain.astype(jnp.float32)[:, None]


def rotate(vectors, where):
    half = vectors.shape[-1] // 2
    freqs = rope_base ** (-2.0 * jnp.arange(half, dtype=jnp.float32) / vectors.shape[-1])
    angle = where[..., None] * freqs
    cosine = jnp.cos(angle)
    sine = jnp.sin(angle)
    first_half = vectors[..., :half]
    second_half = vectors[..., half:]
    return jnp.concatenate(
        [first_half * cosine - second_half * sine, second_half * cosine + first_half * sine],
        axis=-1,
    )


def partial_softmax(queries, keys, values, valid):
    scores = (
        jnp.einsum("rskgd,rpkd->rskgp", queries, keys, preferred_element_type=jnp.float32)
        * score_factor
    )
    maxima = jnp.max(jnp.where(valid, scores, masked_floor), axis=-1)
    expo = jnp.exp(jnp.where(valid, scores - maxima[..., None], masked_floor))
    totals = jnp.sum(expo, axis=-1)
    outputs = jnp.einsum(
        "rskgp,rpkd->rskgd", expo.astype(jnp.bfloat16), values, preferred_element_type=jnp.float32
    )
    return (maxima, totals, outputs)


def shards(
    token_ids,
    cache_lengths,
    embed_table,
    key_cache,
    value_cache,
    norm_attn,
    norm_mlp,
    w_qkv,
    w_out,
    w_gate,
    w_up,
    w_down,
):
    n = lax.axis_size("seq")
    place = lax.axis_index("seq")
    req_all = token_ids.shape[0]
    steps = token_ids.shape[1]
    rows = req_all * steps
    ctx_own = key_cache.shape[1]
    width = embed_table.shape[0] * n
    att_width = H * HD
    kv_width = KVH * HD
    group = H // KVH

    vocab = embed_table.shape[1]
    onehot = (
        token_ids.reshape(-1)[:, None] == jnp.arange(vocab, dtype=jnp.int32)[None, :]
    ).astype(embed_table.dtype)
    picked = lax.dot_general(
        embed_table, onehot, (((1,), (1,)), ((), ())), preferred_element_type=jnp.float32
    ).astype(embed_table.dtype)
    whole = exchange(picked, n, True, 0)
    resid = whole.reshape(width, rows).astype(jnp.float32) * embed_factor

    slot_pos = place * ctx_own + jnp.arange(ctx_own, dtype=jnp.int32)
    cache_valid = (slot_pos[None, :] < cache_lengths[:, None]).reshape(req_all, 1, 1, 1, ctx_own)
    cache_keys = key_cache.reshape(req_all, ctx_own, KVH, HD)
    cache_values = value_cache.reshape(req_all, ctx_own, KVH, HD)

    normed = rms_columns(resid, norm_attn).astype(jnp.bfloat16)
    qkv_cols = lax.dot_general(
        normed, w_qkv, (((0,), (0,)), ((), ())), preferred_element_type=jnp.float32
    ).astype(jnp.bfloat16)
    qkv_got = exchange(qkv_cols, n, True, 1)
    qkv_all = jnp.transpose(qkv_got, (1, 0, 2)).reshape(req_all, steps, -1)
    where = (cache_lengths[:, None] + jnp.arange(steps, dtype=jnp.int32)[None, :]).astype(
        jnp.float32
    )
    queries = rotate(
        qkv_all[..., :att_width].reshape(req_all, steps, H, HD).astype(jnp.float32),
        where[..., None],
    ).astype(jnp.bfloat16)
    keys_new = rotate(
        qkv_all[..., att_width : att_width + kv_width]
        .reshape(req_all, steps, KVH, HD)
        .astype(jnp.float32),
        where[..., None],
    ).astype(jnp.bfloat16)
    values_new = qkv_all[..., att_width + kv_width :].reshape(req_all, steps, KVH, HD)
    grouped = queries.reshape(req_all, steps, KVH, group, HD)
    cache_max, cache_total, cache_out = partial_softmax(
        grouped, cache_keys, cache_values, cache_valid
    )
    fresh_valid = (
        jnp.arange(steps, dtype=jnp.int32)[None, :] <= jnp.arange(steps, dtype=jnp.int32)[:, None]
    ).reshape(1, steps, 1, 1, steps)
    fresh_max, fresh_total, fresh_out = partial_softmax(grouped, keys_new, values_new, fresh_valid)

    pairs = rows * H // n
    lanes = 128
    packed = jnp.concatenate(
        [
            cache_out.reshape(n, pairs, HD),
            cache_max.reshape(n, pairs, 1),
            cache_total.reshape(n, pairs, 1),
            jnp.zeros((n, pairs, lanes - HD - 2), jnp.float32),
        ],
        axis=-1,
    )
    own_fresh_max = lax.dynamic_index_in_dim(fresh_max.reshape(n, pairs), place, 0, False)
    own_fresh_total = lax.dynamic_index_in_dim(fresh_total.reshape(n, pairs), place, 0, False)
    own_fresh_out = lax.dynamic_index_in_dim(fresh_out.reshape(n, pairs, HD), place, 0, False)
    fresh_packed = jnp.concatenate(
        [
            own_fresh_out,
            own_fresh_max[:, None],
            own_fresh_total[:, None],
            jnp.zeros((pairs, lanes - HD - 2), jnp.float32),
        ],
        axis=-1,
    )
    attention = two_phase(
        packed, [fresh_packed], _merge_combine, (pairs, HD), jnp.bfloat16, n, 2
    ).reshape(rows, att_width)

    proj_cols = lax.dot_general(
        w_out, attention, (((0,), (1,)), ((), ())), preferred_element_type=jnp.float32
    ).astype(jnp.bfloat16)
    projected = exchange(proj_cols, n, True, 3).reshape(width, rows)
    middle = resid + branch_factor * projected.astype(jnp.float32)
    normed_mlp = rms_columns(middle, norm_mlp).astype(jnp.bfloat16)
    gate = lax.dot_general(
        normed_mlp, w_gate, (((0,), (0,)), ((), ())), preferred_element_type=jnp.float32
    )
    upward = lax.dot_general(
        normed_mlp, w_up, (((0,), (0,)), ((), ())), preferred_element_type=jnp.float32
    )
    hidden = (jax.nn.silu(gate) * upward).astype(jnp.bfloat16)
    down_part = lax.dot_general(
        w_down, hidden, (((0,), (1,)), ((), ())), preferred_element_type=jnp.float32
    )
    cols = width // n
    middle_own = lax.dynamic_slice_in_dim(middle, place * cols, cols, axis=0)
    out_got = two_phase(
        down_part.reshape(n, cols, rows), [middle_own], _down_combine, (cols, rows), jnp.bfloat16, n, 4
    )
    return jnp.transpose(out_got.reshape(width, rows), (1, 0)).reshape(req_all, steps, width)


def solution(mesh):
    return jax.shard_map(
        shards,
        mesh=mesh,
        in_specs=(
            P("rep", None),
            P("rep"),
            P("seq", None),
            P("rep", "seq", None),
            P("rep", "seq", None),
            P(),
            P(),
            P(None, "seq"),
            P(None, "seq"),
            P(None, "seq"),
            P(None, "seq"),
            P("seq", None),
        ),
        out_specs=P("rep", None, None),
        check_vma=False,
    )
```

```python
import functools

import jax
import jax.numpy as jnp
from jax import lax
from jax.experimental import pallas as pl
from jax.experimental.pallas import tpu as pltpu
from jax.sharding import PartitionSpec as P

H = 32
KVH = 8
HD = 64

MESH_ID = pl.DeviceIdType.MESH


def _greet(n, me, rep):
    barrier = pltpu.get_barrier_semaphore()

    def greet(k, carry):
        peer = lax.rem(me + k, n)
        pl.semaphore_signal(barrier, inc=1, device_id=(peer, rep), device_id_type=MESH_ID)
        return carry

    lax.fori_loop(1, n, greet, 0)
    pl.semaphore_wait(barrier, n - 1)


def _exchange_kernel(n, gather, x_ref, o_ref, send_sems, recv_sems, local_sem):
    buf = o_ref
    me = lax.axis_index("seq")
    rep = lax.axis_index("rep")
    _greet(n, me, rep)
    source = (lambda peer: x_ref) if gather else (lambda peer: x_ref.at[peer])
    _stage(n, me, lambda j: j, rep, source, buf, send_sems, recv_sems, local_sem)


def _nbytes(shape, dtype):
    size = int(jnp.dtype(dtype).itemsize)
    for d in shape:
        size *= int(d)
    return size


def exchange(x, n, gather, cid):
    blk = x.shape if gather else x.shape[1:]
    shape = (n,) + tuple(blk)
    nbytes = _nbytes(shape, x.dtype)
    return pl.pallas_call(
        functools.partial(_exchange_kernel, n, gather),
        out_shape=jax.ShapeDtypeStruct(shape, x.dtype),
        in_specs=[pl.BlockSpec(memory_space=pltpu.VMEM)],
        out_specs=pl.BlockSpec(memory_space=pltpu.VMEM),
        scratch_shapes=[
            pltpu.SemaphoreType.DMA(()),
            pltpu.SemaphoreType.DMA(()),
            pltpu.SemaphoreType.DMA(()),
        ],
        compiler_params=pltpu.CompilerParams(collective_id=cid, has_side_effects=True),
        cost_estimate=pl.CostEstimate(flops=0, transcendentals=0, bytes_accessed=2 * nbytes),
        name="exchange_%d" % cid,
    )(x)


def _split(n):
    low = 1
    for c in range(1, n + 1):
        if n % c == 0 and c * c <= n:
            low = c
    return low


def _stage(m, mine, dev_of, rep, source, buf, send_sem, recv_sem, local_sem):
    def copy(j, slot):
        return pltpu.make_async_remote_copy(
            src_ref=source(j),
            dst_ref=buf.at[slot],
            send_sem=send_sem,
            recv_sem=recv_sem,
            device_id=(dev_of(j), rep),
            device_id_type=MESH_ID,
        )

    def send(k, carry):
        j = lax.rem(mine + k, m)
        copy(j, mine).start()
        return carry

    lax.fori_loop(1, m, send, 0)
    local = pltpu.make_async_copy(source(mine), buf.at[mine], local_sem)
    local.start()
    rest = buf.at[pl.ds(0, m - 1)]
    every = pltpu.make_async_remote_copy(
        src_ref=rest,
        dst_ref=rest,
        send_sem=send_sem,
        recv_sem=recv_sem,
        device_id=(dev_of(lax.rem(mine + 1, m)), rep),
        device_id_type=MESH_ID,
    )
    every.wait_send()
    every.wait_recv()
    local.wait()


def _greet2(low, high, hi, lo, rep):
    barrier = pltpu.get_barrier_semaphore()

    def near(k, carry):
        peer = hi * low + lax.rem(lo + k, low)
        pl.semaphore_signal(barrier, inc=1, device_id=(peer, rep), device_id_type=MESH_ID)
        return carry

    def far(k, carry):
        peer = lax.rem(hi + k, high) * low + lo
        pl.semaphore_signal(barrier, inc=1, device_id=(peer, rep), device_id_type=MESH_ID)
        return carry

    lax.fori_loop(1, low, near, 0)
    lax.fori_loop(1, high, far, 0)
    pl.semaphore_wait(barrier, low + high - 2)


def _gather2_kernel(n, low, x_ref, o_ref, buf1, buf2, s1, r1, l1, s2, r2, l2):
    high = n // low
    me = lax.axis_index("seq")
    rep = lax.axis_index("rep")
    hi = me // low
    lo = lax.rem(me, low)
    _greet2(low, high, hi, lo, rep)
    _stage(low, lo, lambda j: hi * low + j, rep, lambda j: x_ref, buf1, s1, r1, l1)
    _stage(high, hi, lambda j: j * low + lo, rep, lambda j: buf1, buf2, s2, r2, l2)
    o_ref[...] = buf2[...]


def gather2(x, n, cid):
    low = _split(n)
    high = n // low
    blk = tuple(x.shape)
    shape = (high, low) + blk
    nbytes = _nbytes(shape, x.dtype)
    out = pl.pallas_call(
        functools.partial(_gather2_kernel, n, low),
        out_shape=jax.ShapeDtypeStruct(shape, x.dtype),
        in_specs=[pl.BlockSpec(memory_space=pltpu.VMEM)],
        out_specs=pl.BlockSpec(memory_space=pltpu.VMEM),
        scratch_shapes=[
            pltpu.VMEM((low,) + blk, x.dtype),
            pltpu.VMEM(shape, x.dtype),
            pltpu.SemaphoreType.DMA(()),
            pltpu.SemaphoreType.DMA(()),
            pltpu.SemaphoreType.DMA(()),
            pltpu.SemaphoreType.DMA(()),
            pltpu.SemaphoreType.DMA(()),
            pltpu.SemaphoreType.DMA(()),
        ],
        compiler_params=pltpu.CompilerParams(collective_id=cid, has_side_effects=True),
        cost_estimate=pl.CostEstimate(flops=0, transcendentals=0, bytes_accessed=2 * nbytes),
        name="gather2_%d" % cid,
    )(x)
    return out.reshape((n,) + blk)


def _two_phase_kernel(n, combine, n_extra, *refs):
    x_ref = refs[0]
    extras = refs[1 : 1 + n_extra]
    o_ref = refs[1 + n_extra]
    buf1, own, s1, r1, l1, s2, r2, l2 = refs[2 + n_extra :]
    buf2 = o_ref
    me = lax.axis_index("seq")
    rep = lax.axis_index("rep")
    _greet(n, me, rep)
    _stage(n, me, lambda j: j, rep, lambda peer: x_ref.at[peer], buf1, s1, r1, l1)
    own[...] = combine(buf1, *extras)
    _stage(n, me, lambda j: j, rep, lambda peer: own, buf2, s2, r2, l2)


def two_phase(x, extras, combine, own_shape, own_dtype, n, cid):
    first = x.shape
    shape = (n,) + tuple(own_shape)
    nbytes = _nbytes(first, x.dtype) + _nbytes(shape, own_dtype)
    return pl.pallas_call(
        functools.partial(_two_phase_kernel, n, combine, len(extras)),
        out_shape=jax.ShapeDtypeStruct(shape, own_dtype),
        in_specs=[pl.BlockSpec(memory_space=pltpu.VMEM)] * (1 + len(extras)),
        out_specs=pl.BlockSpec(memory_space=pltpu.VMEM),
        scratch_shapes=[
            pltpu.VMEM(first, x.dtype),
            pltpu.VMEM(tuple(own_shape), own_dtype),
            pltpu.SemaphoreType.DMA(()),
            pltpu.SemaphoreType.DMA(()),
            pltpu.SemaphoreType.DMA(()),
            pltpu.SemaphoreType.DMA(()),
            pltpu.SemaphoreType.DMA(()),
            pltpu.SemaphoreType.DMA(()),
        ],
        compiler_params=pltpu.CompilerParams(collective_id=cid, has_side_effects=True),
        cost_estimate=pl.CostEstimate(flops=0, transcendentals=0, bytes_accessed=2 * nbytes),
        name="two_phase_%d" % cid,
    )(x, *extras)


def _merge_combine(buf1, fresh_ref):
    blocks = buf1[...]
    fresh = fresh_ref[...]
    block_max = blocks[:, :, HD : HD + 1]
    fresh_max = fresh[:, HD : HD + 1]
    overall = jnp.maximum(jnp.max(block_max, axis=0), fresh_max)
    block_scale = jnp.exp(block_max - overall[None])
    fresh_scale = jnp.exp(fresh_max - overall)
    weighted = jnp.sum(block_scale * blocks, axis=0) + fresh_scale * fresh
    numer = weighted[:, :HD]
    denom = weighted[:, HD + 1 : HD + 2]
    return (numer / denom).astype(jnp.bfloat16)


def _down_combine(buf1, middle_ref):
    return (middle_ref[...] + branch_factor * jnp.sum(buf1[...], axis=0)).astype(jnp.bfloat16)


STEPS = 4
norm_epsilon = 1e-05
embed_factor = 12.0
score_factor = 0.015625
branch_factor = 0.22
rope_base = 10000000.0
masked_floor = -1e30


def rms_scale(resid, gain):
    mean_square = jnp.mean(resid * resid, axis=-1, keepdims=True)
    return resid * lax.rsqrt(mean_square + norm_epsilon) * gain.astype(jnp.float32)


def rotate(vectors, where):
    half = vectors.shape[-1] // 2
    freqs = rope_base ** (-2.0 * jnp.arange(half, dtype=jnp.float32) / vectors.shape[-1])
    angle = where[..., None] * freqs
    cosine = jnp.cos(angle)
    sine = jnp.sin(angle)
    first_half = vectors[..., :half]
    second_half = vectors[..., half:]
    return jnp.concatenate(
        [first_half * cosine - second_half * sine, second_half * cosine + first_half * sine],
        axis=-1,
    )


def partial_softmax(queries, keys, values, valid):
    scores = (
        jnp.einsum("rskgd,rpkd->rskgp", queries, keys, preferred_element_type=jnp.float32)
        * score_factor
    )
    maxima = jnp.max(jnp.where(valid, scores, masked_floor), axis=-1)
    expo = jnp.exp(jnp.where(valid, scores - maxima[..., None], masked_floor))
    totals = jnp.sum(expo, axis=-1)
    outputs = jnp.einsum(
        "rskgp,rpkd->rskgd", expo.astype(jnp.bfloat16), values, preferred_element_type=jnp.float32
    )
    return (maxima, totals, outputs)


def shards(
    token_ids,
    cache_lengths,
    embed_table,
    key_cache,
    value_cache,
    norm_attn,
    norm_mlp,
    w_qkv,
    w_out,
    w_gate,
    w_up,
    w_down,
):
    n = lax.axis_size("seq")
    place = lax.axis_index("seq")
    req_all = token_ids.shape[0]
    steps = token_ids.shape[1]
    rows = req_all * steps
    ctx_own = key_cache.shape[1]
    width = embed_table.shape[0] * n
    att_width = H * HD
    kv_width = KVH * HD
    group = H // KVH

    vocab = embed_table.shape[1]
    onehot = (
        token_ids.reshape(-1)[:, None] == jnp.arange(vocab, dtype=jnp.int32)[None, :]
    ).astype(embed_table.dtype)
    picked = lax.dot_general(
        onehot, embed_table, (((1,), (1,)), ((), ())), preferred_element_type=jnp.float32
    ).astype(embed_table.dtype)
    whole = exchange(picked, n, True, 0)
    resid = jnp.transpose(whole, (1, 0, 2)).reshape(rows, width).astype(jnp.float32) * embed_factor

    slot_pos = place * ctx_own + jnp.arange(ctx_own, dtype=jnp.int32)
    cache_valid = (slot_pos[None, :] < cache_lengths[:, None]).reshape(req_all, 1, 1, 1, ctx_own)
    cache_keys = key_cache.reshape(req_all, ctx_own, KVH, HD)
    cache_values = value_cache.reshape(req_all, ctx_own, KVH, HD)

    normed = rms_scale(resid, norm_attn).astype(jnp.bfloat16)
    qkv_cols = jnp.dot(normed, w_qkv, preferred_element_type=jnp.float32).astype(jnp.bfloat16)
    qkv_got = exchange(qkv_cols, n, True, 1)
    qkv_all = jnp.transpose(qkv_got, (1, 0, 2)).reshape(req_all, steps, -1)
    where = (cache_lengths[:, None] + jnp.arange(steps, dtype=jnp.int32)[None, :]).astype(
        jnp.float32
    )
    queries = rotate(
        qkv_all[..., :att_width].reshape(req_all, steps, H, HD).astype(jnp.float32),
        where[..., None],
    ).astype(jnp.bfloat16)
    keys_new = rotate(
        qkv_all[..., att_width : att_width + kv_width]
        .reshape(req_all, steps, KVH, HD)
        .astype(jnp.float32),
        where[..., None],
    ).astype(jnp.bfloat16)
    values_new = qkv_all[..., att_width + kv_width :].reshape(req_all, steps, KVH, HD)
    grouped = queries.reshape(req_all, steps, KVH, group, HD)
    cache_max, cache_total, cache_out = partial_softmax(
        grouped, cache_keys, cache_values, cache_valid
    )
    fresh_valid = (
        jnp.arange(steps, dtype=jnp.int32)[None, :] <= jnp.arange(steps, dtype=jnp.int32)[:, None]
    ).reshape(1, steps, 1, 1, steps)
    fresh_max, fresh_total, fresh_out = partial_softmax(grouped, keys_new, values_new, fresh_valid)

    pairs = rows * H // n
    lanes = 128
    packed = jnp.concatenate(
        [
            cache_out.reshape(n, pairs, HD),
            cache_max.reshape(n, pairs, 1),
            cache_total.reshape(n, pairs, 1),
            jnp.zeros((n, pairs, lanes - HD - 2), jnp.float32),
        ],
        axis=-1,
    )
    own_fresh_max = lax.dynamic_index_in_dim(fresh_max.reshape(n, pairs), place, 0, False)
    own_fresh_total = lax.dynamic_index_in_dim(fresh_total.reshape(n, pairs), place, 0, False)
    own_fresh_out = lax.dynamic_index_in_dim(fresh_out.reshape(n, pairs, HD), place, 0, False)
    fresh_packed = jnp.concatenate(
        [
            own_fresh_out,
            own_fresh_max[:, None],
            own_fresh_total[:, None],
            jnp.zeros((pairs, lanes - HD - 2), jnp.float32),
        ],
        axis=-1,
    )
    attention = two_phase(
        packed, [fresh_packed], _merge_combine, (pairs, HD), jnp.bfloat16, n, 2
    ).reshape(rows, att_width)

    proj_cols = jnp.dot(attention, w_out, preferred_element_type=jnp.float32).astype(jnp.bfloat16)
    proj_got = exchange(proj_cols, n, True, 3)
    projected = jnp.transpose(proj_got, (1, 0, 2)).reshape(rows, width)
    middle = resid + branch_factor * projected.astype(jnp.float32)
    normed_mlp = rms_scale(middle, norm_mlp).astype(jnp.bfloat16)
    gate = jnp.dot(normed_mlp, w_gate, preferred_element_type=jnp.float32)
    upward = jnp.dot(normed_mlp, w_up, preferred_element_type=jnp.float32)
    hidden = (jax.nn.silu(gate) * upward).astype(jnp.bfloat16)
    down_part = jnp.dot(hidden, w_down, preferred_element_type=jnp.float32)
    cols = width // n
    middle_own = lax.dynamic_slice_in_dim(middle, place * cols, cols, axis=1)
    down_send = jnp.transpose(down_part.reshape(rows, n, cols), (1, 0, 2))
    out_got = two_phase(down_send, [middle_own], _down_combine, (rows, cols), jnp.bfloat16, n, 4)
    return jnp.transpose(out_got, (1, 0, 2)).reshape(req_all, steps, width)


def solution(mesh):
    return jax.shard_map(
        shards,
        mesh=mesh,
        in_specs=(
            P("rep", None),
            P("rep"),
            P("seq", None),
            P("rep", "seq", None),
            P("rep", "seq", None),
            P(),
            P(),
            P(None, "seq"),
            P(None, "seq"),
            P(None, "seq"),
            P(None, "seq"),
            P("seq", None),
        ),
        out_specs=P("rep", None, None),
        check_vma=False,
    )
```

```python
import functools

import jax
import jax.numpy as jnp
from jax import lax
from jax.experimental import pallas as pl
from jax.experimental.pallas import tpu as pltpu
from jax.sharding import PartitionSpec as P

H = 32
KVH = 8
HD = 64

MESH_ID = pl.DeviceIdType.MESH


def _greet(n, me, rep):
    barrier = pltpu.get_barrier_semaphore()

    def greet(k, carry):
        peer = lax.rem(me + k, n)
        pl.semaphore_signal(barrier, inc=1, device_id=(peer, rep), device_id_type=MESH_ID)
        return carry

    lax.fori_loop(1, n, greet, 0)
    pl.semaphore_wait(barrier, n - 1)


def _exchange_kernel(n, gather, x_ref, o_ref, send_sems, recv_sems, local_sem):
    buf = o_ref
    me = lax.axis_index("seq")
    rep = lax.axis_index("rep")
    _greet(n, me, rep)
    source = (lambda peer: x_ref) if gather else (lambda peer: x_ref.at[peer])
    _stage(n, me, lambda j: j, rep, source, buf, send_sems, recv_sems, local_sem)


def _nbytes(shape, dtype):
    size = int(jnp.dtype(dtype).itemsize)
    for d in shape:
        size *= int(d)
    return size


def exchange(x, n, gather, cid):
    blk = x.shape if gather else x.shape[1:]
    shape = (n,) + tuple(blk)
    nbytes = _nbytes(shape, x.dtype)
    return pl.pallas_call(
        functools.partial(_exchange_kernel, n, gather),
        out_shape=jax.ShapeDtypeStruct(shape, x.dtype),
        in_specs=[pl.BlockSpec(memory_space=pltpu.VMEM)],
        out_specs=pl.BlockSpec(memory_space=pltpu.VMEM),
        scratch_shapes=[
            pltpu.SemaphoreType.DMA(()),
            pltpu.SemaphoreType.DMA(()),
            pltpu.SemaphoreType.DMA(()),
        ],
        compiler_params=pltpu.CompilerParams(collective_id=cid, has_side_effects=True),
        cost_estimate=pl.CostEstimate(flops=0, transcendentals=0, bytes_accessed=2 * nbytes),
        name="exchange_%d" % cid,
    )(x)


def _split(n):
    low = 1
    for c in range(1, n + 1):
        if n % c == 0 and c * c <= n:
            low = c
    return low


def _stage(m, mine, dev_of, rep, source, buf, send_sem, recv_sem, local_sem):
    def copy(j, slot):
        return pltpu.make_async_remote_copy(
            src_ref=source(j),
            dst_ref=buf.at[slot],
            send_sem=send_sem,
            recv_sem=recv_sem,
            device_id=(dev_of(j), rep),
            device_id_type=MESH_ID,
        )

    def send(k, carry):
        j = lax.rem(mine + k, m)
        copy(j, mine).start()
        return carry

    lax.fori_loop(1, m, send, 0)
    local = pltpu.make_async_copy(source(mine), buf.at[mine], local_sem)
    local.start()
    rest = buf.at[pl.ds(0, m - 1)]
    every = pltpu.make_async_remote_copy(
        src_ref=rest,
        dst_ref=rest,
        send_sem=send_sem,
        recv_sem=recv_sem,
        device_id=(dev_of(lax.rem(mine + 1, m)), rep),
        device_id_type=MESH_ID,
    )
    every.wait_send()
    every.wait_recv()
    local.wait()


def _greet2(low, high, hi, lo, rep):
    barrier = pltpu.get_barrier_semaphore()

    def near(k, carry):
        peer = hi * low + lax.rem(lo + k, low)
        pl.semaphore_signal(barrier, inc=1, device_id=(peer, rep), device_id_type=MESH_ID)
        return carry

    def far(k, carry):
        peer = lax.rem(hi + k, high) * low + lo
        pl.semaphore_signal(barrier, inc=1, device_id=(peer, rep), device_id_type=MESH_ID)
        return carry

    lax.fori_loop(1, low, near, 0)
    lax.fori_loop(1, high, far, 0)
    pl.semaphore_wait(barrier, low + high - 2)


def _gather2_kernel(n, low, x_ref, o_ref, buf1, buf2, s1, r1, l1, s2, r2, l2):
    high = n // low
    me = lax.axis_index("seq")
    rep = lax.axis_index("rep")
    hi = me // low
    lo = lax.rem(me, low)
    _greet2(low, high, hi, lo, rep)
    _stage(low, lo, lambda j: hi * low + j, rep, lambda j: x_ref, buf1, s1, r1, l1)
    _stage(high, hi, lambda j: j * low + lo, rep, lambda j: buf1, buf2, s2, r2, l2)
    o_ref[...] = buf2[...]


def gather2(x, n, cid):
    low = _split(n)
    high = n // low
    blk = tuple(x.shape)
    shape = (high, low) + blk
    nbytes = _nbytes(shape, x.dtype)
    out = pl.pallas_call(
        functools.partial(_gather2_kernel, n, low),
        out_shape=jax.ShapeDtypeStruct(shape, x.dtype),
        in_specs=[pl.BlockSpec(memory_space=pltpu.VMEM)],
        out_specs=pl.BlockSpec(memory_space=pltpu.VMEM),
        scratch_shapes=[
            pltpu.VMEM((low,) + blk, x.dtype),
            pltpu.VMEM(shape, x.dtype),
            pltpu.SemaphoreType.DMA(()),
            pltpu.SemaphoreType.DMA(()),
            pltpu.SemaphoreType.DMA(()),
            pltpu.SemaphoreType.DMA(()),
            pltpu.SemaphoreType.DMA(()),
            pltpu.SemaphoreType.DMA(()),
        ],
        compiler_params=pltpu.CompilerParams(collective_id=cid, has_side_effects=True),
        cost_estimate=pl.CostEstimate(flops=0, transcendentals=0, bytes_accessed=2 * nbytes),
        name="gather2_%d" % cid,
    )(x)
    return out.reshape((n,) + blk)


def _two_phase_kernel(n, combine, n_extra, *refs):
    x_ref = refs[0]
    extras = refs[1 : 1 + n_extra]
    o_ref = refs[1 + n_extra]
    buf1, own, s1, r1, l1, s2, r2, l2 = refs[2 + n_extra :]
    buf2 = o_ref
    me = lax.axis_index("seq")
    rep = lax.axis_index("rep")
    _greet(n, me, rep)
    _stage(n, me, lambda j: j, rep, lambda peer: x_ref.at[peer], buf1, s1, r1, l1)
    own[...] = combine(buf1, *extras)
    _stage(n, me, lambda j: j, rep, lambda peer: own, buf2, s2, r2, l2)


def two_phase(x, extras, combine, own_shape, own_dtype, n, cid):
    first = x.shape
    shape = (n,) + tuple(own_shape)
    nbytes = _nbytes(first, x.dtype) + _nbytes(shape, own_dtype)
    return pl.pallas_call(
        functools.partial(_two_phase_kernel, n, combine, len(extras)),
        out_shape=jax.ShapeDtypeStruct(shape, own_dtype),
        in_specs=[pl.BlockSpec(memory_space=pltpu.VMEM)] * (1 + len(extras)),
        out_specs=pl.BlockSpec(memory_space=pltpu.VMEM),
        scratch_shapes=[
            pltpu.VMEM(first, x.dtype),
            pltpu.VMEM(tuple(own_shape), own_dtype),
            pltpu.SemaphoreType.DMA(()),
            pltpu.SemaphoreType.DMA(()),
            pltpu.SemaphoreType.DMA(()),
            pltpu.SemaphoreType.DMA(()),
            pltpu.SemaphoreType.DMA(()),
            pltpu.SemaphoreType.DMA(()),
        ],
        compiler_params=pltpu.CompilerParams(collective_id=cid, has_side_effects=True),
        cost_estimate=pl.CostEstimate(flops=0, transcendentals=0, bytes_accessed=2 * nbytes),
        name="two_phase_%d" % cid,
    )(x, *extras)


def _merge_combine(buf1, fresh_ref):
    blocks = buf1[...]
    fresh = fresh_ref[...]
    block_max = blocks[:, :, HD : HD + 1]
    fresh_max = fresh[:, HD : HD + 1]
    overall = jnp.maximum(jnp.max(block_max, axis=0), fresh_max)
    block_scale = jnp.exp(block_max - overall[None])
    fresh_scale = jnp.exp(fresh_max - overall)
    weighted = jnp.sum(block_scale * blocks, axis=0) + fresh_scale * fresh
    numer = weighted[:, :HD]
    denom = weighted[:, HD + 1 : HD + 2]
    return (numer / denom).astype(jnp.bfloat16)


def _down_combine(buf1, middle_ref):
    return (middle_ref[...] + branch_factor * jnp.sum(buf1[...], axis=0)).astype(jnp.bfloat16)


STEPS = 4
norm_epsilon = 1e-05
embed_factor = 12.0
score_factor = 0.015625
branch_factor = 0.22
rope_base = 10000000.0
masked_floor = -1e30


def rms_scale(resid, gain):
    mean_square = jnp.mean(resid * resid, axis=-1, keepdims=True)
    return resid * lax.rsqrt(mean_square + norm_epsilon) * gain.astype(jnp.float32)


def rotate(vectors, where):
    half = vectors.shape[-1] // 2
    freqs = rope_base ** (-2.0 * jnp.arange(half, dtype=jnp.float32) / vectors.shape[-1])
    angle = where[..., None] * freqs
    cosine = jnp.cos(angle)
    sine = jnp.sin(angle)
    first_half = vectors[..., :half]
    second_half = vectors[..., half:]
    return jnp.concatenate(
        [first_half * cosine - second_half * sine, second_half * cosine + first_half * sine],
        axis=-1,
    )


def partial_softmax(queries, keys, values, valid):
    scores = (
        jnp.einsum("rskgd,rpkd->rskgp", queries, keys, preferred_element_type=jnp.float32)
        * score_factor
    )
    maxima = jnp.max(jnp.where(valid, scores, masked_floor), axis=-1)
    expo = jnp.exp(jnp.where(valid, scores - maxima[..., None], masked_floor))
    totals = jnp.sum(expo, axis=-1)
    outputs = jnp.einsum(
        "rskgp,rpkd->rskgd", expo.astype(jnp.bfloat16), values, preferred_element_type=jnp.float32
    )
    return (maxima, totals, outputs)


def shards(
    token_ids,
    cache_lengths,
    embed_table,
    key_cache,
    value_cache,
    norm_attn,
    norm_mlp,
    w_qkv,
    w_out,
    w_gate,
    w_up,
    w_down,
):
    n = lax.axis_size("seq")
    place = lax.axis_index("seq")
    req_all = token_ids.shape[0]
    steps = token_ids.shape[1]
    rows = req_all * steps
    ctx_own = key_cache.shape[1]
    width = embed_table.shape[0] * n
    att_width = H * HD
    kv_width = KVH * HD
    group = H // KVH

    vocab = embed_table.shape[1]
    onehot = (
        token_ids.reshape(-1)[:, None] == jnp.arange(vocab, dtype=jnp.int32)[None, :]
    ).astype(embed_table.dtype)
    picked = lax.dot_general(
        onehot, embed_table, (((1,), (1,)), ((), ())), preferred_element_type=jnp.float32
    ).astype(embed_table.dtype)
    whole = exchange(picked, n, True, 0)
    resid = jnp.transpose(whole, (1, 0, 2)).reshape(rows, width).astype(jnp.float32) * embed_factor

    slot_pos = place * ctx_own + jnp.arange(ctx_own, dtype=jnp.int32)
    cache_valid = (slot_pos[None, :] < cache_lengths[:, None]).reshape(req_all, 1, 1, 1, ctx_own)
    cache_keys = key_cache.reshape(req_all, ctx_own, KVH, HD)
    cache_values = value_cache.reshape(req_all, ctx_own, KVH, HD)

    normed = rms_scale(resid, norm_attn).astype(jnp.bfloat16)
    qkv_cols = jnp.dot(normed, w_qkv, preferred_element_type=jnp.float32).astype(jnp.bfloat16)
    qkv_got = exchange(qkv_cols, n, True, 1)
    qkv_all = jnp.transpose(qkv_got, (1, 0, 2)).reshape(req_all, steps, -1)
    where = (cache_lengths[:, None] + jnp.arange(steps, dtype=jnp.int32)[None, :]).astype(
        jnp.float32
    )
    queries = rotate(
        qkv_all[..., :att_width].reshape(req_all, steps, H, HD).astype(jnp.float32),
        where[..., None],
    ).astype(jnp.bfloat16)
    keys_new = rotate(
        qkv_all[..., att_width : att_width + kv_width]
        .reshape(req_all, steps, KVH, HD)
        .astype(jnp.float32),
        where[..., None],
    ).astype(jnp.bfloat16)
    values_new = qkv_all[..., att_width + kv_width :].reshape(req_all, steps, KVH, HD)
    grouped = queries.reshape(req_all, steps, KVH, group, HD)
    pick = (jnp.arange(H, dtype=jnp.int32)[:, None] // group) == jnp.arange(KVH, dtype=jnp.int32)[None, :]
    widened = jnp.where(
        pick[None, None, :, :, None], queries[:, :, :, None, :], jnp.zeros((), queries.dtype)
    ).reshape(req_all, steps * H, kv_width)
    scores = (
        jnp.einsum("rqc,rpc->rqp", widened, key_cache, preferred_element_type=jnp.float32)
        * score_factor
    )
    flat_valid = cache_valid.reshape(req_all, 1, ctx_own)
    flat_max = jnp.max(jnp.where(flat_valid, scores, masked_floor), axis=-1)
    expo = jnp.exp(jnp.where(flat_valid, scores - flat_max[..., None], masked_floor))
    flat_total = jnp.sum(expo, axis=-1)
    spread_out = jnp.einsum(
        "rqp,rpc->rqc", expo.astype(jnp.bfloat16), value_cache, preferred_element_type=jnp.float32
    ).reshape(req_all, steps, H, KVH, HD)
    picked_out = jnp.sum(jnp.where(pick[None, None, :, :, None], spread_out, 0.0), axis=3)
    cache_max = flat_max.reshape(req_all, steps, KVH, group)
    cache_total = flat_total.reshape(req_all, steps, KVH, group)
    cache_out = picked_out.reshape(req_all, steps, KVH, group, HD)
    fresh_valid = (
        jnp.arange(steps, dtype=jnp.int32)[None, :] <= jnp.arange(steps, dtype=jnp.int32)[:, None]
    ).reshape(1, steps, 1, 1, steps)
    fresh_max, fresh_total, fresh_out = partial_softmax(grouped, keys_new, values_new, fresh_valid)

    pairs = rows * H // n
    lanes = 128
    packed = jnp.concatenate(
        [
            cache_out.reshape(n, pairs, HD),
            cache_max.reshape(n, pairs, 1),
            cache_total.reshape(n, pairs, 1),
            jnp.zeros((n, pairs, lanes - HD - 2), jnp.float32),
        ],
        axis=-1,
    )
    own_fresh_max = lax.dynamic_index_in_dim(fresh_max.reshape(n, pairs), place, 0, False)
    own_fresh_total = lax.dynamic_index_in_dim(fresh_total.reshape(n, pairs), place, 0, False)
    own_fresh_out = lax.dynamic_index_in_dim(fresh_out.reshape(n, pairs, HD), place, 0, False)
    fresh_packed = jnp.concatenate(
        [
            own_fresh_out,
            own_fresh_max[:, None],
            own_fresh_total[:, None],
            jnp.zeros((pairs, lanes - HD - 2), jnp.float32),
        ],
        axis=-1,
    )
    attention = two_phase(
        packed, [fresh_packed], _merge_combine, (pairs, HD), jnp.bfloat16, n, 2
    ).reshape(rows, att_width)

    proj_cols = jnp.dot(attention, w_out, preferred_element_type=jnp.float32).astype(jnp.bfloat16)
    proj_got = exchange(proj_cols, n, True, 3)
    projected = jnp.transpose(proj_got, (1, 0, 2)).reshape(rows, width)
    middle = resid + branch_factor * projected.astype(jnp.float32)
    normed_mlp = rms_scale(middle, norm_mlp).astype(jnp.bfloat16)
    gate = jnp.dot(normed_mlp, w_gate, preferred_element_type=jnp.float32)
    upward = jnp.dot(normed_mlp, w_up, preferred_element_type=jnp.float32)
    hidden = (jax.nn.silu(gate) * upward).astype(jnp.bfloat16)
    down_part = jnp.dot(hidden, w_down, preferred_element_type=jnp.float32)
    cols = width // n
    middle_own = lax.dynamic_slice_in_dim(middle, place * cols, cols, axis=1)
    down_send = jnp.transpose(down_part.reshape(rows, n, cols), (1, 0, 2))
    out_got = two_phase(down_send, [middle_own], _down_combine, (rows, cols), jnp.bfloat16, n, 4)
    return jnp.transpose(out_got, (1, 0, 2)).reshape(req_all, steps, width)


def solution(mesh):
    return jax.shard_map(
        shards,
        mesh=mesh,
        in_specs=(
            P("rep", None),
            P("rep"),
            P("seq", None),
            P("rep", "seq", None),
            P("rep", "seq", None),
            P(),
            P(),
            P(None, "seq"),
            P(None, "seq"),
            P(None, "seq"),
            P(None, "seq"),
            P("seq", None),
        ),
        out_specs=P("rep", None, None),
        check_vma=False,
    )
```

```python
import functools

import jax
import jax.numpy as jnp
from jax import lax
from jax.experimental import pallas as pl
from jax.experimental.pallas import tpu as pltpu
from jax.sharding import PartitionSpec as P

H = 32
KVH = 8
HD = 64

MESH_ID = pl.DeviceIdType.MESH


def _greet(n, me, rep):
    barrier = pltpu.get_barrier_semaphore()

    def greet(k, carry):
        peer = lax.rem(me + k, n)
        pl.semaphore_signal(barrier, inc=1, device_id=(peer, rep), device_id_type=MESH_ID)
        return carry

    lax.fori_loop(1, n, greet, 0)
    pl.semaphore_wait(barrier, n - 1)


def _exchange_kernel(n, gather, x_ref, o_ref, send_sems, recv_sems, local_sem):
    buf = o_ref
    me = lax.axis_index("seq")
    rep = lax.axis_index("rep")
    _greet(n, me, rep)
    source = (lambda peer: x_ref) if gather else (lambda peer: x_ref.at[peer])
    _stage(n, me, lambda j: j, rep, source, buf, send_sems, recv_sems, local_sem)


def _nbytes(shape, dtype):
    size = int(jnp.dtype(dtype).itemsize)
    for d in shape:
        size *= int(d)
    return size


def exchange(x, n, gather, cid):
    blk = x.shape if gather else x.shape[1:]
    shape = (n,) + tuple(blk)
    nbytes = _nbytes(shape, x.dtype)
    return pl.pallas_call(
        functools.partial(_exchange_kernel, n, gather),
        out_shape=jax.ShapeDtypeStruct(shape, x.dtype),
        in_specs=[pl.BlockSpec(memory_space=pltpu.VMEM)],
        out_specs=pl.BlockSpec(memory_space=pltpu.VMEM),
        scratch_shapes=[
            pltpu.SemaphoreType.DMA(()),
            pltpu.SemaphoreType.DMA(()),
            pltpu.SemaphoreType.DMA(()),
        ],
        compiler_params=pltpu.CompilerParams(collective_id=cid, has_side_effects=True),
        cost_estimate=pl.CostEstimate(flops=0, transcendentals=0, bytes_accessed=2 * nbytes),
        name="exchange_%d" % cid,
    )(x)


def _split(n):
    low = 1
    for c in range(1, n + 1):
        if n % c == 0 and c * c <= n:
            low = c
    return low


def _stage(m, mine, dev_of, rep, source, buf, send_sem, recv_sem, local_sem):
    def copy(j, slot):
        return pltpu.make_async_remote_copy(
            src_ref=source(j),
            dst_ref=buf.at[slot],
            send_sem=send_sem,
            recv_sem=recv_sem,
            device_id=(dev_of(j), rep),
            device_id_type=MESH_ID,
        )

    half = m // 2

    def send(t, carry):
        k = half + ((t + 1) // 2) * (2 * (t % 2) - 1)
        j = lax.rem(mine + k, m)
        copy(j, mine).start()
        return carry

    lax.fori_loop(0, m - 1, send, 0)
    local = pltpu.make_async_copy(source(mine), buf.at[mine], local_sem)
    local.start()
    rest = buf.at[pl.ds(0, m - 1)]
    every = pltpu.make_async_remote_copy(
        src_ref=rest,
        dst_ref=rest,
        send_sem=send_sem,
        recv_sem=recv_sem,
        device_id=(dev_of(lax.rem(mine + 1, m)), rep),
        device_id_type=MESH_ID,
    )
    every.wait_send()
    every.wait_recv()
    local.wait()


def _greet2(low, high, hi, lo, rep):
    barrier = pltpu.get_barrier_semaphore()

    def near(k, carry):
        peer = hi * low + lax.rem(lo + k, low)
        pl.semaphore_signal(barrier, inc=1, device_id=(peer, rep), device_id_type=MESH_ID)
        return carry

    def far(k, carry):
        peer = lax.rem(hi + k, high) * low + lo
        pl.semaphore_signal(barrier, inc=1, device_id=(peer, rep), device_id_type=MESH_ID)
        return carry

    lax.fori_loop(1, low, near, 0)
    lax.fori_loop(1, high, far, 0)
    pl.semaphore_wait(barrier, low + high - 2)


def _gather2_kernel(n, low, x_ref, o_ref, buf1, buf2, s1, r1, l1, s2, r2, l2):
    high = n // low
    me = lax.axis_index("seq")
    rep = lax.axis_index("rep")
    hi = me // low
    lo = lax.rem(me, low)
    _greet2(low, high, hi, lo, rep)
    _stage(low, lo, lambda j: hi * low + j, rep, lambda j: x_ref, buf1, s1, r1, l1)
    _stage(high, hi, lambda j: j * low + lo, rep, lambda j: buf1, buf2, s2, r2, l2)
    o_ref[...] = buf2[...]


def gather2(x, n, cid):
    low = _split(n)
    high = n // low
    blk = tuple(x.shape)
    shape = (high, low) + blk
    nbytes = _nbytes(shape, x.dtype)
    out = pl.pallas_call(
        functools.partial(_gather2_kernel, n, low),
        out_shape=jax.ShapeDtypeStruct(shape, x.dtype),
        in_specs=[pl.BlockSpec(memory_space=pltpu.VMEM)],
        out_specs=pl.BlockSpec(memory_space=pltpu.VMEM),
        scratch_shapes=[
            pltpu.VMEM((low,) + blk, x.dtype),
            pltpu.VMEM(shape, x.dtype),
            pltpu.SemaphoreType.DMA(()),
            pltpu.SemaphoreType.DMA(()),
            pltpu.SemaphoreType.DMA(()),
            pltpu.SemaphoreType.DMA(()),
            pltpu.SemaphoreType.DMA(()),
            pltpu.SemaphoreType.DMA(()),
        ],
        compiler_params=pltpu.CompilerParams(collective_id=cid, has_side_effects=True),
        cost_estimate=pl.CostEstimate(flops=0, transcendentals=0, bytes_accessed=2 * nbytes),
        name="gather2_%d" % cid,
    )(x)
    return out.reshape((n,) + blk)


def _two_phase_kernel(n, combine, n_extra, *refs):
    x_ref = refs[0]
    extras = refs[1 : 1 + n_extra]
    o_ref = refs[1 + n_extra]
    buf1, own, s1, r1, l1, s2, r2, l2 = refs[2 + n_extra :]
    buf2 = o_ref
    me = lax.axis_index("seq")
    rep = lax.axis_index("rep")
    _greet(n, me, rep)
    _stage(n, me, lambda j: j, rep, lambda peer: x_ref.at[peer], buf1, s1, r1, l1)
    own[...] = combine(buf1, *extras)
    _stage(n, me, lambda j: j, rep, lambda peer: own, buf2, s2, r2, l2)


def two_phase(x, extras, combine, own_shape, own_dtype, n, cid):
    first = x.shape
    shape = (n,) + tuple(own_shape)
    nbytes = _nbytes(first, x.dtype) + _nbytes(shape, own_dtype)
    return pl.pallas_call(
        functools.partial(_two_phase_kernel, n, combine, len(extras)),
        out_shape=jax.ShapeDtypeStruct(shape, own_dtype),
        in_specs=[pl.BlockSpec(memory_space=pltpu.VMEM)] * (1 + len(extras)),
        out_specs=pl.BlockSpec(memory_space=pltpu.VMEM),
        scratch_shapes=[
            pltpu.VMEM(first, x.dtype),
            pltpu.VMEM(tuple(own_shape), own_dtype),
            pltpu.SemaphoreType.DMA(()),
            pltpu.SemaphoreType.DMA(()),
            pltpu.SemaphoreType.DMA(()),
            pltpu.SemaphoreType.DMA(()),
            pltpu.SemaphoreType.DMA(()),
            pltpu.SemaphoreType.DMA(()),
        ],
        compiler_params=pltpu.CompilerParams(collective_id=cid, has_side_effects=True),
        cost_estimate=pl.CostEstimate(flops=0, transcendentals=0, bytes_accessed=2 * nbytes),
        name="two_phase_%d" % cid,
    )(x, *extras)


def _merge_combine(buf1, fresh_ref):
    blocks = buf1[...]
    fresh = fresh_ref[...]
    block_max = blocks[:, :, HD : HD + 1]
    fresh_max = fresh[:, HD : HD + 1]
    overall = jnp.maximum(jnp.max(block_max, axis=0), fresh_max)
    block_scale = jnp.exp(block_max - overall[None])
    fresh_scale = jnp.exp(fresh_max - overall)
    weighted = jnp.sum(block_scale * blocks, axis=0) + fresh_scale * fresh
    numer = weighted[:, :HD]
    denom = weighted[:, HD + 1 : HD + 2]
    return (numer / denom).astype(jnp.bfloat16)


def _down_combine(buf1, middle_ref):
    return (middle_ref[...] + branch_factor * jnp.sum(buf1[...], axis=0)).astype(jnp.bfloat16)


STEPS = 4
norm_epsilon = 1e-05
embed_factor = 12.0
score_factor = 0.015625
branch_factor = 0.22
rope_base = 10000000.0
masked_floor = -1e30


def rms_scale(resid, gain):
    mean_square = jnp.mean(resid * resid, axis=-1, keepdims=True)
    return resid * lax.rsqrt(mean_square + norm_epsilon) * gain.astype(jnp.float32)


def rotate(vectors, where):
    half = vectors.shape[-1] // 2
    freqs = rope_base ** (-2.0 * jnp.arange(half, dtype=jnp.float32) / vectors.shape[-1])
    angle = where[..., None] * freqs
    cosine = jnp.cos(angle)
    sine = jnp.sin(angle)
    first_half = vectors[..., :half]
    second_half = vectors[..., half:]
    return jnp.concatenate(
        [first_half * cosine - second_half * sine, second_half * cosine + first_half * sine],
        axis=-1,
    )


def partial_softmax(queries, keys, values, valid):
    scores = (
        jnp.einsum("rskgd,rpkd->rskgp", queries, keys, preferred_element_type=jnp.float32)
        * score_factor
    )
    maxima = jnp.max(jnp.where(valid, scores, masked_floor), axis=-1)
    expo = jnp.exp(jnp.where(valid, scores - maxima[..., None], masked_floor))
    totals = jnp.sum(expo, axis=-1)
    outputs = jnp.einsum(
        "rskgp,rpkd->rskgd", expo.astype(jnp.bfloat16), values, preferred_element_type=jnp.float32
    )
    return (maxima, totals, outputs)


def shards(
    token_ids,
    cache_lengths,
    embed_table,
    key_cache,
    value_cache,
    norm_attn,
    norm_mlp,
    w_qkv,
    w_out,
    w_gate,
    w_up,
    w_down,
):
    n = lax.axis_size("seq")
    place = lax.axis_index("seq")
    req_all = token_ids.shape[0]
    steps = token_ids.shape[1]
    rows = req_all * steps
    ctx_own = key_cache.shape[1]
    width = embed_table.shape[0] * n
    att_width = H * HD
    kv_width = KVH * HD
    group = H // KVH

    vocab = embed_table.shape[1]
    onehot = (
        token_ids.reshape(-1)[:, None] == jnp.arange(vocab, dtype=jnp.int32)[None, :]
    ).astype(embed_table.dtype)
    picked = lax.dot_general(
        onehot, embed_table, (((1,), (1,)), ((), ())), preferred_element_type=jnp.float32
    ).astype(embed_table.dtype)
    whole = exchange(picked, n, True, 0)
    resid = jnp.transpose(whole, (1, 0, 2)).reshape(rows, width).astype(jnp.float32) * embed_factor

    slot_pos = place * ctx_own + jnp.arange(ctx_own, dtype=jnp.int32)
    cache_valid = (slot_pos[None, :] < cache_lengths[:, None]).reshape(req_all, 1, 1, 1, ctx_own)
    cache_keys = key_cache.reshape(req_all, ctx_own, KVH, HD)
    cache_values = value_cache.reshape(req_all, ctx_own, KVH, HD)

    normed = rms_scale(resid, norm_attn).astype(jnp.bfloat16)
    qkv_cols = jnp.dot(normed, w_qkv, preferred_element_type=jnp.float32).astype(jnp.bfloat16)
    qkv_got = exchange(qkv_cols, n, True, 1)
    qkv_all = jnp.transpose(qkv_got, (1, 0, 2)).reshape(req_all, steps, -1)
    where = (cache_lengths[:, None] + jnp.arange(steps, dtype=jnp.int32)[None, :]).astype(
        jnp.float32
    )
    queries = rotate(
        qkv_all[..., :att_width].reshape(req_all, steps, H, HD).astype(jnp.float32),
        where[..., None],
    ).astype(jnp.bfloat16)
    keys_new = rotate(
        qkv_all[..., att_width : att_width + kv_width]
        .reshape(req_all, steps, KVH, HD)
        .astype(jnp.float32),
        where[..., None],
    ).astype(jnp.bfloat16)
    values_new = qkv_all[..., att_width + kv_width :].reshape(req_all, steps, KVH, HD)
    grouped = queries.reshape(req_all, steps, KVH, group, HD)
    cache_max, cache_total, cache_out = partial_softmax(
        grouped, cache_keys, cache_values, cache_valid
    )
    fresh_valid = (
        jnp.arange(steps, dtype=jnp.int32)[None, :] <= jnp.arange(steps, dtype=jnp.int32)[:, None]
    ).reshape(1, steps, 1, 1, steps)
    fresh_max, fresh_total, fresh_out = partial_softmax(grouped, keys_new, values_new, fresh_valid)

    pairs = rows * H // n
    lanes = 128
    packed = jnp.concatenate(
        [
            cache_out.reshape(n, pairs, HD),
            cache_max.reshape(n, pairs, 1),
            cache_total.reshape(n, pairs, 1),
            jnp.zeros((n, pairs, lanes - HD - 2), jnp.float32),
        ],
        axis=-1,
    )
    own_fresh_max = lax.dynamic_index_in_dim(fresh_max.reshape(n, pairs), place, 0, False)
    own_fresh_total = lax.dynamic_index_in_dim(fresh_total.reshape(n, pairs), place, 0, False)
    own_fresh_out = lax.dynamic_index_in_dim(fresh_out.reshape(n, pairs, HD), place, 0, False)
    fresh_packed = jnp.concatenate(
        [
            own_fresh_out,
            own_fresh_max[:, None],
            own_fresh_total[:, None],
            jnp.zeros((pairs, lanes - HD - 2), jnp.float32),
        ],
        axis=-1,
    )
    attention = two_phase(
        packed, [fresh_packed], _merge_combine, (pairs, HD), jnp.bfloat16, n, 2
    ).reshape(rows, att_width)

    proj_cols = jnp.dot(attention, w_out, preferred_element_type=jnp.float32).astype(jnp.bfloat16)
    proj_got = exchange(proj_cols, n, True, 3)
    projected = jnp.transpose(proj_got, (1, 0, 2)).reshape(rows, width)
    middle = resid + branch_factor * projected.astype(jnp.float32)
    normed_mlp = rms_scale(middle, norm_mlp).astype(jnp.bfloat16)
    gate = jnp.dot(normed_mlp, w_gate, preferred_element_type=jnp.float32)
    upward = jnp.dot(normed_mlp, w_up, preferred_element_type=jnp.float32)
    hidden = (jax.nn.silu(gate) * upward).astype(jnp.bfloat16)
    down_part = jnp.dot(hidden, w_down, preferred_element_type=jnp.float32)
    cols = width // n
    middle_own = lax.dynamic_slice_in_dim(middle, place * cols, cols, axis=1)
    down_send = jnp.transpose(down_part.reshape(rows, n, cols), (1, 0, 2))
    out_got = two_phase(down_send, [middle_own], _down_combine, (rows, cols), jnp.bfloat16, n, 4)
    return jnp.transpose(out_got, (1, 0, 2)).reshape(req_all, steps, width)


def solution(mesh):
    return jax.shard_map(
        shards,
        mesh=mesh,
        in_specs=(
            P("rep", None),
            P("rep"),
            P("seq", None),
            P("rep", "seq", None),
            P("rep", "seq", None),
            P(),
            P(),
            P(None, "seq"),
            P(None, "seq"),
            P(None, "seq"),
            P(None, "seq"),
            P("seq", None),
        ),
        out_specs=P("rep", None, None),
        check_vma=False,
    )
```

```python
import functools

import jax
import jax.numpy as jnp
from jax import lax
from jax.experimental import pallas as pl
from jax.experimental.pallas import tpu as pltpu
from jax.sharding import PartitionSpec as P

H = 32
KVH = 8
HD = 64

MESH_ID = pl.DeviceIdType.MESH


def _greet(n, me, rep):
    barrier = pltpu.get_barrier_semaphore()

    half = n // 2

    def greet(t, carry):
        k = half + ((t + 1) // 2) * (2 * (t % 2) - 1)
        peer = lax.rem(me + k, n)
        pl.semaphore_signal(barrier, inc=1, device_id=(peer, rep), device_id_type=MESH_ID)
        return carry

    lax.fori_loop(0, n - 1, greet, 0)
    pl.semaphore_wait(barrier, n - 1)


def _exchange_kernel(n, gather, x_ref, o_ref, send_sems, recv_sems, local_sem):
    buf = o_ref
    me = lax.axis_index("seq")
    rep = lax.axis_index("rep")
    _greet(n, me, rep)
    source = (lambda peer: x_ref) if gather else (lambda peer: x_ref.at[peer])
    _stage(n, me, lambda j: j, rep, source, buf, send_sems, recv_sems, local_sem)


def _nbytes(shape, dtype):
    size = int(jnp.dtype(dtype).itemsize)
    for d in shape:
        size *= int(d)
    return size


def exchange(x, n, gather, cid):
    blk = x.shape if gather else x.shape[1:]
    shape = (n,) + tuple(blk)
    nbytes = _nbytes(shape, x.dtype)
    return pl.pallas_call(
        functools.partial(_exchange_kernel, n, gather),
        out_shape=jax.ShapeDtypeStruct(shape, x.dtype),
        in_specs=[pl.BlockSpec(memory_space=pltpu.VMEM)],
        out_specs=pl.BlockSpec(memory_space=pltpu.VMEM),
        scratch_shapes=[
            pltpu.SemaphoreType.DMA(()),
            pltpu.SemaphoreType.DMA(()),
            pltpu.SemaphoreType.DMA(()),
        ],
        compiler_params=pltpu.CompilerParams(collective_id=cid, has_side_effects=True),
        cost_estimate=pl.CostEstimate(flops=0, transcendentals=0, bytes_accessed=2 * nbytes),
        name="exchange_%d" % cid,
    )(x)


def _split(n):
    low = 1
    for c in range(1, n + 1):
        if n % c == 0 and c * c <= n:
            low = c
    return low


def _stage(m, mine, dev_of, rep, source, buf, send_sem, recv_sem, local_sem):
    def copy(j, slot):
        return pltpu.make_async_remote_copy(
            src_ref=source(j),
            dst_ref=buf.at[slot],
            send_sem=send_sem,
            recv_sem=recv_sem,
            device_id=(dev_of(j), rep),
            device_id_type=MESH_ID,
        )

    half = m // 2

    def send(t, carry):
        k = half + ((t + 1) // 2) * (2 * (t % 2) - 1)
        j = lax.rem(mine + k, m)
        copy(j, mine).start()
        return carry

    lax.fori_loop(0, m - 1, send, 0)
    local = pltpu.make_async_copy(source(mine), buf.at[mine], local_sem)
    local.start()
    rest = buf.at[pl.ds(0, m - 1)]
    every = pltpu.make_async_remote_copy(
        src_ref=rest,
        dst_ref=rest,
        send_sem=send_sem,
        recv_sem=recv_sem,
        device_id=(dev_of(lax.rem(mine + 1, m)), rep),
        device_id_type=MESH_ID,
    )
    every.wait_send()
    every.wait_recv()
    local.wait()


def _greet2(low, high, hi, lo, rep):
    barrier = pltpu.get_barrier_semaphore()

    def near(k, carry):
        peer = hi * low + lax.rem(lo + k, low)
        pl.semaphore_signal(barrier, inc=1, device_id=(peer, rep), device_id_type=MESH_ID)
        return carry

    def far(k, carry):
        peer = lax.rem(hi + k, high) * low + lo
        pl.semaphore_signal(barrier, inc=1, device_id=(peer, rep), device_id_type=MESH_ID)
        return carry

    lax.fori_loop(1, low, near, 0)
    lax.fori_loop(1, high, far, 0)
    pl.semaphore_wait(barrier, low + high - 2)


def _gather2_kernel(n, low, x_ref, o_ref, buf1, buf2, s1, r1, l1, s2, r2, l2):
    high = n // low
    me = lax.axis_index("seq")
    rep = lax.axis_index("rep")
    hi = me // low
    lo = lax.rem(me, low)
    _greet2(low, high, hi, lo, rep)
    _stage(low, lo, lambda j: hi * low + j, rep, lambda j: x_ref, buf1, s1, r1, l1)
    _stage(high, hi, lambda j: j * low + lo, rep, lambda j: buf1, buf2, s2, r2, l2)
    o_ref[...] = buf2[...]


def gather2(x, n, cid):
    low = _split(n)
    high = n // low
    blk = tuple(x.shape)
    shape = (high, low) + blk
    nbytes = _nbytes(shape, x.dtype)
    out = pl.pallas_call(
        functools.partial(_gather2_kernel, n, low),
        out_shape=jax.ShapeDtypeStruct(shape, x.dtype),
        in_specs=[pl.BlockSpec(memory_space=pltpu.VMEM)],
        out_specs=pl.BlockSpec(memory_space=pltpu.VMEM),
        scratch_shapes=[
            pltpu.VMEM((low,) + blk, x.dtype),
            pltpu.VMEM(shape, x.dtype),
            pltpu.SemaphoreType.DMA(()),
            pltpu.SemaphoreType.DMA(()),
            pltpu.SemaphoreType.DMA(()),
            pltpu.SemaphoreType.DMA(()),
            pltpu.SemaphoreType.DMA(()),
            pltpu.SemaphoreType.DMA(()),
        ],
        compiler_params=pltpu.CompilerParams(collective_id=cid, has_side_effects=True),
        cost_estimate=pl.CostEstimate(flops=0, transcendentals=0, bytes_accessed=2 * nbytes),
        name="gather2_%d" % cid,
    )(x)
    return out.reshape((n,) + blk)


def _two_phase_kernel(n, combine, n_extra, *refs):
    x_ref = refs[0]
    extras = refs[1 : 1 + n_extra]
    o_ref = refs[1 + n_extra]
    buf1, own, s1, r1, l1, s2, r2, l2 = refs[2 + n_extra :]
    buf2 = o_ref
    me = lax.axis_index("seq")
    rep = lax.axis_index("rep")
    _greet(n, me, rep)
    _stage(n, me, lambda j: j, rep, lambda peer: x_ref.at[peer], buf1, s1, r1, l1)
    own[...] = combine(buf1, *extras)
    _stage(n, me, lambda j: j, rep, lambda peer: own, buf2, s2, r2, l2)


def two_phase(x, extras, combine, own_shape, own_dtype, n, cid):
    first = x.shape
    shape = (n,) + tuple(own_shape)
    nbytes = _nbytes(first, x.dtype) + _nbytes(shape, own_dtype)
    return pl.pallas_call(
        functools.partial(_two_phase_kernel, n, combine, len(extras)),
        out_shape=jax.ShapeDtypeStruct(shape, own_dtype),
        in_specs=[pl.BlockSpec(memory_space=pltpu.VMEM)] * (1 + len(extras)),
        out_specs=pl.BlockSpec(memory_space=pltpu.VMEM),
        scratch_shapes=[
            pltpu.VMEM(first, x.dtype),
            pltpu.VMEM(tuple(own_shape), own_dtype),
            pltpu.SemaphoreType.DMA(()),
            pltpu.SemaphoreType.DMA(()),
            pltpu.SemaphoreType.DMA(()),
            pltpu.SemaphoreType.DMA(()),
            pltpu.SemaphoreType.DMA(()),
            pltpu.SemaphoreType.DMA(()),
        ],
        compiler_params=pltpu.CompilerParams(collective_id=cid, has_side_effects=True),
        cost_estimate=pl.CostEstimate(flops=0, transcendentals=0, bytes_accessed=2 * nbytes),
        name="two_phase_%d" % cid,
    )(x, *extras)


def _merge_combine(buf1, fresh_ref):
    blocks = buf1[...]
    fresh = fresh_ref[...]
    block_max = blocks[:, :, HD : HD + 1]
    fresh_max = fresh[:, HD : HD + 1]
    overall = jnp.maximum(jnp.max(block_max, axis=0), fresh_max)
    block_scale = jnp.exp(block_max - overall[None])
    fresh_scale = jnp.exp(fresh_max - overall)
    weighted = jnp.sum(block_scale * blocks, axis=0) + fresh_scale * fresh
    numer = weighted[:, :HD]
    denom = weighted[:, HD + 1 : HD + 2]
    return (numer / denom).astype(jnp.bfloat16)


def _down_combine(buf1, middle_ref):
    return (middle_ref[...] + branch_factor * jnp.sum(buf1[...], axis=0)).astype(jnp.bfloat16)


STEPS = 4
norm_epsilon = 1e-05
embed_factor = 12.0
score_factor = 0.015625
branch_factor = 0.22
rope_base = 10000000.0
masked_floor = -1e30


def rms_scale(resid, gain):
    mean_square = jnp.mean(resid * resid, axis=-1, keepdims=True)
    return resid * lax.rsqrt(mean_square + norm_epsilon) * gain.astype(jnp.float32)


def rotate(vectors, where):
    half = vectors.shape[-1] // 2
    freqs = rope_base ** (-2.0 * jnp.arange(half, dtype=jnp.float32) / vectors.shape[-1])
    angle = where[..., None] * freqs
    cosine = jnp.cos(angle)
    sine = jnp.sin(angle)
    first_half = vectors[..., :half]
    second_half = vectors[..., half:]
    return jnp.concatenate(
        [first_half * cosine - second_half * sine, second_half * cosine + first_half * sine],
        axis=-1,
    )


def partial_softmax(queries, keys, values, valid):
    scores = (
        jnp.einsum("rskgd,rpkd->rskgp", queries, keys, preferred_element_type=jnp.float32)
        * score_factor
    )
    maxima = jnp.max(jnp.where(valid, scores, masked_floor), axis=-1)
    expo = jnp.exp(jnp.where(valid, scores - maxima[..., None], masked_floor))
    totals = jnp.sum(expo, axis=-1)
    outputs = jnp.einsum(
        "rskgp,rpkd->rskgd", expo.astype(jnp.bfloat16), values, preferred_element_type=jnp.float32
    )
    return (maxima, totals, outputs)


def shards(
    token_ids,
    cache_lengths,
    embed_table,
    key_cache,
    value_cache,
    norm_attn,
    norm_mlp,
    w_qkv,
    w_out,
    w_gate,
    w_up,
    w_down,
):
    n = lax.axis_size("seq")
    place = lax.axis_index("seq")
    req_all = token_ids.shape[0]
    steps = token_ids.shape[1]
    rows = req_all * steps
    ctx_own = key_cache.shape[1]
    width = embed_table.shape[0] * n
    att_width = H * HD
    kv_width = KVH * HD
    group = H // KVH

    vocab = embed_table.shape[1]
    onehot = (
        token_ids.reshape(-1)[:, None] == jnp.arange(vocab, dtype=jnp.int32)[None, :]
    ).astype(embed_table.dtype)
    picked = lax.dot_general(
        onehot, embed_table, (((1,), (1,)), ((), ())), preferred_element_type=jnp.float32
    ).astype(embed_table.dtype)
    whole = exchange(picked, n, True, 0)
    resid = jnp.transpose(whole, (1, 0, 2)).reshape(rows, width).astype(jnp.float32) * embed_factor

    slot_pos = place * ctx_own + jnp.arange(ctx_own, dtype=jnp.int32)
    cache_valid = (slot_pos[None, :] < cache_lengths[:, None]).reshape(req_all, 1, 1, 1, ctx_own)
    cache_keys = key_cache.reshape(req_all, ctx_own, KVH, HD)
    cache_values = value_cache.reshape(req_all, ctx_own, KVH, HD)

    normed = rms_scale(resid, norm_attn).astype(jnp.bfloat16)
    qkv_cols = jnp.dot(normed, w_qkv, preferred_element_type=jnp.float32).astype(jnp.bfloat16)
    qkv_got = exchange(qkv_cols, n, True, 1)
    qkv_all = jnp.transpose(qkv_got, (1, 0, 2)).reshape(req_all, steps, -1)
    where = (cache_lengths[:, None] + jnp.arange(steps, dtype=jnp.int32)[None, :]).astype(
        jnp.float32
    )
    queries = rotate(
        qkv_all[..., :att_width].reshape(req_all, steps, H, HD).astype(jnp.float32),
        where[..., None],
    ).astype(jnp.bfloat16)
    keys_new = rotate(
        qkv_all[..., att_width : att_width + kv_width]
        .reshape(req_all, steps, KVH, HD)
        .astype(jnp.float32),
        where[..., None],
    ).astype(jnp.bfloat16)
    values_new = qkv_all[..., att_width + kv_width :].reshape(req_all, steps, KVH, HD)
    grouped = queries.reshape(req_all, steps, KVH, group, HD)
    cache_max, cache_total, cache_out = partial_softmax(
        grouped, cache_keys, cache_values, cache_valid
    )
    fresh_valid = (
        jnp.arange(steps, dtype=jnp.int32)[None, :] <= jnp.arange(steps, dtype=jnp.int32)[:, None]
    ).reshape(1, steps, 1, 1, steps)
    fresh_max, fresh_total, fresh_out = partial_softmax(grouped, keys_new, values_new, fresh_valid)

    pairs = rows * H // n
    lanes = 128
    packed = jnp.concatenate(
        [
            cache_out.reshape(n, pairs, HD),
            cache_max.reshape(n, pairs, 1),
            cache_total.reshape(n, pairs, 1),
            jnp.zeros((n, pairs, lanes - HD - 2), jnp.float32),
        ],
        axis=-1,
    )
    own_fresh_max = lax.dynamic_index_in_dim(fresh_max.reshape(n, pairs), place, 0, False)
    own_fresh_total = lax.dynamic_index_in_dim(fresh_total.reshape(n, pairs), place, 0, False)
    own_fresh_out = lax.dynamic_index_in_dim(fresh_out.reshape(n, pairs, HD), place, 0, False)
    fresh_packed = jnp.concatenate(
        [
            own_fresh_out,
            own_fresh_max[:, None],
            own_fresh_total[:, None],
            jnp.zeros((pairs, lanes - HD - 2), jnp.float32),
        ],
        axis=-1,
    )
    attention = two_phase(
        packed, [fresh_packed], _merge_combine, (pairs, HD), jnp.bfloat16, n, 2
    ).reshape(rows, att_width)

    proj_cols = jnp.dot(attention, w_out, preferred_element_type=jnp.float32).astype(jnp.bfloat16)
    proj_got = exchange(proj_cols, n, True, 3)
    projected = jnp.transpose(proj_got, (1, 0, 2)).reshape(rows, width)
    middle = resid + branch_factor * projected.astype(jnp.float32)
    normed_mlp = rms_scale(middle, norm_mlp).astype(jnp.bfloat16)
    gate = jnp.dot(normed_mlp, w_gate, preferred_element_type=jnp.float32)
    upward = jnp.dot(normed_mlp, w_up, preferred_element_type=jnp.float32)
    hidden = (jax.nn.silu(gate) * upward).astype(jnp.bfloat16)
    down_part = jnp.dot(hidden, w_down, preferred_element_type=jnp.float32)
    cols = width // n
    middle_own = lax.dynamic_slice_in_dim(middle, place * cols, cols, axis=1)
    down_send = jnp.transpose(down_part.reshape(rows, n, cols), (1, 0, 2))
    out_got = two_phase(down_send, [middle_own], _down_combine, (rows, cols), jnp.bfloat16, n, 4)
    return jnp.transpose(out_got, (1, 0, 2)).reshape(req_all, steps, width)


def solution(mesh):
    return jax.shard_map(
        shards,
        mesh=mesh,
        in_specs=(
            P("rep", None),
            P("rep"),
            P("seq", None),
            P("rep", "seq", None),
            P("rep", "seq", None),
            P(),
            P(),
            P(None, "seq"),
            P(None, "seq"),
            P(None, "seq"),
            P(None, "seq"),
            P("seq", None),
        ),
        out_specs=P("rep", None, None),
        check_vma=False,
    )
```

```python
import functools

import jax
import jax.numpy as jnp
from jax import lax
from jax.experimental import pallas as pl
from jax.experimental.pallas import tpu as pltpu
from jax.sharding import PartitionSpec as P

H = 32
KVH = 8
HD = 64

MESH_ID = pl.DeviceIdType.MESH


def _greet(n, me, rep):
    barrier = pltpu.get_barrier_semaphore()

    def greet(k, carry):
        peer = lax.rem(me + k, n)
        pl.semaphore_signal(barrier, inc=1, device_id=(peer, rep), device_id_type=MESH_ID)
        return carry

    lax.fori_loop(1, n, greet, 0)
    pl.semaphore_wait(barrier, n - 1)


def _exchange_kernel(n, gather, x_ref, o_ref, send_sems, recv_sems, local_sem):
    buf = o_ref
    me = lax.axis_index("seq")
    rep = lax.axis_index("rep")
    _greet(n, me, rep)
    source = (lambda peer: x_ref) if gather else (lambda peer: x_ref.at[peer])
    _stage(n, me, lambda j: j, rep, source, buf, send_sems, recv_sems, local_sem)


def _nbytes(shape, dtype):
    size = int(jnp.dtype(dtype).itemsize)
    for d in shape:
        size *= int(d)
    return size


def exchange(x, n, gather, cid):
    blk = x.shape if gather else x.shape[1:]
    shape = (n,) + tuple(blk)
    nbytes = _nbytes(shape, x.dtype)
    return pl.pallas_call(
        functools.partial(_exchange_kernel, n, gather),
        out_shape=jax.ShapeDtypeStruct(shape, x.dtype),
        in_specs=[pl.BlockSpec(memory_space=pltpu.VMEM)],
        out_specs=pl.BlockSpec(memory_space=pltpu.VMEM),
        scratch_shapes=[
            pltpu.SemaphoreType.DMA(()),
            pltpu.SemaphoreType.DMA(()),
            pltpu.SemaphoreType.DMA(()),
        ],
        compiler_params=pltpu.CompilerParams(collective_id=cid, has_side_effects=True),
        cost_estimate=pl.CostEstimate(flops=0, transcendentals=0, bytes_accessed=2 * nbytes),
        name="exchange_%d" % cid,
    )(x)


def _split(n):
    low = 1
    for c in range(1, n + 1):
        if n % c == 0 and c * c <= n:
            low = c
    return low


def _stage(m, mine, dev_of, rep, source, buf, send_sem, recv_sem, local_sem):
    def copy(j, slot):
        return pltpu.make_async_remote_copy(
            src_ref=source(j),
            dst_ref=buf.at[slot],
            send_sem=send_sem,
            recv_sem=recv_sem,
            device_id=(dev_of(j), rep),
            device_id_type=MESH_ID,
        )

    half = m // 2

    def send(t, carry):
        k = half + ((t + 1) // 2) * (2 * (t % 2) - 1)
        j = lax.rem(mine + k, m)
        copy(j, mine).start()
        return carry

    local = pltpu.make_async_copy(source(mine), buf.at[mine], local_sem)
    local.start()
    lax.fori_loop(0, m - 1, send, 0)
    rest = buf.at[pl.ds(0, m - 1)]
    every = pltpu.make_async_remote_copy(
        src_ref=rest,
        dst_ref=rest,
        send_sem=send_sem,
        recv_sem=recv_sem,
        device_id=(dev_of(lax.rem(mine + 1, m)), rep),
        device_id_type=MESH_ID,
    )
    every.wait_send()
    every.wait_recv()
    local.wait()


def _greet2(low, high, hi, lo, rep):
    barrier = pltpu.get_barrier_semaphore()

    def near(k, carry):
        peer = hi * low + lax.rem(lo + k, low)
        pl.semaphore_signal(barrier, inc=1, device_id=(peer, rep), device_id_type=MESH_ID)
        return carry

    def far(k, carry):
        peer = lax.rem(hi + k, high) * low + lo
        pl.semaphore_signal(barrier, inc=1, device_id=(peer, rep), device_id_type=MESH_ID)
        return carry

    lax.fori_loop(1, low, near, 0)
    lax.fori_loop(1, high, far, 0)
    pl.semaphore_wait(barrier, low + high - 2)


def _gather2_kernel(n, low, x_ref, o_ref, buf1, buf2, s1, r1, l1, s2, r2, l2):
    high = n // low
    me = lax.axis_index("seq")
    rep = lax.axis_index("rep")
    hi = me // low
    lo = lax.rem(me, low)
    _greet2(low, high, hi, lo, rep)
    _stage(low, lo, lambda j: hi * low + j, rep, lambda j: x_ref, buf1, s1, r1, l1)
    _stage(high, hi, lambda j: j * low + lo, rep, lambda j: buf1, buf2, s2, r2, l2)
    o_ref[...] = buf2[...]


def gather2(x, n, cid):
    low = _split(n)
    high = n // low
    blk = tuple(x.shape)
    shape = (high, low) + blk
    nbytes = _nbytes(shape, x.dtype)
    out = pl.pallas_call(
        functools.partial(_gather2_kernel, n, low),
        out_shape=jax.ShapeDtypeStruct(shape, x.dtype),
        in_specs=[pl.BlockSpec(memory_space=pltpu.VMEM)],
        out_specs=pl.BlockSpec(memory_space=pltpu.VMEM),
        scratch_shapes=[
            pltpu.VMEM((low,) + blk, x.dtype),
            pltpu.VMEM(shape, x.dtype),
            pltpu.SemaphoreType.DMA(()),
            pltpu.SemaphoreType.DMA(()),
            pltpu.SemaphoreType.DMA(()),
            pltpu.SemaphoreType.DMA(()),
            pltpu.SemaphoreType.DMA(()),
            pltpu.SemaphoreType.DMA(()),
        ],
        compiler_params=pltpu.CompilerParams(collective_id=cid, has_side_effects=True),
        cost_estimate=pl.CostEstimate(flops=0, transcendentals=0, bytes_accessed=2 * nbytes),
        name="gather2_%d" % cid,
    )(x)
    return out.reshape((n,) + blk)


def _two_phase_kernel(n, combine, n_extra, *refs):
    x_ref = refs[0]
    extras = refs[1 : 1 + n_extra]
    o_ref = refs[1 + n_extra]
    buf1, own, s1, r1, l1, s2, r2, l2 = refs[2 + n_extra :]
    buf2 = o_ref
    me = lax.axis_index("seq")
    rep = lax.axis_index("rep")
    _greet(n, me, rep)
    _stage(n, me, lambda j: j, rep, lambda peer: x_ref.at[peer], buf1, s1, r1, l1)
    own[...] = combine(buf1, *extras)
    _stage(n, me, lambda j: j, rep, lambda peer: own, buf2, s2, r2, l2)


def two_phase(x, extras, combine, own_shape, own_dtype, n, cid):
    first = x.shape
    shape = (n,) + tuple(own_shape)
    nbytes = _nbytes(first, x.dtype) + _nbytes(shape, own_dtype)
    return pl.pallas_call(
        functools.partial(_two_phase_kernel, n, combine, len(extras)),
        out_shape=jax.ShapeDtypeStruct(shape, own_dtype),
        in_specs=[pl.BlockSpec(memory_space=pltpu.VMEM)] * (1 + len(extras)),
        out_specs=pl.BlockSpec(memory_space=pltpu.VMEM),
        scratch_shapes=[
            pltpu.VMEM(first, x.dtype),
            pltpu.VMEM(tuple(own_shape), own_dtype),
            pltpu.SemaphoreType.DMA(()),
            pltpu.SemaphoreType.DMA(()),
            pltpu.SemaphoreType.DMA(()),
            pltpu.SemaphoreType.DMA(()),
            pltpu.SemaphoreType.DMA(()),
            pltpu.SemaphoreType.DMA(()),
        ],
        compiler_params=pltpu.CompilerParams(collective_id=cid, has_side_effects=True),
        cost_estimate=pl.CostEstimate(flops=0, transcendentals=0, bytes_accessed=2 * nbytes),
        name="two_phase_%d" % cid,
    )(x, *extras)


def _merge_combine(buf1, fresh_ref):
    blocks = buf1[...]
    fresh = fresh_ref[...]
    block_max = blocks[:, :, HD : HD + 1]
    fresh_max = fresh[:, HD : HD + 1]
    overall = jnp.maximum(jnp.max(block_max, axis=0), fresh_max)
    block_scale = jnp.exp(block_max - overall[None])
    fresh_scale = jnp.exp(fresh_max - overall)
    weighted = jnp.sum(block_scale * blocks, axis=0) + fresh_scale * fresh
    numer = weighted[:, :HD]
    denom = weighted[:, HD + 1 : HD + 2]
    return (numer / denom).astype(jnp.bfloat16)


def _down_combine(buf1, middle_ref):
    return (middle_ref[...] + branch_factor * jnp.sum(buf1[...], axis=0)).astype(jnp.bfloat16)


STEPS = 4
norm_epsilon = 1e-05
embed_factor = 12.0
score_factor = 0.015625
branch_factor = 0.22
rope_base = 10000000.0
masked_floor = -1e30


def rms_scale(resid, gain):
    mean_square = jnp.mean(resid * resid, axis=-1, keepdims=True)
    return resid * lax.rsqrt(mean_square + norm_epsilon) * gain.astype(jnp.float32)


def rotate(vectors, where):
    half = vectors.shape[-1] // 2
    freqs = rope_base ** (-2.0 * jnp.arange(half, dtype=jnp.float32) / vectors.shape[-1])
    angle = where[..., None] * freqs
    cosine = jnp.cos(angle)
    sine = jnp.sin(angle)
    first_half = vectors[..., :half]
    second_half = vectors[..., half:]
    return jnp.concatenate(
        [first_half * cosine - second_half * sine, second_half * cosine + first_half * sine],
        axis=-1,
    )


def partial_softmax(queries, keys, values, valid):
    scores = (
        jnp.einsum("rskgd,rpkd->rskgp", queries, keys, preferred_element_type=jnp.float32)
        * score_factor
    )
    maxima = jnp.max(jnp.where(valid, scores, masked_floor), axis=-1)
    expo = jnp.exp(jnp.where(valid, scores - maxima[..., None], masked_floor))
    totals = jnp.sum(expo, axis=-1)
    outputs = jnp.einsum(
        "rskgp,rpkd->rskgd", expo.astype(jnp.bfloat16), values, preferred_element_type=jnp.float32
    )
    return (maxima, totals, outputs)


def shards(
    token_ids,
    cache_lengths,
    embed_table,
    key_cache,
    value_cache,
    norm_attn,
    norm_mlp,
    w_qkv,
    w_out,
    w_gate,
    w_up,
    w_down,
):
    n = lax.axis_size("seq")
    place = lax.axis_index("seq")
    req_all = token_ids.shape[0]
    steps = token_ids.shape[1]
    rows = req_all * steps
    ctx_own = key_cache.shape[1]
    width = embed_table.shape[0] * n
    att_width = H * HD
    kv_width = KVH * HD
    group = H // KVH

    vocab = embed_table.shape[1]
    onehot = (
        token_ids.reshape(-1)[:, None] == jnp.arange(vocab, dtype=jnp.int32)[None, :]
    ).astype(embed_table.dtype)
    picked = lax.dot_general(
        onehot, embed_table, (((1,), (1,)), ((), ())), preferred_element_type=jnp.float32
    ).astype(embed_table.dtype)
    whole = exchange(picked, n, True, 0)
    resid = jnp.transpose(whole, (1, 0, 2)).reshape(rows, width).astype(jnp.float32) * embed_factor

    slot_pos = place * ctx_own + jnp.arange(ctx_own, dtype=jnp.int32)
    cache_valid = (slot_pos[None, :] < cache_lengths[:, None]).reshape(req_all, 1, 1, 1, ctx_own)
    cache_keys = key_cache.reshape(req_all, ctx_own, KVH, HD)
    cache_values = value_cache.reshape(req_all, ctx_own, KVH, HD)

    normed = rms_scale(resid, norm_attn).astype(jnp.bfloat16)
    qkv_cols = jnp.dot(normed, w_qkv, preferred_element_type=jnp.float32).astype(jnp.bfloat16)
    qkv_got = exchange(qkv_cols, n, True, 1)
    qkv_all = jnp.transpose(qkv_got, (1, 0, 2)).reshape(req_all, steps, -1)
    where = (cache_lengths[:, None] + jnp.arange(steps, dtype=jnp.int32)[None, :]).astype(
        jnp.float32
    )
    queries = rotate(
        qkv_all[..., :att_width].reshape(req_all, steps, H, HD).astype(jnp.float32),
        where[..., None],
    ).astype(jnp.bfloat16)
    keys_new = rotate(
        qkv_all[..., att_width : att_width + kv_width]
        .reshape(req_all, steps, KVH, HD)
        .astype(jnp.float32),
        where[..., None],
    ).astype(jnp.bfloat16)
    values_new = qkv_all[..., att_width + kv_width :].reshape(req_all, steps, KVH, HD)
    grouped = queries.reshape(req_all, steps, KVH, group, HD)
    cache_max, cache_total, cache_out = partial_softmax(
        grouped, cache_keys, cache_values, cache_valid
    )
    fresh_valid = (
        jnp.arange(steps, dtype=jnp.int32)[None, :] <= jnp.arange(steps, dtype=jnp.int32)[:, None]
    ).reshape(1, steps, 1, 1, steps)
    fresh_max, fresh_total, fresh_out = partial_softmax(grouped, keys_new, values_new, fresh_valid)

    pairs = rows * H // n
    lanes = 128
    packed = jnp.concatenate(
        [
            cache_out.reshape(n, pairs, HD),
            cache_max.reshape(n, pairs, 1),
            cache_total.reshape(n, pairs, 1),
            jnp.zeros((n, pairs, lanes - HD - 2), jnp.float32),
        ],
        axis=-1,
    )
    own_fresh_max = lax.dynamic_index_in_dim(fresh_max.reshape(n, pairs), place, 0, False)
    own_fresh_total = lax.dynamic_index_in_dim(fresh_total.reshape(n, pairs), place, 0, False)
    own_fresh_out = lax.dynamic_index_in_dim(fresh_out.reshape(n, pairs, HD), place, 0, False)
    fresh_packed = jnp.concatenate(
        [
            own_fresh_out,
            own_fresh_max[:, None],
            own_fresh_total[:, None],
            jnp.zeros((pairs, lanes - HD - 2), jnp.float32),
        ],
        axis=-1,
    )
    attention = two_phase(
        packed, [fresh_packed], _merge_combine, (pairs, HD), jnp.bfloat16, n, 2
    ).reshape(rows, att_width)

    proj_cols = jnp.dot(attention, w_out, preferred_element_type=jnp.float32).astype(jnp.bfloat16)
    proj_got = exchange(proj_cols, n, True, 3)
    projected = jnp.transpose(proj_got, (1, 0, 2)).reshape(rows, width)
    middle = resid + branch_factor * projected.astype(jnp.float32)
    normed_mlp = rms_scale(middle, norm_mlp).astype(jnp.bfloat16)
    gate = jnp.dot(normed_mlp, w_gate, preferred_element_type=jnp.float32)
    upward = jnp.dot(normed_mlp, w_up, preferred_element_type=jnp.float32)
    hidden = (jax.nn.silu(gate) * upward).astype(jnp.bfloat16)
    down_part = jnp.dot(hidden, w_down, preferred_element_type=jnp.float32)
    cols = width // n
    middle_own = lax.dynamic_slice_in_dim(middle, place * cols, cols, axis=1)
    down_send = jnp.transpose(down_part.reshape(rows, n, cols), (1, 0, 2))
    out_got = two_phase(down_send, [middle_own], _down_combine, (rows, cols), jnp.bfloat16, n, 4)
    return jnp.transpose(out_got, (1, 0, 2)).reshape(req_all, steps, width)


def solution(mesh):
    return jax.shard_map(
        shards,
        mesh=mesh,
        in_specs=(
            P("rep", None),
            P("rep"),
            P("seq", None),
            P("rep", "seq", None),
            P("rep", "seq", None),
            P(),
            P(),
            P(None, "seq"),
            P(None, "seq"),
            P(None, "seq"),
            P(None, "seq"),
            P("seq", None),
        ),
        out_specs=P("rep", None, None),
        check_vma=False,
    )
```
